512 devices in a mesh: seq: 64 (over x_hi, z, core), tensor: 8 (over x_lo, y).
Axes of the slice: x: 4 (x_hi: 2, x_lo: 2; x = x_hi * 2 + x_lo), y: 4, z: 16, core: 2. Of those that a mesh axis runs over, the one named last changes fastest.
Arguments:
- projected: bfloat16 [3, 16384, 4096], P(None, 'seq', 'tensor'), may hold values from -6 to 6
- feat_weight: float32 [3, 7, 4096], P(None, None, 'tensor'), may hold values from -2 to 2
- long_filter: float32 [4096, 16384], P(('tensor', 'seq')), may hold values from -1.2 to 1.2
- skip_gain: float32 [4096], P(('tensor', 'seq')), may hold values from 0.5 to 1.5
- out_values: bfloat16 [4096, 2048], P('tensor'), may hold values from -0.125 to 0.125
- out_scales: float32 [32, 16], P('tensor'), may hold values from 0.125 to 1
Outputs:
- mixed: bfloat16 [16384, 2048], P('seq', 'tensor')
The draws below stay inside these ranges and needn't reach their ends.
All inputs are finite; a program needn't handle non-finite values.
Results may differ from the reference program's by a relative error of at most 0.023.
Values may be sent and summed in bfloat16 or wider, within the bound.
No kernel may reach another device: no remote copies, remote signals or barrier semaphores. Data moves between devices by JAX's collectives and lax.ppermute only.
A program may use at most 64 MiB of HBM per device.

```python
import math
import jax
import jax.numpy as jnp
from jax import lax

CHANNEL_COUNT = 4096
D_OUT = 2048
KS = 7
BLK = 128
SEQUENCE_LENGTH = 16384
N_TENSOR = 8


def draw_long_filter(key, part):
    random_child_keys = [jax.random.fold_in(key, 101 + index) for index in range(8)]
    slow_share = 0.5
    chooser = jax.random.uniform(random_child_keys[0], (CHANNEL_COUNT, 1))
    slow_decay = jnp.exp(jax.random.uniform(random_child_keys[1], (CHANNEL_COUNT, 1), minval=math.log(0.1 / SEQUENCE_LENGTH), maxval=math.log(1.0 / SEQUENCE_LENGTH)))
    fast_decay = jnp.exp(jax.random.uniform(random_child_keys[2], (CHANNEL_COUNT, 1), minval=math.log(1.0 / 50.0), maxval=math.log(1.0 / 30.0)))
    decay_rate = jnp.where(chooser < slow_share, slow_decay, fast_decay)
    delay_index = jnp.arange(SEQUENCE_LENGTH, dtype=jnp.int32)[None, :]
    lag_grid = delay_index.astype(jnp.float32)
    decay_profile = jnp.exp(-decay_rate * lag_grid)
    for spike_index in range(2):
        spike_position = jax.random.randint(random_child_keys[3 + spike_index], (CHANNEL_COUNT, 1), 1, SEQUENCE_LENGTH)
        multiplier = jax.random.uniform(random_child_keys[5 + spike_index], (CHANNEL_COUNT, 1), minval=0.6, maxval=0.8)
        decay_profile = decay_profile * jnp.where(delay_index >= spike_position, multiplier, 1.0)
    scaling = jnp.sqrt(jnp.expm1(-2.0 * decay_rate) / jnp.expm1(-2.0 * decay_rate * SEQUENCE_LENGTH))
    rough_part = jax.random.truncated_normal(random_child_keys[7], -4.0, 4.0, (CHANNEL_COUNT, SEQUENCE_LENGTH))
    return (decay_profile * scaling * rough_part).astype(jnp.float32)


def raised(drawn, stream_key, source, target, parts, factor):
    owner, partner = [(jnp.arange(drawn.shape[dim]) // (drawn.shape[dim] // parts)).reshape([-1 if axis == dim else 1 for axis in range(drawn.ndim)]) for dim in (source, target)]
    chosen = jax.random.permutation(stream_key, parts)[partner]
    strong = (owner == chosen) | (owner == (partner + parts // 2) % parts)
    return jnp.where(strong, factor * drawn, drawn)


def level_of(own_key, extent, shards, low, largest):
    def one(position, blocks):
        draws = jax.random.uniform(jax.random.fold_in(jax.random.fold_in(own_key, 6), position), (blocks,), jnp.float32, low / len(shards), largest / len(shards))
        return jnp.repeat(jnp.exp(draws), extent[position] // blocks).reshape((-1,) + (1,) * (len(extent) - position - 1))

    factor_of = one(*shards[0])
    for cut in shards[1:]:
        factor_of = factor_of * one(*cut)
    return factor_of


def scatter_about(stream_key, dims, deviation, most, split=(), kind=jnp.bfloat16):
    entries = deviation * jax.random.normal(stream_key, dims, jnp.float32)
    if split:
        entries = entries * level_of(stream_key, dims, split, -0.22, 0.18)
    return jnp.clip(entries, -most, most).astype(kind)


def heavy_noise(key, extent, scale, limit, pieces, heavy, held_as=jnp.bfloat16):
    values = scale * jax.random.normal(key, extent, jnp.float32)
    if pieces:
        values = values * level_of(key, extent, pieces, -0.22, 0.18)
    return jnp.clip(raised(values, jax.random.fold_in(key, 3), *heavy), -limit, limit).astype(held_as)


def setup_inputs(seed: int = 0) -> dict:
    key_list = jax.random.split(jax.random.key(seed), 7)
    projected = scatter_about(key_list[0], (3, SEQUENCE_LENGTH, CHANNEL_COUNT), 1.0, 6.0, ((1, 64), (2, 8)))
    feat_weight = scatter_about(key_list[1], (3, KS, CHANNEL_COUNT), 0.35, 2.0, ((2, 8),), jnp.float32)
    long_filter = draw_long_filter(jax.random.fold_in(key_list[6], 71), 0)
    skip_gain = jnp.clip(0.5 + 1.0 * jax.random.uniform(key_list[3], (CHANNEL_COUNT,), jnp.float32) ** level_of(key_list[3], (CHANNEL_COUNT,), ((0, 512),), -0.2, 0.2), 0.5, 1.5)
    out_values = heavy_noise(key_list[4], (CHANNEL_COUNT, D_OUT), CHANNEL_COUNT ** -0.5, 0.125, ((0, 8),), (0, 1, 8, 2.0))
    out_scales = jnp.clip(jnp.exp(math.log(1.0) - 2.0794415 * jax.random.uniform(key_list[5], (CHANNEL_COUNT // BLK, D_OUT // BLK), jnp.float32) ** level_of(key_list[5], (CHANNEL_COUNT // BLK, D_OUT // BLK), ((0, 8),), -0.2, 0.2)), 0.125, 1.0)
    return dict(projected=projected, feat_weight=feat_weight, long_filter=long_filter, skip_gain=skip_gain, out_values=out_values, out_scales=out_scales)


def reference(projected, feat_weight, long_filter, skip_gain, out_values, out_scales):
    tap_count = KS
    padded = jnp.pad(projected, ((0, 0), (tap_count - 1, 0), (0, 0)))
    running = jnp.zeros(projected.shape, jnp.float32)
    for lag_idx in range(tap_count):
        offset = tap_count - 1 - lag_idx
        running = running + feat_weight[:, lag_idx, None, :] * padded[:, offset:offset + SEQUENCE_LENGTH, :].astype(jnp.float32)
    featured = running.astype(jnp.bfloat16)
    gated_kv = (featured[1].astype(jnp.float32) * featured[2].astype(jnp.float32)).astype(jnp.bfloat16)
    chan_block = math.gcd(CHANNEL_COUNT, 256)
    kv_rows = jnp.transpose(gated_kv, (1, 0)).reshape(CHANNEL_COUNT // chan_block, chan_block, SEQUENCE_LENGTH)
    filter_rows = long_filter.reshape(CHANNEL_COUNT // chan_block, chan_block, SEQUENCE_LENGTH)
    gain_rows = skip_gain.reshape(CHANNEL_COUNT // chan_block, chan_block)

    def convolve(inputs):
        kv_values = inputs[0].astype(jnp.float32)
        filter_taps = inputs[1]
        gains = inputs[2]
        spectrum = jnp.fft.rfft(kv_values, n=2 * SEQUENCE_LENGTH, axis=1) * jnp.fft.rfft(filter_taps, n=2 * SEQUENCE_LENGTH, axis=1)
        convolved = jnp.fft.irfft(spectrum, n=2 * SEQUENCE_LENGTH, axis=1)[:, :SEQUENCE_LENGTH]
        return (convolved + gains[:, None] * kv_values).astype(jnp.bfloat16)

    filtered = lax.map(convolve, (kv_rows, filter_rows, gain_rows)).reshape(CHANNEL_COUNT, SEQUENCE_LENGTH)
    gated = (featured[0].astype(jnp.float32) * jnp.transpose(filtered, (1, 0)).astype(jnp.float32)).astype(jnp.bfloat16)
    group_ch = CHANNEL_COUNT // N_TENSOR
    per_group = group_ch // BLK
    out_total = jnp.zeros((SEQUENCE_LENGTH, D_OUT), jnp.float32)
    for group_idx in range(N_TENSOR):
        partial_value = jnp.zeros((SEQUENCE_LENGTH, D_OUT), jnp.float32)
        for inner_idx in range(per_group):
            block_row = group_idx * per_group + inner_idx
            low_row = block_row * BLK
            product = jnp.dot(gated[:, low_row:low_row + BLK], out_values[low_row:low_row + BLK, :], preferred_element_type=jnp.float32)
            partial_value = partial_value + product * jnp.repeat(out_scales[block_row], BLK)[None, :]
        rounded = lax.optimization_barrier(partial_value.astype(jnp.bfloat16))
        out_total = out_total + rounded.astype(jnp.float32)
    return out_total.astype(jnp.bfloat16)
```

```python
import math

import jax
import jax.numpy as jnp
from jax import lax
from jax.sharding import PartitionSpec as P

KS = 7
BLK = 128


TRIPLE = lax.Precision.HIGH


def passed_along(x, axis, by):
    size = lax.axis_size(axis)
    pairs = [(i, i + by) for i in range(size) if 0 <= i + by < size]
    return lax.ppermute(x, axis, pairs)


def split_length(whole):
    for candidate in range(2, whole + 1, 2):
        if whole % candidate == 0 and candidate * candidate >= whole:
            return (candidate, whole // candidate)
    return (whole, 1)


def angle_pair(row_count, col_count, period):
    row_ids = lax.broadcasted_iota(jnp.int32, (row_count, col_count), 0)
    col_ids = lax.broadcasted_iota(jnp.int32, (row_count, col_count), 1)
    angles = (row_ids * col_ids % period).astype(jnp.float32) * (2.0 * math.pi / period)
    return (jnp.cos(angles), jnp.sin(angles))


def make_tables(length):
    whole = 2 * length
    size_a, size_b = split_length(whole)
    return (
        angle_pair(size_a, size_a, size_a),
        angle_pair(size_b, size_b, size_b),
        angle_pair(size_a, size_b, whole),
        size_a,
        size_b,
    )


def right_mul(signal, matrix):
    return jnp.einsum("ckn,nm->ckm", signal, matrix, precision=TRIPLE)


def forward(signal, tables):
    (cos_a, sin_a), (cos_b, sin_b), (cos_t, sin_t), size_a, size_b = tables
    half_a = size_a // 2
    blocks = signal.reshape(signal.shape[0], half_a, size_b)
    real_a = jnp.einsum("kn,cnb->ckb", cos_a[:, :half_a], blocks, precision=TRIPLE)
    imag_a = -jnp.einsum("kn,cnb->ckb", sin_a[:, :half_a], blocks, precision=TRIPLE)
    real_t = real_a * cos_t + imag_a * sin_t
    imag_t = imag_a * cos_t - real_a * sin_t
    real_f = right_mul(real_t, cos_b) + right_mul(imag_t, sin_b)
    imag_f = right_mul(imag_t, cos_b) - right_mul(real_t, sin_b)
    return (real_f, imag_f)


def inverse(real_f, imag_f, tables):
    (cos_a, sin_a), (cos_b, sin_b), (cos_t, sin_t), size_a, size_b = tables
    half_a = size_a // 2
    real_z = right_mul(real_f, cos_b) - right_mul(imag_f, sin_b)
    imag_z = right_mul(imag_f, cos_b) + right_mul(real_f, sin_b)
    real_w = real_z * cos_t - imag_z * sin_t
    imag_w = imag_z * cos_t + real_z * sin_t
    out_half = jnp.einsum("nk,ckb->cnb", cos_a[:half_a, :], real_w, precision=TRIPLE) - jnp.einsum(
        "nk,ckb->cnb", sin_a[:half_a, :], imag_w, precision=TRIPLE
    )
    return out_half.reshape(out_half.shape[0], half_a * size_b) * (1.0 / (size_a * size_b))


def long_mix(gated_kv, spectrum, own_gain, tables):
    kv_values = gated_kv.astype(jnp.float32)
    real_u, imag_u = forward(kv_values, tables)
    real_h, imag_h = spectrum
    real_p = real_u * real_h - imag_u * imag_h
    imag_p = real_u * imag_h + imag_u * real_h
    convolved = inverse(real_p, imag_p, tables)
    return (convolved + own_gain[:, None] * kv_values).astype(jnp.bfloat16)


def featurize(extended, weights, length):
    tap_count = weights.shape[1]
    running = jnp.zeros(extended.shape[:1] + (length,) + extended.shape[2:], jnp.float32)
    for lag_idx in range(tap_count):
        offset = tap_count - 1 - lag_idx
        running = running + weights[:, lag_idx, None, :] * extended[
            :, offset : offset + length, :
        ].astype(jnp.float32)
    return running.astype(jnp.bfloat16)


def multiply_round(left_arr, right_arr):
    return (left_arr.astype(jnp.float32) * right_arr.astype(jnp.float32)).astype(jnp.bfloat16)


def local(projected, feat_weight, long_filter, skip_gain, out_values, out_scales):
    groups = lax.axis_size("seq")
    tok_rows = projected.shape[1]
    local_ch = projected.shape[2]
    length = tok_rows * groups
    tables = make_tables(length)
    spectrum = forward(long_filter, tables)
    rim_width = KS - 1
    prior_rows = passed_along(projected[:, tok_rows - rim_width :, :], "seq", 1)
    featured = featurize(jnp.concatenate([prior_rows, projected], axis=1), feat_weight, tok_rows)
    gated_kv = multiply_round(featured[1], featured[2])
    kv_cols = jnp.transpose(gated_kv, (1, 0))
    kv_owned = lax.all_to_all(kv_cols, "seq", split_axis=0, concat_axis=1, tiled=True)
    filtered = long_mix(kv_owned, spectrum, skip_gain, tables)
    filtered_home = lax.all_to_all(filtered, "seq", split_axis=1, concat_axis=0, tiled=True)
    gated = multiply_round(featured[0], jnp.transpose(filtered_home, (1, 0)))
    block_count = local_ch // BLK
    out_width = out_values.shape[1]
    stacked = gated.reshape(tok_rows, block_count, BLK)
    weight_blocks = out_values.reshape(block_count, BLK, out_width)
    scale_cols = jnp.repeat(out_scales, BLK, axis=1)
    products = jnp.einsum(
        "tbk,bkn->btn", stacked, weight_blocks, preferred_element_type=jnp.float32
    )
    partial = jnp.sum(products * scale_cols[:, None, :], axis=0).astype(jnp.bfloat16)
    summed = lax.psum_scatter(partial, "tensor", scatter_dimension=1, tiled=True)
    return summed


def solution(mesh):
    return jax.shard_map(
        local,
        mesh=mesh,
        in_specs=(
            P(None, "seq", "tensor"),
            P(None, None, "tensor"),
            P(("tensor", "seq"), None),
            P(("tensor", "seq")),
            P("tensor", None),
            P("tensor", None),
        ),
        out_specs=P("seq", "tensor"),
        check_vma=False,
    )
```

```python
import math

import jax
import jax.numpy as jnp
from jax import lax
from jax.sharding import PartitionSpec as P

KS = 7
BLK = 128


TRIPLE = lax.Precision.HIGH


def passed_along(x, axis, by):
    size = lax.axis_size(axis)
    pairs = [(i, i + by) for i in range(size) if 0 <= i + by < size]
    return lax.ppermute(x, axis, pairs)


def split_length(whole):
    for candidate in range(2, whole + 1, 2):
        if whole % candidate == 0 and candidate * candidate >= whole:
            return (candidate, whole // candidate)
    return (whole, 1)


def angle_pair(row_count, col_count, period):
    row_ids = lax.broadcasted_iota(jnp.int32, (row_count, col_count), 0)
    col_ids = lax.broadcasted_iota(jnp.int32, (row_count, col_count), 1)
    angles = (row_ids * col_ids % period).astype(jnp.float32) * (2.0 * math.pi / period)
    return (jnp.cos(angles), jnp.sin(angles))


def make_tables(length):
    whole = 2 * length
    size_a, size_b = split_length(whole)
    return (
        angle_pair(size_a, size_a, size_a),
        angle_pair(size_b, size_b, size_b),
        angle_pair(size_a, size_b, whole),
        size_a,
        size_b,
    )


def right_mul(signal, matrix):
    return jnp.einsum("ckn,nm->ckm", signal, matrix, precision=TRIPLE)


def forward(signal, tables):
    (cos_a, sin_a), (cos_b, sin_b), (cos_t, sin_t), size_a, size_b = tables
    half_a = size_a // 2
    blocks = signal.reshape(signal.shape[0], half_a, size_b)
    real_a = jnp.einsum("kn,cnb->ckb", cos_a[:, :half_a], blocks, precision=TRIPLE)
    imag_a = -jnp.einsum("kn,cnb->ckb", sin_a[:, :half_a], blocks, precision=TRIPLE)
    real_t = real_a * cos_t + imag_a * sin_t
    imag_t = imag_a * cos_t - real_a * sin_t
    real_f = right_mul(real_t, cos_b) + right_mul(imag_t, sin_b)
    imag_f = right_mul(imag_t, cos_b) - right_mul(real_t, sin_b)
    return (real_f, imag_f)


def inverse(real_f, imag_f, tables):
    (cos_a, sin_a), (cos_b, sin_b), (cos_t, sin_t), size_a, size_b = tables
    half_a = size_a // 2
    real_z = right_mul(real_f, cos_b) - right_mul(imag_f, sin_b)
    imag_z = right_mul(imag_f, cos_b) + right_mul(real_f, sin_b)
    real_w = real_z * cos_t - imag_z * sin_t
    imag_w = imag_z * cos_t + real_z * sin_t
    out_half = jnp.einsum("nk,ckb->cnb", cos_a[:half_a, :], real_w, precision=TRIPLE) - jnp.einsum(
        "nk,ckb->cnb", sin_a[:half_a, :], imag_w, precision=TRIPLE
    )
    return out_half.reshape(out_half.shape[0], half_a * size_b) * (1.0 / (size_a * size_b))


def long_mix(gated_kv, spectrum, own_gain, tables):
    kv_values = gated_kv.astype(jnp.float32)
    real_u, imag_u = forward(kv_values, tables)
    real_h, imag_h = spectrum
    real_p = real_u * real_h - imag_u * imag_h
    imag_p = real_u * imag_h + imag_u * real_h
    convolved = inverse(real_p, imag_p, tables)
    return (convolved + own_gain[:, None] * kv_values).astype(jnp.bfloat16)


def featurize(extended, weights, length):
    tap_count = weights.shape[1]
    running = jnp.zeros(extended.shape[:1] + (length,) + extended.shape[2:], jnp.float32)
    for lag_idx in range(tap_count):
        offset = tap_count - 1 - lag_idx
        running = running + weights[:, lag_idx, None, :] * extended[
            :, offset : offset + length, :
        ].astype(jnp.float32)
    return running.astype(jnp.bfloat16)


def multiply_round(left_arr, right_arr):
    return (left_arr.astype(jnp.float32) * right_arr.astype(jnp.float32)).astype(jnp.bfloat16)


def local(projected, feat_weight, long_filter, skip_gain, out_values, out_scales):
    groups = lax.axis_size("seq")
    tok_rows = projected.shape[1]
    local_ch = projected.shape[2]
    length = tok_rows * groups
    tables = make_tables(length)
    spectrum = forward(long_filter, tables)
    rim_width = KS - 1
    prior_rows = passed_along(projected[:, tok_rows - rim_width :, :], "seq", 1)
    featured = featurize(jnp.concatenate([prior_rows, projected], axis=1), feat_weight, tok_rows)
    gated_kv = multiply_round(featured[1], featured[2])
    kv_cols = jnp.transpose(gated_kv, (1, 0))
    kv_owned = lax.all_to_all(kv_cols, "seq", split_axis=0, concat_axis=1, tiled=True)
    filtered = long_mix(kv_owned, spectrum, skip_gain, tables)
    filtered_home = lax.all_to_all(filtered, "seq", split_axis=1, concat_axis=0, tiled=True)
    gated = multiply_round(featured[0], jnp.transpose(filtered_home, (1, 0)))
    block_count = local_ch // BLK
    out_width = out_values.shape[1]
    stacked = gated.reshape(tok_rows, block_count, BLK)
    weight_blocks = out_values.reshape(block_count, BLK, out_width)
    scale_cols = jnp.repeat(out_scales, BLK, axis=1)
    products = jnp.einsum(
        "tbk,bkn->btn", stacked, weight_blocks, preferred_element_type=jnp.float32
    )
    partial = jnp.sum(products * scale_cols[:, None, :], axis=0).astype(jnp.bfloat16)
    n_tensor = lax.axis_size("tensor")
    pieces = partial.reshape(tok_rows, n_tensor, out_width // n_tensor).transpose(1, 0, 2)
    gathered = lax.all_to_all(pieces, "tensor", 0, 0, tiled=True)
    return jnp.sum(gathered.astype(jnp.float32), axis=0).astype(jnp.bfloat16)


def solution(mesh):
    return jax.shard_map(
        local,
        mesh=mesh,
        in_specs=(
            P(None, "seq", "tensor"),
            P(None, None, "tensor"),
            P(("tensor", "seq"), None),
            P(("tensor", "seq")),
            P("tensor", None),
            P("tensor", None),
        ),
        out_specs=P("seq", "tensor"),
        check_vma=False,
    )
```

```python
import math

import jax
import jax.numpy as jnp
from jax import lax
from jax.sharding import PartitionSpec as P
from jax.experimental import pallas as pl
from jax.experimental.pallas import tpu as pltpu

KS = 7
BLK = 128


TRIPLE = lax.Precision.HIGH


def passed_along(x, axis, by):
    size = lax.axis_size(axis)
    pairs = [(i, i + by) for i in range(size) if 0 <= i + by < size]
    return lax.ppermute(x, axis, pairs)


def split_length(whole):
    for candidate in range(2, whole + 1, 2):
        if whole % candidate == 0 and candidate * candidate >= whole:
            return (candidate, whole // candidate)
    return (whole, 1)


def angle_pair(row_count, col_count, period):
    row_ids = lax.broadcasted_iota(jnp.int32, (row_count, col_count), 0)
    col_ids = lax.broadcasted_iota(jnp.int32, (row_count, col_count), 1)
    angles = (row_ids * col_ids % period).astype(jnp.float32) * (2.0 * math.pi / period)
    return (jnp.cos(angles), jnp.sin(angles))


def make_tables(length):
    whole = 2 * length
    size_a, size_b = split_length(whole)
    return (
        angle_pair(size_a, size_a, size_a),
        angle_pair(size_b, size_b, size_b),
        angle_pair(size_a, size_b, whole),
        size_a,
        size_b,
    )


def right_mul(signal, matrix):
    return jnp.einsum("ckn,nm->ckm", signal, matrix, precision=TRIPLE)


def forward(signal, tables):
    (cos_a, sin_a), (cos_b, sin_b), (cos_t, sin_t), size_a, size_b = tables
    half_a = size_a // 2
    blocks = signal.reshape(signal.shape[0], half_a, size_b)
    real_a = jnp.einsum("kn,cnb->ckb", cos_a[:, :half_a], blocks, precision=TRIPLE)
    imag_a = -jnp.einsum("kn,cnb->ckb", sin_a[:, :half_a], blocks, precision=TRIPLE)
    real_t = real_a * cos_t + imag_a * sin_t
    imag_t = imag_a * cos_t - real_a * sin_t
    real_f = right_mul(real_t, cos_b) + right_mul(imag_t, sin_b)
    imag_f = right_mul(imag_t, cos_b) - right_mul(real_t, sin_b)
    return (real_f, imag_f)


def inverse(real_f, imag_f, tables):
    (cos_a, sin_a), (cos_b, sin_b), (cos_t, sin_t), size_a, size_b = tables
    half_a = size_a // 2
    real_z = right_mul(real_f, cos_b) - right_mul(imag_f, sin_b)
    imag_z = right_mul(imag_f, cos_b) + right_mul(real_f, sin_b)
    real_w = real_z * cos_t - imag_z * sin_t
    imag_w = imag_z * cos_t + real_z * sin_t
    out_half = jnp.einsum("nk,ckb->cnb", cos_a[:half_a, :], real_w, precision=TRIPLE) - jnp.einsum(
        "nk,ckb->cnb", sin_a[:half_a, :], imag_w, precision=TRIPLE
    )
    return out_half.reshape(out_half.shape[0], half_a * size_b) * (1.0 / (size_a * size_b))


def long_mix(gated_kv, spectrum, own_gain, tables):
    kv_values = gated_kv.astype(jnp.float32)
    real_u, imag_u = forward(kv_values, tables)
    real_h, imag_h = spectrum
    real_p = real_u * real_h - imag_u * imag_h
    imag_p = real_u * imag_h + imag_u * real_h
    convolved = inverse(real_p, imag_p, tables)
    return (convolved + own_gain[:, None] * kv_values).astype(jnp.bfloat16)


def featurize(extended, weights, length):
    tap_count = weights.shape[1]
    running = jnp.zeros(extended.shape[:1] + (length,) + extended.shape[2:], jnp.float32)
    for lag_idx in range(tap_count):
        offset = tap_count - 1 - lag_idx
        running = running + weights[:, lag_idx, None, :] * extended[
            :, offset : offset + length, :
        ].astype(jnp.float32)
    return running.astype(jnp.bfloat16)


def _feat_body(proj_ref, prior_ref, w_ref, q_ref, kv_ref, ext_ref):
    rows = proj_ref.shape[1]
    feats = []
    for a in range(3):
        ext_ref[0:2, :] = jnp.zeros((2, ext_ref.shape[1]), jnp.float32)
        ext_ref[2:8, :] = prior_ref[a].astype(jnp.float32)
        ext_ref[8 : 8 + rows, :] = proj_ref[a].astype(jnp.float32)
        acc = jnp.zeros((rows, ext_ref.shape[1]), jnp.float32)
        for j in range(KS):
            acc = acc + w_ref[a, j : j + 1, :] * ext_ref[8 - j : 8 - j + rows, :]
        feats.append(acc.astype(jnp.bfloat16))
    q_ref[...] = feats[0]
    kv_ref[...] = (feats[1].astype(jnp.float32) * feats[2].astype(jnp.float32)).astype(jnp.bfloat16)

def featurize_kv(projected, prior, weights, lane_block=128, interpret=False):
    _, rows, chans = projected.shape
    grid = (chans // lane_block,)
    return pl.pallas_call(
        _feat_body,
        grid=grid,
        in_specs=[
            pl.BlockSpec((3, rows, lane_block), lambda i: (0, 0, i)),
            pl.BlockSpec((3, KS - 1, lane_block), lambda i: (0, 0, i)),
            pl.BlockSpec((3, KS, lane_block), lambda i: (0, 0, i)),
        ],
        out_specs=[
            pl.BlockSpec((rows, lane_block), lambda i: (0, i)),
            pl.BlockSpec((rows, lane_block), lambda i: (0, i)),
        ],
        out_shape=[jax.ShapeDtypeStruct((rows, chans), jnp.bfloat16)] * 2,
        scratch_shapes=[pltpu.VMEM((rows + 8, lane_block), jnp.float32)],
        interpret=interpret,
    )(projected, prior, weights)


def multiply_round(left_arr, right_arr):
    return (left_arr.astype(jnp.float32) * right_arr.astype(jnp.float32)).astype(jnp.bfloat16)


def local(projected, feat_weight, long_filter, skip_gain, out_values, out_scales):
    groups = lax.axis_size("seq")
    tok_rows = projected.shape[1]
    local_ch = projected.shape[2]
    length = tok_rows * groups
    tables = make_tables(length)
    spectrum = forward(long_filter, tables)
    rim_width = KS - 1
    prior_rows = passed_along(projected[:, tok_rows - rim_width :, :], "seq", 1)
    q_feat, gated_kv = featurize_kv(projected, prior_rows, feat_weight)
    kv_cols = jnp.transpose(gated_kv, (1, 0))
    kv_owned = lax.all_to_all(kv_cols, "seq", split_axis=0, concat_axis=1, tiled=True)
    filtered = long_mix(kv_owned, spectrum, skip_gain, tables)
    filtered_home = lax.all_to_all(filtered, "seq", split_axis=1, concat_axis=0, tiled=True)
    gated = multiply_round(q_feat, jnp.transpose(filtered_home, (1, 0)))
    block_count = local_ch // BLK
    out_width = out_values.shape[1]
    stacked = gated.reshape(tok_rows, block_count, BLK)
    weight_blocks = out_values.reshape(block_count, BLK, out_width)
    scale_cols = jnp.repeat(out_scales, BLK, axis=1)
    products = jnp.einsum(
        "tbk,bkn->btn", stacked, weight_blocks, preferred_element_type=jnp.float32
    )
    partial = jnp.sum(products * scale_cols[:, None, :], axis=0).astype(jnp.bfloat16)
    n_tensor = lax.axis_size("tensor")
    pieces = partial.reshape(tok_rows, n_tensor, out_width // n_tensor).transpose(1, 0, 2)
    gathered = lax.all_to_all(pieces, "tensor", 0, 0, tiled=True)
    return jnp.sum(gathered.astype(jnp.float32), axis=0).astype(jnp.bfloat16)


def solution(mesh):
    return jax.shard_map(
        local,
        mesh=mesh,
        in_specs=(
            P(None, "seq", "tensor"),
            P(None, None, "tensor"),
            P(("tensor", "seq"), None),
            P(("tensor", "seq")),
            P("tensor", None),
            P("tensor", None),
        ),
        out_specs=P("seq", "tensor"),
        check_vma=False,
    )
```

```python
import math

import jax
import jax.numpy as jnp
from jax import lax
from jax.sharding import PartitionSpec as P
from jax.experimental import pallas as pl
from jax.experimental.pallas import tpu as pltpu

KS = 7
BLK = 128


TRIPLE = lax.Precision.HIGH


def passed_along(x, axis, by):
    size = lax.axis_size(axis)
    pairs = [(i, i + by) for i in range(size) if 0 <= i + by < size]
    return lax.ppermute(x, axis, pairs)


def split_length(whole):
    for candidate in range(2, whole + 1, 2):
        if whole % candidate == 0 and candidate * candidate >= whole:
            return (candidate, whole // candidate)
    return (whole, 1)


def angle_pair(row_count, col_count, period):
    row_ids = lax.broadcasted_iota(jnp.int32, (row_count, col_count), 0)
    col_ids = lax.broadcasted_iota(jnp.int32, (row_count, col_count), 1)
    angles = (row_ids * col_ids % period).astype(jnp.float32) * (2.0 * math.pi / period)
    return (jnp.cos(angles), jnp.sin(angles))


def make_tables(length):
    whole = 2 * length
    size_a, size_b = split_length(whole)
    return (
        angle_pair(size_a, size_a, size_a),
        angle_pair(size_b, size_b, size_b),
        angle_pair(size_a, size_b, whole),
        size_a,
        size_b,
    )


def right_mul(signal, matrix):
    return jnp.einsum("ckn,nm->ckm", signal, matrix, precision=TRIPLE)


def forward(signal, tables):
    (cos_a, sin_a), (cos_b, sin_b), (cos_t, sin_t), size_a, size_b = tables
    half_a = size_a // 2
    blocks = signal.reshape(signal.shape[0], half_a, size_b)
    real_a = jnp.einsum("kn,cnb->ckb", cos_a[:, :half_a], blocks, precision=TRIPLE)
    imag_a = -jnp.einsum("kn,cnb->ckb", sin_a[:, :half_a], blocks, precision=TRIPLE)
    real_t = real_a * cos_t + imag_a * sin_t
    imag_t = imag_a * cos_t - real_a * sin_t
    real_f = right_mul(real_t, cos_b) + right_mul(imag_t, sin_b)
    imag_f = right_mul(imag_t, cos_b) - right_mul(real_t, sin_b)
    return (real_f, imag_f)


def inverse(real_f, imag_f, tables):
    (cos_a, sin_a), (cos_b, sin_b), (cos_t, sin_t), size_a, size_b = tables
    half_a = size_a // 2
    real_z = right_mul(real_f, cos_b) - right_mul(imag_f, sin_b)
    imag_z = right_mul(imag_f, cos_b) + right_mul(real_f, sin_b)
    real_w = real_z * cos_t - imag_z * sin_t
    imag_w = imag_z * cos_t + real_z * sin_t
    out_half = jnp.einsum("nk,ckb->cnb", cos_a[:half_a, :], real_w, precision=TRIPLE) - jnp.einsum(
        "nk,ckb->cnb", sin_a[:half_a, :], imag_w, precision=TRIPLE
    )
    return out_half.reshape(out_half.shape[0], half_a * size_b) * (1.0 / (size_a * size_b))


def long_mix(gated_kv, spectrum, own_gain, tables):
    kv_values = gated_kv.astype(jnp.float32)
    real_u, imag_u = forward(kv_values, tables)
    real_h, imag_h = spectrum
    real_p = real_u * real_h - imag_u * imag_h
    imag_p = real_u * imag_h + imag_u * real_h
    convolved = inverse(real_p, imag_p, tables)
    return (convolved + own_gain[:, None] * kv_values).astype(jnp.bfloat16)


def featurize(extended, weights, length):
    tap_count = weights.shape[1]
    running = jnp.zeros(extended.shape[:1] + (length,) + extended.shape[2:], jnp.float32)
    for lag_idx in range(tap_count):
        offset = tap_count - 1 - lag_idx
        running = running + weights[:, lag_idx, None, :] * extended[
            :, offset : offset + length, :
        ].astype(jnp.float32)
    return running.astype(jnp.bfloat16)


def _feat_body(proj_ref, prior_ref, w_ref, q_ref, kv_ref, ext_ref):
    rows = proj_ref.shape[1]
    feats = []
    for a in range(3):
        ext_ref[0:2, :] = jnp.zeros((2, ext_ref.shape[1]), jnp.float32)
        ext_ref[2:8, :] = prior_ref[a].astype(jnp.float32)
        ext_ref[8 : 8 + rows, :] = proj_ref[a].astype(jnp.float32)
        acc = jnp.zeros((rows, ext_ref.shape[1]), jnp.float32)
        for j in range(KS):
            acc = acc + w_ref[a, j : j + 1, :] * ext_ref[8 - j : 8 - j + rows, :]
        feats.append(acc.astype(jnp.bfloat16))
    q_ref[...] = feats[0]
    kv_ref[...] = (feats[1].astype(jnp.float32) * feats[2].astype(jnp.float32)).astype(jnp.bfloat16)

def featurize_kv(projected, prior, weights, lane_block=128, interpret=False):
    _, rows, chans = projected.shape
    grid = (chans // lane_block,)
    return pl.pallas_call(
        _feat_body,
        grid=grid,
        in_specs=[
            pl.BlockSpec((3, rows, lane_block), lambda i: (0, 0, i)),
            pl.BlockSpec((3, KS - 1, lane_block), lambda i: (0, 0, i)),
            pl.BlockSpec((3, KS, lane_block), lambda i: (0, 0, i)),
        ],
        out_specs=[
            pl.BlockSpec((rows, lane_block), lambda i: (0, i)),
            pl.BlockSpec((rows, lane_block), lambda i: (0, i)),
        ],
        out_shape=[jax.ShapeDtypeStruct((rows, chans), jnp.bfloat16)] * 2,
        scratch_shapes=[pltpu.VMEM((rows + 8, lane_block), jnp.float32)],
        interpret=interpret,
    )(projected, prior, weights)


def _split(a):
    hi = a.astype(jnp.bfloat16)
    return hi, (a - hi.astype(jnp.float32)).astype(jnp.bfloat16)


def _mm(a, b):
    return jnp.dot(a, b, preferred_element_type=jnp.float32)


def _left3(t_hi, t_lo, v):
    v_hi, v_lo = _split(v)
    return _mm(t_hi, v_hi) + _mm(t_lo, v_hi) + _mm(t_hi, v_lo)


def _right3(v, t_hi, t_lo):
    v_hi, v_lo = _split(v)
    return _mm(v_hi, t_hi) + _mm(v_lo, t_hi) + _mm(v_hi, t_lo)


def _conv_body(x_ref, h_ref, g_ref, ca_h, ca_l, sa_h, sa_l, cb_h, cb_l, sb_h, sb_l,
               ct_ref, st_ref, inv_h, inv_l, o_ref):
    rows = ct_ref.shape[0]
    ct = ct_ref[...]
    st = st_ref[...]

    def spectrum(a_re, a_im):
        t_re = a_re * ct + a_im * st
        t_im = a_im * ct - a_re * st
        stacked = jnp.concatenate([t_re, t_im], axis=0)
        r_c = _right3(stacked, cb_h[...], cb_l[...])
        r_s = _right3(stacked, sb_h[...], sb_l[...])
        return r_c[:rows] + r_s[rows:], r_c[rows:] - r_s[:rows]

    for c in range(x_ref.shape[0]):
        h = h_ref[c]
        fh_re, fh_im = spectrum(_left3(ca_h[...], ca_l[...], h), -_left3(sa_h[...], sa_l[...], h))
        x_b = x_ref[c]
        a_re = _mm(ca_h[...], x_b) + _mm(ca_l[...], x_b)
        a_im = -(_mm(sa_h[...], x_b) + _mm(sa_l[...], x_b))
        fx_re, fx_im = spectrum(a_re, a_im)
        p_re = fx_re * fh_re - fx_im * fh_im
        p_im = fx_re * fh_im + fx_im * fh_re
        stacked = jnp.concatenate([p_re, p_im], axis=0)
        q_c = _right3(stacked, cb_h[...], cb_l[...])
        q_s = _right3(stacked, sb_h[...], sb_l[...])
        z_re = q_c[:rows] - q_s[rows:]
        z_im = q_c[rows:] + q_s[:rows]
        w_re = z_re * ct - z_im * st
        w_im = z_im * ct + z_re * st
        out = _left3(inv_h[...], inv_l[...], jnp.concatenate([w_re, w_im], axis=0))
        x_f = x_b.astype(jnp.float32)
        o_ref[c] = (out * (1.0 / (rows * ct_ref.shape[1])) + g_ref[c] * x_f).astype(jnp.bfloat16)


def conv_tables(size_a, size_b):
    whole = size_a * size_b
    half_a = size_a // 2

    def pair(r, c, period):
        ri = lax.broadcasted_iota(jnp.int32, (r, c), 0)
        ci = lax.broadcasted_iota(jnp.int32, (r, c), 1)
        ang = (ri * ci % period).astype(jnp.float32) * (2.0 * math.pi / period)
        return jnp.cos(ang), jnp.sin(ang)

    cos_a, sin_a = pair(size_a, half_a, size_a)
    cos_b, sin_b = pair(size_b, size_b, size_b)
    cos_t, sin_t = pair(size_a, size_b, whole)
    inv = jnp.concatenate([cos_a.T, -sin_a.T], axis=1)
    return (*_split(cos_a), *_split(sin_a), *_split(cos_b), *_split(sin_b), cos_t, sin_t, *_split(inv))


def long_conv(kv, filt, gain, ch_block=2, interpret=False):
    ch, length = kv.shape
    size_b = 128
    half_a = length // size_b
    size_a = 2 * half_a
    x = kv.reshape(ch, half_a, size_b)
    h = filt.reshape(ch, half_a, size_b)
    g = jnp.broadcast_to(gain[:, None, None], (ch, 1, size_b))
    tabs = conv_tables(size_a, size_b)
    full = lambda t: pl.BlockSpec(t.shape, lambda i: (0,) * t.ndim)
    out = pl.pallas_call(
        _conv_body,
        grid=(ch // ch_block,),
        in_specs=[
            pl.BlockSpec((ch_block, half_a, size_b), lambda i: (i, 0, 0)),
            pl.BlockSpec((ch_block, half_a, size_b), lambda i: (i, 0, 0)),
            pl.BlockSpec((ch_block, 1, size_b), lambda i: (i, 0, 0)),
        ] + [full(t) for t in tabs],
        out_specs=pl.BlockSpec((ch_block, half_a, size_b), lambda i: (i, 0, 0)),
        out_shape=jax.ShapeDtypeStruct((ch, half_a, size_b), jnp.bfloat16),
        interpret=interpret,
    )(x, h, g, *tabs)
    return out.reshape(ch, length)


def multiply_round(left_arr, right_arr):
    return (left_arr.astype(jnp.float32) * right_arr.astype(jnp.float32)).astype(jnp.bfloat16)


def local(projected, feat_weight, long_filter, skip_gain, out_values, out_scales):
    groups = lax.axis_size("seq")
    tok_rows = projected.shape[1]
    local_ch = projected.shape[2]
    length = tok_rows * groups
    rim_width = KS - 1
    prior_rows = passed_along(projected[:, tok_rows - rim_width :, :], "seq", 1)
    q_feat, gated_kv = featurize_kv(projected, prior_rows, feat_weight)
    kv_cols = jnp.transpose(gated_kv, (1, 0))
    kv_owned = lax.all_to_all(kv_cols, "seq", split_axis=0, concat_axis=1, tiled=True)
    filtered = long_conv(kv_owned, long_filter, skip_gain)
    filtered_home = lax.all_to_all(filtered, "seq", split_axis=1, concat_axis=0, tiled=True)
    gated = multiply_round(q_feat, jnp.transpose(filtered_home, (1, 0)))
    block_count = local_ch // BLK
    out_width = out_values.shape[1]
    stacked = gated.reshape(tok_rows, block_count, BLK)
    weight_blocks = out_values.reshape(block_count, BLK, out_width)
    scale_cols = jnp.repeat(out_scales, BLK, axis=1)
    products = jnp.einsum(
        "tbk,bkn->btn", stacked, weight_blocks, preferred_element_type=jnp.float32
    )
    partial = jnp.sum(products * scale_cols[:, None, :], axis=0).astype(jnp.bfloat16)
    n_tensor = lax.axis_size("tensor")
    pieces = partial.reshape(tok_rows, n_tensor, out_width // n_tensor).transpose(1, 0, 2)
    gathered = lax.all_to_all(pieces, "tensor", 0, 0, tiled=True)
    return jnp.sum(gathered.astype(jnp.float32), axis=0).astype(jnp.bfloat16)


def solution(mesh):
    return jax.shard_map(
        local,
        mesh=mesh,
        in_specs=(
            P(None, "seq", "tensor"),
            P(None, None, "tensor"),
            P(("tensor", "seq"), None),
            P(("tensor", "seq")),
            P("tensor", None),
            P("tensor", None),
        ),
        out_specs=P("seq", "tensor"),
        check_vma=False,
    )
```

```python
import math

import jax
import jax.numpy as jnp
from jax import lax
from jax.sharding import PartitionSpec as P
from jax.experimental import pallas as pl
from jax.experimental.pallas import tpu as pltpu

KS = 7
BLK = 128


TRIPLE = lax.Precision.HIGH


def passed_along(x, axis, by):
    size = lax.axis_size(axis)
    pairs = [(i, i + by) for i in range(size) if 0 <= i + by < size]
    return lax.ppermute(x, axis, pairs)


def split_length(whole):
    for candidate in range(2, whole + 1, 2):
        if whole % candidate == 0 and candidate * candidate >= whole:
            return (candidate, whole // candidate)
    return (whole, 1)


def angle_pair(row_count, col_count, period):
    row_ids = lax.broadcasted_iota(jnp.int32, (row_count, col_count), 0)
    col_ids = lax.broadcasted_iota(jnp.int32, (row_count, col_count), 1)
    angles = (row_ids * col_ids % period).astype(jnp.float32) * (2.0 * math.pi / period)
    return (jnp.cos(angles), jnp.sin(angles))


def make_tables(length):
    whole = 2 * length
    size_a, size_b = split_length(whole)
    return (
        angle_pair(size_a, size_a, size_a),
        angle_pair(size_b, size_b, size_b),
        angle_pair(size_a, size_b, whole),
        size_a,
        size_b,
    )


def right_mul(signal, matrix):
    return jnp.einsum("ckn,nm->ckm", signal, matrix, precision=TRIPLE)


def forward(signal, tables):
    (cos_a, sin_a), (cos_b, sin_b), (cos_t, sin_t), size_a, size_b = tables
    half_a = size_a // 2
    blocks = signal.reshape(signal.shape[0], half_a, size_b)
    real_a = jnp.einsum("kn,cnb->ckb", cos_a[:, :half_a], blocks, precision=TRIPLE)
    imag_a = -jnp.einsum("kn,cnb->ckb", sin_a[:, :half_a], blocks, precision=TRIPLE)
    real_t = real_a * cos_t + imag_a * sin_t
    imag_t = imag_a * cos_t - real_a * sin_t
    real_f = right_mul(real_t, cos_b) + right_mul(imag_t, sin_b)
    imag_f = right_mul(imag_t, cos_b) - right_mul(real_t, sin_b)
    return (real_f, imag_f)


def inverse(real_f, imag_f, tables):
    (cos_a, sin_a), (cos_b, sin_b), (cos_t, sin_t), size_a, size_b = tables
    half_a = size_a // 2
    real_z = right_mul(real_f, cos_b) - right_mul(imag_f, sin_b)
    imag_z = right_mul(imag_f, cos_b) + right_mul(real_f, sin_b)
    real_w = real_z * cos_t - imag_z * sin_t
    imag_w = imag_z * cos_t + real_z * sin_t
    out_half = jnp.einsum("nk,ckb->cnb", cos_a[:half_a, :], real_w, precision=TRIPLE) - jnp.einsum(
        "nk,ckb->cnb", sin_a[:half_a, :], imag_w, precision=TRIPLE
    )
    return out_half.reshape(out_half.shape[0], half_a * size_b) * (1.0 / (size_a * size_b))


def long_mix(gated_kv, spectrum, own_gain, tables):
    kv_values = gated_kv.astype(jnp.float32)
    real_u, imag_u = forward(kv_values, tables)
    real_h, imag_h = spectrum
    real_p = real_u * real_h - imag_u * imag_h
    imag_p = real_u * imag_h + imag_u * real_h
    convolved = inverse(real_p, imag_p, tables)
    return (convolved + own_gain[:, None] * kv_values).astype(jnp.bfloat16)


def featurize(extended, weights, length):
    tap_count = weights.shape[1]
    running = jnp.zeros(extended.shape[:1] + (length,) + extended.shape[2:], jnp.float32)
    for lag_idx in range(tap_count):
        offset = tap_count - 1 - lag_idx
        running = running + weights[:, lag_idx, None, :] * extended[
            :, offset : offset + length, :
        ].astype(jnp.float32)
    return running.astype(jnp.bfloat16)


def _feat_body(proj_ref, prior_ref, w_ref, q_ref, kv_ref, ext_ref):
    rows = proj_ref.shape[1]
    feats = []
    for a in range(3):
        ext_ref[0:2, :] = jnp.zeros((2, ext_ref.shape[1]), jnp.float32)
        ext_ref[2:8, :] = prior_ref[a].astype(jnp.float32)
        ext_ref[8 : 8 + rows, :] = proj_ref[a].astype(jnp.float32)
        acc = jnp.zeros((rows, ext_ref.shape[1]), jnp.float32)
        for j in range(KS):
            acc = acc + w_ref[a, j : j + 1, :] * ext_ref[8 - j : 8 - j + rows, :]
        feats.append(acc.astype(jnp.bfloat16))
    q_ref[...] = feats[0]
    kv_ref[...] = (feats[1].astype(jnp.float32) * feats[2].astype(jnp.float32)).astype(jnp.bfloat16)

def featurize_kv(projected, prior, weights, lane_block=128, interpret=False):
    _, rows, chans = projected.shape
    grid = (chans // lane_block,)
    return pl.pallas_call(
        _feat_body,
        grid=grid,
        in_specs=[
            pl.BlockSpec((3, rows, lane_block), lambda i: (0, 0, i)),
            pl.BlockSpec((3, KS - 1, lane_block), lambda i: (0, 0, i)),
            pl.BlockSpec((3, KS, lane_block), lambda i: (0, 0, i)),
        ],
        out_specs=[
            pl.BlockSpec((rows, lane_block), lambda i: (0, i)),
            pl.BlockSpec((rows, lane_block), lambda i: (0, i)),
        ],
        out_shape=[jax.ShapeDtypeStruct((rows, chans), jnp.bfloat16)] * 2,
        scratch_shapes=[pltpu.VMEM((rows + 8, lane_block), jnp.float32)],
        interpret=interpret,
    )(projected, prior, weights)


def _split(a):
    hi = a.astype(jnp.bfloat16)
    return hi, (a - hi.astype(jnp.float32)).astype(jnp.bfloat16)


def _mm(a, b):
    return jnp.dot(a, b, preferred_element_type=jnp.float32)


def _left3(t_hi, t_lo, v):
    v_hi, v_lo = _split(v)
    return _mm(t_hi, v_hi) + _mm(t_lo, v_hi) + _mm(t_hi, v_lo)


def _right3(v, t_hi, t_lo):
    v_hi, v_lo = _split(v)
    return _mm(v_hi, t_hi) + _mm(v_lo, t_hi) + _mm(v_hi, t_lo)


def _conv_body(x_ref, h_ref, g_ref, ca_h, ca_l, sa_h, sa_l, cb_h, cb_l, sb_h, sb_l,
               ct_ref, st_ref, inv_h, inv_l, o_ref):
    rows = ct_ref.shape[0]
    ct = ct_ref[...]
    st = st_ref[...]

    def spectrum(a_re, a_im):
        t_re = a_re * ct + a_im * st
        t_im = a_im * ct - a_re * st
        stacked = jnp.concatenate([t_re, t_im], axis=0)
        r_c = _right3(stacked, cb_h[...], cb_l[...])
        r_s = _right3(stacked, sb_h[...], sb_l[...])
        return r_c[:rows] + r_s[rows:], r_c[rows:] - r_s[:rows]

    for c in range(x_ref.shape[0]):
        h = h_ref[c]
        fh_re, fh_im = spectrum(_left3(ca_h[...], ca_l[...], h), -_left3(sa_h[...], sa_l[...], h))
        x_b = x_ref[c]
        a_re = _mm(ca_h[...], x_b) + _mm(ca_l[...], x_b)
        a_im = -(_mm(sa_h[...], x_b) + _mm(sa_l[...], x_b))
        fx_re, fx_im = spectrum(a_re, a_im)
        p_re = fx_re * fh_re - fx_im * fh_im
        p_im = fx_re * fh_im + fx_im * fh_re
        stacked = jnp.concatenate([p_re, p_im], axis=0)
        q_c = _right3(stacked, cb_h[...], cb_l[...])
        q_s = _right3(stacked, sb_h[...], sb_l[...])
        z_re = q_c[:rows] - q_s[rows:]
        z_im = q_c[rows:] + q_s[:rows]
        w_re = z_re * ct - z_im * st
        w_im = z_im * ct + z_re * st
        out = _left3(inv_h[...], inv_l[...], jnp.concatenate([w_re, w_im], axis=0))
        x_f = x_b.astype(jnp.float32)
        o_ref[c] = (out * (1.0 / (rows * ct_ref.shape[1])) + g_ref[c] * x_f).astype(jnp.bfloat16)


def conv_tables(size_a, size_b):
    whole = size_a * size_b
    half_a = size_a // 2

    def pair(r, c, period):
        ri = lax.broadcasted_iota(jnp.int32, (r, c), 0)
        ci = lax.broadcasted_iota(jnp.int32, (r, c), 1)
        ang = (ri * ci % period).astype(jnp.float32) * (2.0 * math.pi / period)
        return jnp.cos(ang), jnp.sin(ang)

    cos_a, sin_a = pair(size_a, half_a, size_a)
    cos_b, sin_b = pair(size_b, size_b, size_b)
    cos_t, sin_t = pair(size_a, size_b, whole)
    inv = jnp.concatenate([cos_a.T, -sin_a.T], axis=1)
    return (*_split(cos_a), *_split(sin_a), *_split(cos_b), *_split(sin_b), cos_t, sin_t, *_split(inv))


def long_conv(kv, filt, gain, ch_block=2, interpret=False):
    ch, length = kv.shape
    size_b = 128
    half_a = length // size_b
    size_a = 2 * half_a
    x = kv.reshape(ch, half_a, size_b)
    h = filt.reshape(ch, half_a, size_b)
    g = jnp.broadcast_to(gain[:, None, None], (ch, 1, size_b))
    tabs = conv_tables(size_a, size_b)
    full = lambda t: pl.BlockSpec(t.shape, lambda i: (0,) * t.ndim)
    out = pl.pallas_call(
        _conv_body,
        grid=(ch // ch_block,),
        in_specs=[
            pl.BlockSpec((ch_block, half_a, size_b), lambda i: (i, 0, 0)),
            pl.BlockSpec((ch_block, half_a, size_b), lambda i: (i, 0, 0)),
            pl.BlockSpec((ch_block, 1, size_b), lambda i: (i, 0, 0)),
        ] + [full(t) for t in tabs],
        out_specs=pl.BlockSpec((ch_block, half_a, size_b), lambda i: (i, 0, 0)),
        out_shape=jax.ShapeDtypeStruct((ch, half_a, size_b), jnp.bfloat16),
        interpret=interpret,
    )(x, h, g, *tabs)
    return out.reshape(ch, length)


def multiply_round(left_arr, right_arr):
    return (left_arr.astype(jnp.float32) * right_arr.astype(jnp.float32)).astype(jnp.bfloat16)


def reduce_over_tensor(pieces, me, n_tensor):
    total = lax.dynamic_index_in_dim(pieces, me, 0, keepdims=False).astype(jnp.float32)
    for shift in range(1, n_tensor):
        sent = lax.dynamic_index_in_dim(pieces, (me + shift) % n_tensor, 0, keepdims=False)
        pairs = [(i, (i + shift) % n_tensor) for i in range(n_tensor)]
        total = total + lax.ppermute(sent, "tensor", pairs).astype(jnp.float32)
    return total.astype(jnp.bfloat16)


def local(projected, feat_weight, long_filter, skip_gain, out_values, out_scales):
    groups = lax.axis_size("seq")
    tok_rows = projected.shape[1]
    local_ch = projected.shape[2]
    length = tok_rows * groups
    rim_width = KS - 1
    prior_rows = passed_along(projected[:, tok_rows - rim_width :, :], "seq", 1)
    q_feat, gated_kv = featurize_kv(projected, prior_rows, feat_weight)
    kv_cols = jnp.transpose(gated_kv, (1, 0))
    kv_owned = lax.all_to_all(kv_cols, "seq", split_axis=0, concat_axis=1, tiled=True)
    filtered = long_conv(kv_owned, long_filter, skip_gain)
    n_tensor = lax.axis_size("tensor")
    block_count = local_ch // BLK
    out_width = out_values.shape[1]
    piece_width = out_width // n_tensor
    weight_blocks = out_values.reshape(block_count, BLK, n_tensor, piece_width)
    scale_cols = jnp.repeat(out_scales, BLK, axis=1).reshape(block_count, n_tensor, 1, piece_width)
    me = lax.axis_index("tensor")
    chunks = 2
    chunk_rows = tok_rows // chunks
    by_chunk = filtered.reshape(filtered.shape[0], groups, chunks, chunk_rows)
    outs = []
    pieces = None
    for h in range(chunks):
        part = by_chunk[:, :, h, :].reshape(filtered.shape[0], groups * chunk_rows)
        if pieces is not None:
            part, pieces = lax.optimization_barrier((part, pieces))
            outs.append(reduce_over_tensor(pieces, me, n_tensor))
        part_home = lax.all_to_all(part, "seq", split_axis=1, concat_axis=0, tiled=True)
        q_part = q_feat[h * chunk_rows : (h + 1) * chunk_rows]
        gated = multiply_round(q_part, jnp.transpose(part_home, (1, 0)))
        stacked = gated.reshape(chunk_rows, block_count, BLK)
        products = jnp.einsum(
            "tbk,bkjn->bjtn", stacked, weight_blocks, preferred_element_type=jnp.float32
        )
        pieces = jnp.sum(products * scale_cols, axis=0).astype(jnp.bfloat16)
    outs.append(reduce_over_tensor(pieces, me, n_tensor))
    return jnp.concatenate(outs, axis=0)


def solution(mesh):
    return jax.shard_map(
        local,
        mesh=mesh,
        in_specs=(
            P(None, "seq", "tensor"),
            P(None, None, "tensor"),
            P(("tensor", "seq"), None),
            P(("tensor", "seq")),
            P("tensor", None),
            P("tensor", None),
        ),
        out_specs=P("seq", "tensor"),
        check_vma=False,
    )
```

```python
import math

import jax
import jax.numpy as jnp
from jax import lax
from jax.sharding import PartitionSpec as P
from jax.experimental import pallas as pl
from jax.experimental.pallas import tpu as pltpu

KS = 7
BLK = 128


TRIPLE = lax.Precision.HIGH


def passed_along(x, axis, by):
    size = lax.axis_size(axis)
    pairs = [(i, i + by) for i in range(size) if 0 <= i + by < size]
    return lax.ppermute(x, axis, pairs)


def split_length(whole):
    for candidate in range(2, whole + 1, 2):
        if whole % candidate == 0 and candidate * candidate >= whole:
            return (candidate, whole // candidate)
    return (whole, 1)


def angle_pair(row_count, col_count, period):
    row_ids = lax.broadcasted_iota(jnp.int32, (row_count, col_count), 0)
    col_ids = lax.broadcasted_iota(jnp.int32, (row_count, col_count), 1)
    angles = (row_ids * col_ids % period).astype(jnp.float32) * (2.0 * math.pi / period)
    return (jnp.cos(angles), jnp.sin(angles))


def make_tables(length):
    whole = 2 * length
    size_a, size_b = split_length(whole)
    return (
        angle_pair(size_a, size_a, size_a),
        angle_pair(size_b, size_b, size_b),
        angle_pair(size_a, size_b, whole),
        size_a,
        size_b,
    )


def right_mul(signal, matrix):
    return jnp.einsum("ckn,nm->ckm", signal, matrix, precision=TRIPLE)


def forward(signal, tables):
    (cos_a, sin_a), (cos_b, sin_b), (cos_t, sin_t), size_a, size_b = tables
    half_a = size_a // 2
    blocks = signal.reshape(signal.shape[0], half_a, size_b)
    real_a = jnp.einsum("kn,cnb->ckb", cos_a[:, :half_a], blocks, precision=TRIPLE)
    imag_a = -jnp.einsum("kn,cnb->ckb", sin_a[:, :half_a], blocks, precision=TRIPLE)
    real_t = real_a * cos_t + imag_a * sin_t
    imag_t = imag_a * cos_t - real_a * sin_t
    real_f = right_mul(real_t, cos_b) + right_mul(imag_t, sin_b)
    imag_f = right_mul(imag_t, cos_b) - right_mul(real_t, sin_b)
    return (real_f, imag_f)


def inverse(real_f, imag_f, tables):
    (cos_a, sin_a), (cos_b, sin_b), (cos_t, sin_t), size_a, size_b = tables
    half_a = size_a // 2
    real_z = right_mul(real_f, cos_b) - right_mul(imag_f, sin_b)
    imag_z = right_mul(imag_f, cos_b) + right_mul(real_f, sin_b)
    real_w = real_z * cos_t - imag_z * sin_t
    imag_w = imag_z * cos_t + real_z * sin_t
    out_half = jnp.einsum("nk,ckb->cnb", cos_a[:half_a, :], real_w, precision=TRIPLE) - jnp.einsum(
        "nk,ckb->cnb", sin_a[:half_a, :], imag_w, precision=TRIPLE
    )
    return out_half.reshape(out_half.shape[0], half_a * size_b) * (1.0 / (size_a * size_b))


def long_mix(gated_kv, spectrum, own_gain, tables):
    kv_values = gated_kv.astype(jnp.float32)
    real_u, imag_u = forward(kv_values, tables)
    real_h, imag_h = spectrum
    real_p = real_u * real_h - imag_u * imag_h
    imag_p = real_u * imag_h + imag_u * real_h
    convolved = inverse(real_p, imag_p, tables)
    return (convolved + own_gain[:, None] * kv_values).astype(jnp.bfloat16)


def featurize(extended, weights, length):
    tap_count = weights.shape[1]
    running = jnp.zeros(extended.shape[:1] + (length,) + extended.shape[2:], jnp.float32)
    for lag_idx in range(tap_count):
        offset = tap_count - 1 - lag_idx
        running = running + weights[:, lag_idx, None, :] * extended[
            :, offset : offset + length, :
        ].astype(jnp.float32)
    return running.astype(jnp.bfloat16)


def _feat_body(proj_ref, prior_ref, w_ref, q_ref, kv_ref, ext_ref):
    rows = proj_ref.shape[1]
    feats = []
    for a in range(3):
        ext_ref[0:2, :] = jnp.zeros((2, ext_ref.shape[1]), jnp.float32)
        ext_ref[2:8, :] = prior_ref[a].astype(jnp.float32)
        ext_ref[8 : 8 + rows, :] = proj_ref[a].astype(jnp.float32)
        acc = jnp.zeros((rows, ext_ref.shape[1]), jnp.float32)
        for j in range(KS):
            acc = acc + w_ref[a, j : j + 1, :] * ext_ref[8 - j : 8 - j + rows, :]
        feats.append(acc.astype(jnp.bfloat16))
    q_ref[...] = feats[0]
    kv_ref[...] = (feats[1].astype(jnp.float32) * feats[2].astype(jnp.float32)).astype(jnp.bfloat16)

def featurize_kv(projected, prior, weights, lane_block=128, interpret=False):
    _, rows, chans = projected.shape
    grid = (chans // lane_block,)
    return pl.pallas_call(
        _feat_body,
        grid=grid,
        in_specs=[
            pl.BlockSpec((3, rows, lane_block), lambda i: (0, 0, i)),
            pl.BlockSpec((3, KS - 1, lane_block), lambda i: (0, 0, i)),
            pl.BlockSpec((3, KS, lane_block), lambda i: (0, 0, i)),
        ],
        out_specs=[
            pl.BlockSpec((rows, lane_block), lambda i: (0, i)),
            pl.BlockSpec((rows, lane_block), lambda i: (0, i)),
        ],
        out_shape=[jax.ShapeDtypeStruct((rows, chans), jnp.bfloat16)] * 2,
        scratch_shapes=[pltpu.VMEM((rows + 8, lane_block), jnp.float32)],
        interpret=interpret,
    )(projected, prior, weights)


def _split(a):
    hi = a.astype(jnp.bfloat16)
    return hi, (a - hi.astype(jnp.float32)).astype(jnp.bfloat16)


def _mm(a, b):
    return jnp.dot(a, b, preferred_element_type=jnp.float32)


def _left3(t_hi, t_lo, v):
    v_hi, v_lo = _split(v)
    return _mm(t_hi, v_hi) + _mm(t_lo, v_hi) + _mm(t_hi, v_lo)


def _right3(v, t_hi, t_lo):
    v_hi, v_lo = _split(v)
    return _mm(v_hi, t_hi) + _mm(v_lo, t_hi) + _mm(v_hi, t_lo)


def _spectrum(a_re, a_im, ct, st, cb_h, cb_l, sb_h, sb_l):
    rows = ct.shape[0]
    t_re = a_re * ct + a_im * st
    t_im = a_im * ct - a_re * st
    stacked = jnp.concatenate([t_re, t_im], axis=0)
    r_c = _right3(stacked, cb_h, cb_l)
    r_s = _right3(stacked, sb_h, sb_l)
    return r_c[:rows] + r_s[rows:], r_c[rows:] - r_s[:rows]


def _filter_body(h_ref, ca_h, ca_l, sa_h, sa_l, cb_h, cb_l, sb_h, sb_l, ct_ref, st_ref, re_ref, im_ref):
    ct = ct_ref[...]
    st = st_ref[...]
    for c in range(h_ref.shape[0]):
        h = h_ref[c]
        a_re = _left3(ca_h[...], ca_l[...], h)
        a_im = -_left3(sa_h[...], sa_l[...], h)
        re_ref[c], im_ref[c] = _spectrum(a_re, a_im, ct, st, cb_h[...], cb_l[...], sb_h[...], sb_l[...])


def _conv_body(x_ref, fh_re_ref, fh_im_ref, g_ref, ca_h, ca_l, sa_h, sa_l, cb_h, cb_l, sb_h, sb_l,
               ct_ref, st_ref, inv_h, inv_l, o_ref):
    rows = ct_ref.shape[0]
    ct = ct_ref[...]
    st = st_ref[...]
    for c in range(x_ref.shape[0]):
        x_b = x_ref[c]
        a_re = _mm(ca_h[...], x_b) + _mm(ca_l[...], x_b)
        a_im = -(_mm(sa_h[...], x_b) + _mm(sa_l[...], x_b))
        fx_re, fx_im = _spectrum(a_re, a_im, ct, st, cb_h[...], cb_l[...], sb_h[...], sb_l[...])
        fh_re = fh_re_ref[c]
        fh_im = fh_im_ref[c]
        p_re = fx_re * fh_re - fx_im * fh_im
        p_im = fx_re * fh_im + fx_im * fh_re
        stacked = jnp.concatenate([p_re, p_im], axis=0)
        q_c = _right3(stacked, cb_h[...], cb_l[...])
        q_s = _right3(stacked, sb_h[...], sb_l[...])
        z_re = q_c[:rows] - q_s[rows:]
        z_im = q_c[rows:] + q_s[:rows]
        w_re = z_re * ct - z_im * st
        w_im = z_im * ct + z_re * st
        out = _left3(inv_h[...], inv_l[...], jnp.concatenate([w_re, w_im], axis=0))
        x_f = x_b.astype(jnp.float32)
        o_ref[c] = (out * (1.0 / (rows * ct_ref.shape[1])) + g_ref[c] * x_f).astype(jnp.bfloat16)


def conv_tables(size_a, size_b):
    whole = size_a * size_b
    half_a = size_a // 2

    def pair(r, c, period):
        ri = lax.broadcasted_iota(jnp.int32, (r, c), 0)
        ci = lax.broadcasted_iota(jnp.int32, (r, c), 1)
        ang = (ri * ci % period).astype(jnp.float32) * (2.0 * math.pi / period)
        return jnp.cos(ang), jnp.sin(ang)

    cos_a, sin_a = pair(size_a, half_a, size_a)
    cos_b, sin_b = pair(size_b, size_b, size_b)
    cos_t, sin_t = pair(size_a, size_b, whole)
    inv = jnp.concatenate([cos_a.T, -sin_a.T], axis=1)
    return (*_split(cos_a), *_split(sin_a), *_split(cos_b), *_split(sin_b), cos_t, sin_t, *_split(inv))


def filter_spectrum(filt, tabs, ch_block=2):
    ch, length = filt.shape
    size_b = 128
    half_a = length // size_b
    size_a = 2 * half_a
    h = filt.reshape(ch, half_a, size_b)
    full = lambda t: pl.BlockSpec(t.shape, lambda i: (0,) * t.ndim)
    blk_out = pl.BlockSpec((ch_block, size_a, size_b), lambda i: (i, 0, 0))
    return pl.pallas_call(
        _filter_body,
        grid=(ch // ch_block,),
        in_specs=[pl.BlockSpec((ch_block, half_a, size_b), lambda i: (i, 0, 0))]
        + [full(t) for t in tabs[:10]],
        out_specs=[blk_out, blk_out],
        out_shape=[jax.ShapeDtypeStruct((ch, size_a, size_b), jnp.float32)] * 2,
    )(h, *tabs[:10])


def long_conv(kv, spectrum, gain, tabs, ch_block=2):
    ch, length = kv.shape
    size_b = 128
    half_a = length // size_b
    size_a = 2 * half_a
    x = kv.reshape(ch, half_a, size_b)
    g = jnp.broadcast_to(gain[:, None, None], (ch, 1, size_b))
    full = lambda t: pl.BlockSpec(t.shape, lambda i: (0,) * t.ndim)
    blk_spec = pl.BlockSpec((ch_block, size_a, size_b), lambda i: (i, 0, 0))
    out = pl.pallas_call(
        _conv_body,
        grid=(ch // ch_block,),
        in_specs=[
            pl.BlockSpec((ch_block, half_a, size_b), lambda i: (i, 0, 0)),
            blk_spec,
            blk_spec,
            pl.BlockSpec((ch_block, 1, size_b), lambda i: (i, 0, 0)),
        ] + [full(t) for t in tabs],
        out_specs=pl.BlockSpec((ch_block, half_a, size_b), lambda i: (i, 0, 0)),
        out_shape=jax.ShapeDtypeStruct((ch, half_a, size_b), jnp.bfloat16),
    )(x, *spectrum, g, *tabs)
    return out.reshape(ch, length)


def multiply_round(left_arr, right_arr):
    return (left_arr.astype(jnp.float32) * right_arr.astype(jnp.float32)).astype(jnp.bfloat16)


def local(projected, feat_weight, long_filter, skip_gain, out_values, out_scales):
    groups = lax.axis_size("seq")
    tok_rows = projected.shape[1]
    local_ch = projected.shape[2]
    length = tok_rows * groups
    rim_width = KS - 1
    prior_rows = passed_along(projected[:, tok_rows - rim_width :, :], "seq", 1)
    q_feat, gated_kv = featurize_kv(projected, prior_rows, feat_weight)
    tabs = conv_tables(2 * length // 128, 128)
    spectrum = filter_spectrum(long_filter, tabs)
    kv_cols = jnp.transpose(gated_kv, (1, 0))
    kv_owned = lax.all_to_all(kv_cols, "seq", split_axis=0, concat_axis=1, tiled=True)
    filtered = long_conv(kv_owned, spectrum, skip_gain, tabs)
    filtered_home = lax.all_to_all(filtered, "seq", split_axis=1, concat_axis=0, tiled=True)
    gated = multiply_round(q_feat, jnp.transpose(filtered_home, (1, 0)))
    block_count = local_ch // BLK
    out_width = out_values.shape[1]
    stacked = gated.reshape(tok_rows, block_count, BLK)
    weight_blocks = out_values.reshape(block_count, BLK, out_width)
    scale_cols = jnp.repeat(out_scales, BLK, axis=1)
    products = jnp.einsum(
        "tbk,bkn->btn", stacked, weight_blocks, preferred_element_type=jnp.float32
    )
    partial = jnp.sum(products * scale_cols[:, None, :], axis=0).astype(jnp.bfloat16)
    n_tensor = lax.axis_size("tensor")
    pieces = partial.reshape(tok_rows, n_tensor, out_width // n_tensor).transpose(1, 0, 2)
    gathered = lax.all_to_all(pieces, "tensor", 0, 0, tiled=True)
    return jnp.sum(gathered.astype(jnp.float32), axis=0).astype(jnp.bfloat16)


def solution(mesh):
    return jax.shard_map(
        local,
        mesh=mesh,
        in_specs=(
            P(None, "seq", "tensor"),
            P(None, None, "tensor"),
            P(("tensor", "seq"), None),
            P(("tensor", "seq")),
            P("tensor", None),
            P("tensor", None),
        ),
        out_specs=P("seq", "tensor"),
        check_vma=False,
    )
```

```python
import math

import jax
import jax.numpy as jnp
from jax import lax
from jax.sharding import PartitionSpec as P
from jax.experimental import pallas as pl
from jax.experimental.pallas import tpu as pltpu

KS = 7
BLK = 128


TRIPLE = lax.Precision.HIGH


def passed_along(x, axis, by):
    size = lax.axis_size(axis)
    pairs = [(i, i + by) for i in range(size) if 0 <= i + by < size]
    return lax.ppermute(x, axis, pairs)


def split_length(whole):
    for candidate in range(2, whole + 1, 2):
        if whole % candidate == 0 and candidate * candidate >= whole:
            return (candidate, whole // candidate)
    return (whole, 1)


def angle_pair(row_count, col_count, period):
    row_ids = lax.broadcasted_iota(jnp.int32, (row_count, col_count), 0)
    col_ids = lax.broadcasted_iota(jnp.int32, (row_count, col_count), 1)
    angles = (row_ids * col_ids % period).astype(jnp.float32) * (2.0 * math.pi / period)
    return (jnp.cos(angles), jnp.sin(angles))


def make_tables(length):
    whole = 2 * length
    size_a, size_b = split_length(whole)
    return (
        angle_pair(size_a, size_a, size_a),
        angle_pair(size_b, size_b, size_b),
        angle_pair(size_a, size_b, whole),
        size_a,
        size_b,
    )


def right_mul(signal, matrix):
    return jnp.einsum("ckn,nm->ckm", signal, matrix, precision=TRIPLE)


def forward(signal, tables):
    (cos_a, sin_a), (cos_b, sin_b), (cos_t, sin_t), size_a, size_b = tables
    half_a = size_a // 2
    blocks = signal.reshape(signal.shape[0], half_a, size_b)
    real_a = jnp.einsum("kn,cnb->ckb", cos_a[:, :half_a], blocks, precision=TRIPLE)
    imag_a = -jnp.einsum("kn,cnb->ckb", sin_a[:, :half_a], blocks, precision=TRIPLE)
    real_t = real_a * cos_t + imag_a * sin_t
    imag_t = imag_a * cos_t - real_a * sin_t
    real_f = right_mul(real_t, cos_b) + right_mul(imag_t, sin_b)
    imag_f = right_mul(imag_t, cos_b) - right_mul(real_t, sin_b)
    return (real_f, imag_f)


def inverse(real_f, imag_f, tables):
    (cos_a, sin_a), (cos_b, sin_b), (cos_t, sin_t), size_a, size_b = tables
    half_a = size_a // 2
    real_z = right_mul(real_f, cos_b) - right_mul(imag_f, sin_b)
    imag_z = right_mul(imag_f, cos_b) + right_mul(real_f, sin_b)
    real_w = real_z * cos_t - imag_z * sin_t
    imag_w = imag_z * cos_t + real_z * sin_t
    out_half = jnp.einsum("nk,ckb->cnb", cos_a[:half_a, :], real_w, precision=TRIPLE) - jnp.einsum(
        "nk,ckb->cnb", sin_a[:half_a, :], imag_w, precision=TRIPLE
    )
    return out_half.reshape(out_half.shape[0], half_a * size_b) * (1.0 / (size_a * size_b))


def long_mix(gated_kv, spectrum, own_gain, tables):
    kv_values = gated_kv.astype(jnp.float32)
    real_u, imag_u = forward(kv_values, tables)
    real_h, imag_h = spectrum
    real_p = real_u * real_h - imag_u * imag_h
    imag_p = real_u * imag_h + imag_u * real_h
    convolved = inverse(real_p, imag_p, tables)
    return (convolved + own_gain[:, None] * kv_values).astype(jnp.bfloat16)


def featurize(extended, weights, length):
    tap_count = weights.shape[1]
    running = jnp.zeros(extended.shape[:1] + (length,) + extended.shape[2:], jnp.float32)
    for lag_idx in range(tap_count):
        offset = tap_count - 1 - lag_idx
        running = running + weights[:, lag_idx, None, :] * extended[
            :, offset : offset + length, :
        ].astype(jnp.float32)
    return running.astype(jnp.bfloat16)


def _feat_body(proj_ref, prior_ref, w_ref, q_ref, kv_ref, ext_ref):
    rows = proj_ref.shape[1]
    feats = []
    for a in range(3):
        ext_ref[0:2, :] = jnp.zeros((2, ext_ref.shape[1]), jnp.float32)
        ext_ref[2:8, :] = prior_ref[a].astype(jnp.float32)
        ext_ref[8 : 8 + rows, :] = proj_ref[a].astype(jnp.float32)
        acc = jnp.zeros((rows, ext_ref.shape[1]), jnp.float32)
        for j in range(KS):
            acc = acc + w_ref[a, j : j + 1, :] * ext_ref[8 - j : 8 - j + rows, :]
        feats.append(acc.astype(jnp.bfloat16))
    q_ref[...] = feats[0]
    kv_ref[...] = (feats[1].astype(jnp.float32) * feats[2].astype(jnp.float32)).astype(jnp.bfloat16)

def featurize_kv(projected, prior, weights, lane_block=128, interpret=False):
    _, rows, chans = projected.shape
    grid = (chans // lane_block,)
    return pl.pallas_call(
        _feat_body,
        grid=grid,
        in_specs=[
            pl.BlockSpec((3, rows, lane_block), lambda i: (0, 0, i)),
            pl.BlockSpec((3, KS - 1, lane_block), lambda i: (0, 0, i)),
            pl.BlockSpec((3, KS, lane_block), lambda i: (0, 0, i)),
        ],
        out_specs=[
            pl.BlockSpec((rows, lane_block), lambda i: (0, i)),
            pl.BlockSpec((rows, lane_block), lambda i: (0, i)),
        ],
        out_shape=[jax.ShapeDtypeStruct((rows, chans), jnp.bfloat16)] * 2,
        scratch_shapes=[pltpu.VMEM((rows + 8, lane_block), jnp.float32)],
        interpret=interpret,
    )(projected, prior, weights)


def _split(a):
    hi = a.astype(jnp.bfloat16)
    return hi, (a - hi.astype(jnp.float32)).astype(jnp.bfloat16)


def _mm(a, b):
    return jnp.dot(a, b, preferred_element_type=jnp.float32)


def _left3(t_hi, t_lo, v):
    v_hi, v_lo = _split(v)
    return _mm(t_hi, v_hi) + _mm(t_lo, v_hi) + _mm(t_hi, v_lo)


def _right3(v, t_hi, t_lo):
    v_hi, v_lo = _split(v)
    return _mm(v_hi, t_hi) + _mm(v_lo, t_hi) + _mm(v_hi, t_lo)


def _spectrum(a_re, a_im, ct, st, cb_h, cb_l, sb_h, sb_l):
    rows = ct.shape[0]
    t_re = a_re * ct + a_im * st
    t_im = a_im * ct - a_re * st
    stacked = jnp.concatenate([t_re, t_im], axis=0)
    r_c = _right3(stacked, cb_h, cb_l)
    r_s = _right3(stacked, sb_h, sb_l)
    return r_c[:rows] + r_s[rows:], r_c[rows:] - r_s[:rows]


def _filter_body(h_ref, ca_h, ca_l, sa_h, sa_l, cb_h, cb_l, sb_h, sb_l, ct_ref, st_ref, re_ref, im_ref):
    ct = ct_ref[...]
    st = st_ref[...]
    for c in range(h_ref.shape[0]):
        h = h_ref[c]
        a_re = _left3(ca_h[...], ca_l[...], h)
        a_im = -_left3(sa_h[...], sa_l[...], h)
        re_ref[c], im_ref[c] = _spectrum(a_re, a_im, ct, st, cb_h[...], cb_l[...], sb_h[...], sb_l[...])


def _conv_body(x_ref, fh_re_ref, fh_im_ref, g_ref, ca_h, ca_l, sa_h, sa_l, cb_h, cb_l, sb_h, sb_l,
               ct_ref, st_ref, inv_h, inv_l, o_ref):
    rows = ct_ref.shape[0]
    ct = ct_ref[...]
    st = st_ref[...]
    for c in range(x_ref.shape[0]):
        x_b = x_ref[c]
        a_re = _mm(ca_h[...], x_b) + _mm(ca_l[...], x_b)
        a_im = -(_mm(sa_h[...], x_b) + _mm(sa_l[...], x_b))
        fx_re, fx_im = _spectrum(a_re, a_im, ct, st, cb_h[...], cb_l[...], sb_h[...], sb_l[...])
        fh_re = fh_re_ref[c]
        fh_im = fh_im_ref[c]
        p_re = fx_re * fh_re - fx_im * fh_im
        p_im = fx_re * fh_im + fx_im * fh_re
        stacked = jnp.concatenate([p_re, p_im], axis=0)
        q_c = _right3(stacked, cb_h[...], cb_l[...])
        q_s = _right3(stacked, sb_h[...], sb_l[...])
        z_re = q_c[:rows] - q_s[rows:]
        z_im = q_c[rows:] + q_s[:rows]
        w_re = z_re * ct - z_im * st
        w_im = z_im * ct + z_re * st
        out = _left3(inv_h[...], inv_l[...], jnp.concatenate([w_re, w_im], axis=0))
        x_f = x_b.astype(jnp.float32)
        o_ref[c] = (out * (1.0 / (rows * ct_ref.shape[1])) + g_ref[c] * x_f).astype(jnp.bfloat16)


def conv_tables(size_a, size_b):
    whole = size_a * size_b
    half_a = size_a // 2

    def pair(r, c, period):
        ri = lax.broadcasted_iota(jnp.int32, (r, c), 0)
        ci = lax.broadcasted_iota(jnp.int32, (r, c), 1)
        ang = (ri * ci % period).astype(jnp.float32) * (2.0 * math.pi / period)
        return jnp.cos(ang), jnp.sin(ang)

    cos_a, sin_a = pair(size_a, half_a, size_a)
    cos_b, sin_b = pair(size_b, size_b, size_b)
    cos_t, sin_t = pair(size_a, size_b, whole)
    inv = jnp.concatenate([cos_a.T, -sin_a.T], axis=1)
    return (*_split(cos_a), *_split(sin_a), *_split(cos_b), *_split(sin_b), cos_t, sin_t, *_split(inv))


def filter_spectrum(filt, tabs, ch_block=2, size_b=256):
    ch, length = filt.shape
    half_a = length // size_b
    size_a = 2 * half_a
    h = filt.reshape(ch, half_a, size_b)
    full = lambda t: pl.BlockSpec(t.shape, lambda i: (0,) * t.ndim)
    blk_out = pl.BlockSpec((ch_block, size_a, size_b), lambda i: (i, 0, 0))
    return pl.pallas_call(
        _filter_body,
        grid=(ch // ch_block,),
        in_specs=[pl.BlockSpec((ch_block, half_a, size_b), lambda i: (i, 0, 0))]
        + [full(t) for t in tabs[:10]],
        out_specs=[blk_out, blk_out],
        out_shape=[jax.ShapeDtypeStruct((ch, size_a, size_b), jnp.float32)] * 2,
    )(h, *tabs[:10])


def long_conv(kv, spectrum, gain, tabs, ch_block=2, size_b=256):
    ch, length = kv.shape
    half_a = length // size_b
    size_a = 2 * half_a
    x = kv.reshape(ch, half_a, size_b)
    g = jnp.broadcast_to(gain[:, None, None], (ch, 1, size_b))
    full = lambda t: pl.BlockSpec(t.shape, lambda i: (0,) * t.ndim)
    blk_spec = pl.BlockSpec((ch_block, size_a, size_b), lambda i: (i, 0, 0))
    out = pl.pallas_call(
        _conv_body,
        grid=(ch // ch_block,),
        in_specs=[
            pl.BlockSpec((ch_block, half_a, size_b), lambda i: (i, 0, 0)),
            blk_spec,
            blk_spec,
            pl.BlockSpec((ch_block, 1, size_b), lambda i: (i, 0, 0)),
        ] + [full(t) for t in tabs],
        out_specs=pl.BlockSpec((ch_block, half_a, size_b), lambda i: (i, 0, 0)),
        out_shape=jax.ShapeDtypeStruct((ch, half_a, size_b), jnp.bfloat16),
    )(x, *spectrum, g, *tabs)
    return out.reshape(ch, length)


def multiply_round(left_arr, right_arr):
    return (left_arr.astype(jnp.float32) * right_arr.astype(jnp.float32)).astype(jnp.bfloat16)


def local(projected, feat_weight, long_filter, skip_gain, out_values, out_scales):
    groups = lax.axis_size("seq")
    tok_rows = projected.shape[1]
    local_ch = projected.shape[2]
    length = tok_rows * groups
    rim_width = KS - 1
    prior_rows = passed_along(projected[:, tok_rows - rim_width :, :], "seq", 1)
    q_feat, gated_kv = featurize_kv(projected, prior_rows, feat_weight)
    tabs = conv_tables(2 * length // 256, 256)
    spectrum = filter_spectrum(long_filter, tabs)
    kv_cols = jnp.transpose(gated_kv, (1, 0))
    kv_owned = lax.all_to_all(kv_cols, "seq", split_axis=0, concat_axis=1, tiled=True)
    filtered = long_conv(kv_owned, spectrum, skip_gain, tabs)
    filtered_home = lax.all_to_all(filtered, "seq", split_axis=1, concat_axis=0, tiled=True)
    gated = multiply_round(q_feat, jnp.transpose(filtered_home, (1, 0)))
    block_count = local_ch // BLK
    out_width = out_values.shape[1]
    stacked = gated.reshape(tok_rows, block_count, BLK)
    weight_blocks = out_values.reshape(block_count, BLK, out_width)
    scale_cols = jnp.repeat(out_scales, BLK, axis=1)
    products = jnp.einsum(
        "tbk,bkn->btn", stacked, weight_blocks, preferred_element_type=jnp.float32
    )
    partial = jnp.sum(products * scale_cols[:, None, :], axis=0).astype(jnp.bfloat16)
    n_tensor = lax.axis_size("tensor")
    pieces = partial.reshape(tok_rows, n_tensor, out_width // n_tensor).transpose(1, 0, 2)
    gathered = lax.all_to_all(pieces, "tensor", 0, 0, tiled=True)
    return jnp.sum(gathered.astype(jnp.float32), axis=0).astype(jnp.bfloat16)


def solution(mesh):
    return jax.shard_map(
        local,
        mesh=mesh,
        in_specs=(
            P(None, "seq", "tensor"),
            P(None, None, "tensor"),
            P(("tensor", "seq"), None),
            P(("tensor", "seq")),
            P("tensor", None),
            P("tensor", None),
        ),
        out_specs=P("seq", "tensor"),
        check_vma=False,
    )
```

```python
import math

import jax
import jax.numpy as jnp
from jax import lax
from jax.sharding import PartitionSpec as P
from jax.experimental import pallas as pl
from jax.experimental.pallas import tpu as pltpu

KS = 7
BLK = 128


TRIPLE = lax.Precision.HIGH


def passed_along(x, axis, by):
    size = lax.axis_size(axis)
    pairs = [(i, i + by) for i in range(size) if 0 <= i + by < size]
    return lax.ppermute(x, axis, pairs)


def split_length(whole):
    for candidate in range(2, whole + 1, 2):
        if whole % candidate == 0 and candidate * candidate >= whole:
            return (candidate, whole // candidate)
    return (whole, 1)


def angle_pair(row_count, col_count, period):
    row_ids = lax.broadcasted_iota(jnp.int32, (row_count, col_count), 0)
    col_ids = lax.broadcasted_iota(jnp.int32, (row_count, col_count), 1)
    angles = (row_ids * col_ids % period).astype(jnp.float32) * (2.0 * math.pi / period)
    return (jnp.cos(angles), jnp.sin(angles))


def make_tables(length):
    whole = 2 * length
    size_a, size_b = split_length(whole)
    return (
        angle_pair(size_a, size_a, size_a),
        angle_pair(size_b, size_b, size_b),
        angle_pair(size_a, size_b, whole),
        size_a,
        size_b,
    )


def right_mul(signal, matrix):
    return jnp.einsum("ckn,nm->ckm", signal, matrix, precision=TRIPLE)


def forward(signal, tables):
    (cos_a, sin_a), (cos_b, sin_b), (cos_t, sin_t), size_a, size_b = tables
    half_a = size_a // 2
    blocks = signal.reshape(signal.shape[0], half_a, size_b)
    real_a = jnp.einsum("kn,cnb->ckb", cos_a[:, :half_a], blocks, precision=TRIPLE)
    imag_a = -jnp.einsum("kn,cnb->ckb", sin_a[:, :half_a], blocks, precision=TRIPLE)
    real_t = real_a * cos_t + imag_a * sin_t
    imag_t = imag_a * cos_t - real_a * sin_t
    real_f = right_mul(real_t, cos_b) + right_mul(imag_t, sin_b)
    imag_f = right_mul(imag_t, cos_b) - right_mul(real_t, sin_b)
    return (real_f, imag_f)


def inverse(real_f, imag_f, tables):
    (cos_a, sin_a), (cos_b, sin_b), (cos_t, sin_t), size_a, size_b = tables
    half_a = size_a // 2
    real_z = right_mul(real_f, cos_b) - right_mul(imag_f, sin_b)
    imag_z = right_mul(imag_f, cos_b) + right_mul(real_f, sin_b)
    real_w = real_z * cos_t - imag_z * sin_t
    imag_w = imag_z * cos_t + real_z * sin_t
    out_half = jnp.einsum("nk,ckb->cnb", cos_a[:half_a, :], real_w, precision=TRIPLE) - jnp.einsum(
        "nk,ckb->cnb", sin_a[:half_a, :], imag_w, precision=TRIPLE
    )
    return out_half.reshape(out_half.shape[0], half_a * size_b) * (1.0 / (size_a * size_b))


def long_mix(gated_kv, spectrum, own_gain, tables):
    kv_values = gated_kv.astype(jnp.float32)
    real_u, imag_u = forward(kv_values, tables)
    real_h, imag_h = spectrum
    real_p = real_u * real_h - imag_u * imag_h
    imag_p = real_u * imag_h + imag_u * real_h
    convolved = inverse(real_p, imag_p, tables)
    return (convolved + own_gain[:, None] * kv_values).astype(jnp.bfloat16)


def featurize(extended, weights, length):
    tap_count = weights.shape[1]
    running = jnp.zeros(extended.shape[:1] + (length,) + extended.shape[2:], jnp.float32)
    for lag_idx in range(tap_count):
        offset = tap_count - 1 - lag_idx
        running = running + weights[:, lag_idx, None, :] * extended[
            :, offset : offset + length, :
        ].astype(jnp.float32)
    return running.astype(jnp.bfloat16)


def _feat_body(proj_ref, prior_ref, w_ref, q_ref, kv_ref, ext_ref):
    rows = proj_ref.shape[1]
    feats = []
    for a in range(3):
        ext_ref[0:2, :] = jnp.zeros((2, ext_ref.shape[1]), jnp.float32)
        ext_ref[2:8, :] = prior_ref[a].astype(jnp.float32)
        ext_ref[8 : 8 + rows, :] = proj_ref[a].astype(jnp.float32)
        acc = jnp.zeros((rows, ext_ref.shape[1]), jnp.float32)
        for j in range(KS):
            acc = acc + w_ref[a, j : j + 1, :] * ext_ref[8 - j : 8 - j + rows, :]
        feats.append(acc.astype(jnp.bfloat16))
    q_ref[...] = feats[0].astype(jnp.float32).T.astype(jnp.bfloat16)
    kv = feats[1].astype(jnp.float32) * feats[2].astype(jnp.float32)
    kv_ref[...] = kv.astype(jnp.bfloat16).astype(jnp.float32).T.astype(jnp.bfloat16)

def featurize_kv(projected, prior, weights, lane_block=128, interpret=False):
    _, rows, chans = projected.shape
    grid = (chans // lane_block,)
    return pl.pallas_call(
        _feat_body,
        grid=grid,
        in_specs=[
            pl.BlockSpec((3, rows, lane_block), lambda i: (0, 0, i)),
            pl.BlockSpec((3, KS - 1, lane_block), lambda i: (0, 0, i)),
            pl.BlockSpec((3, KS, lane_block), lambda i: (0, 0, i)),
        ],
        out_specs=[
            pl.BlockSpec((lane_block, rows), lambda i: (i, 0)),
            pl.BlockSpec((lane_block, rows), lambda i: (i, 0)),
        ],
        out_shape=[jax.ShapeDtypeStruct((chans, rows), jnp.bfloat16)] * 2,
        scratch_shapes=[pltpu.VMEM((rows + 8, lane_block), jnp.float32)],
        interpret=interpret,
    )(projected, prior, weights)


def _split(a):
    hi = a.astype(jnp.bfloat16)
    return hi, (a - hi.astype(jnp.float32)).astype(jnp.bfloat16)


def _mm(a, b):
    return jnp.dot(a, b, preferred_element_type=jnp.float32)


def _left3(t_hi, t_lo, v):
    v_hi, v_lo = _split(v)
    return _mm(t_hi, v_hi) + _mm(t_lo, v_hi) + _mm(t_hi, v_lo)


def _right3(v, t_hi, t_lo):
    v_hi, v_lo = _split(v)
    return _mm(v_hi, t_hi) + _mm(v_lo, t_hi) + _mm(v_hi, t_lo)


def _spectrum(a_re, a_im, ct, st, cb_h, cb_l, sb_h, sb_l):
    rows = ct.shape[0]
    t_re = a_re * ct + a_im * st
    t_im = a_im * ct - a_re * st
    stacked = jnp.concatenate([t_re, t_im], axis=0)
    r_c = _right3(stacked, cb_h, cb_l)
    r_s = _right3(stacked, sb_h, sb_l)
    return r_c[:rows] + r_s[rows:], r_c[rows:] - r_s[:rows]


def _filter_body(h_ref, ca_h, ca_l, sa_h, sa_l, cb_h, cb_l, sb_h, sb_l, ct_ref, st_ref, re_ref, im_ref):
    ct = ct_ref[...]
    st = st_ref[...]
    for c in range(h_ref.shape[0]):
        h = h_ref[c]
        a_re = _left3(ca_h[...], ca_l[...], h)
        a_im = -_left3(sa_h[...], sa_l[...], h)
        re_ref[c], im_ref[c] = _spectrum(a_re, a_im, ct, st, cb_h[...], cb_l[...], sb_h[...], sb_l[...])


def _conv_body(x_ref, fh_re_ref, fh_im_ref, g_ref, ca_h, ca_l, sa_h, sa_l, cb_h, cb_l, sb_h, sb_l,
               ct_ref, st_ref, inv_h, inv_l, o_ref):
    rows = ct_ref.shape[0]
    ct = ct_ref[...]
    st = st_ref[...]
    for c in range(x_ref.shape[0]):
        x_b = x_ref[c]
        a_re = _mm(ca_h[...], x_b) + _mm(ca_l[...], x_b)
        a_im = -(_mm(sa_h[...], x_b) + _mm(sa_l[...], x_b))
        fx_re, fx_im = _spectrum(a_re, a_im, ct, st, cb_h[...], cb_l[...], sb_h[...], sb_l[...])
        fh_re = fh_re_ref[c]
        fh_im = fh_im_ref[c]
        p_re = fx_re * fh_re - fx_im * fh_im
        p_im = fx_re * fh_im + fx_im * fh_re
        stacked = jnp.concatenate([p_re, p_im], axis=0)
        q_c = _right3(stacked, cb_h[...], cb_l[...])
        q_s = _right3(stacked, sb_h[...], sb_l[...])
        z_re = q_c[:rows] - q_s[rows:]
        z_im = q_c[rows:] + q_s[:rows]
        w_re = z_re * ct - z_im * st
        w_im = z_im * ct + z_re * st
        out = _left3(inv_h[...], inv_l[...], jnp.concatenate([w_re, w_im], axis=0))
        x_f = x_b.astype(jnp.float32)
        o_ref[c] = (out * (1.0 / (rows * ct_ref.shape[1])) + g_ref[c] * x_f).astype(jnp.bfloat16)


def conv_tables(size_a, size_b):
    whole = size_a * size_b
    half_a = size_a // 2

    def pair(r, c, period):
        ri = lax.broadcasted_iota(jnp.int32, (r, c), 0)
        ci = lax.broadcasted_iota(jnp.int32, (r, c), 1)
        ang = (ri * ci % period).astype(jnp.float32) * (2.0 * math.pi / period)
        return jnp.cos(ang), jnp.sin(ang)

    cos_a, sin_a = pair(size_a, half_a, size_a)
    cos_b, sin_b = pair(size_b, size_b, size_b)
    cos_t, sin_t = pair(size_a, size_b, whole)
    inv = jnp.concatenate([cos_a.T, -sin_a.T], axis=1)
    return (*_split(cos_a), *_split(sin_a), *_split(cos_b), *_split(sin_b), cos_t, sin_t, *_split(inv))


def filter_spectrum(filt, tabs, ch_block=2, size_b=256):
    ch, length = filt.shape
    half_a = length // size_b
    size_a = 2 * half_a
    h = filt.reshape(ch, half_a, size_b)
    full = lambda t: pl.BlockSpec(t.shape, lambda i: (0,) * t.ndim)
    blk_out = pl.BlockSpec((ch_block, size_a, size_b), lambda i: (i, 0, 0))
    return pl.pallas_call(
        _filter_body,
        grid=(ch // ch_block,),
        in_specs=[pl.BlockSpec((ch_block, half_a, size_b), lambda i: (i, 0, 0))]
        + [full(t) for t in tabs[:10]],
        out_specs=[blk_out, blk_out],
        out_shape=[jax.ShapeDtypeStruct((ch, size_a, size_b), jnp.float32)] * 2,
    )(h, *tabs[:10])


def long_conv(kv, spectrum, gain, tabs, ch_block=2, size_b=256):
    ch, length = kv.shape
    half_a = length // size_b
    size_a = 2 * half_a
    x = kv.reshape(ch, half_a, size_b)
    g = jnp.broadcast_to(gain[:, None, None], (ch, 1, size_b))
    full = lambda t: pl.BlockSpec(t.shape, lambda i: (0,) * t.ndim)
    blk_spec = pl.BlockSpec((ch_block, size_a, size_b), lambda i: (i, 0, 0))
    out = pl.pallas_call(
        _conv_body,
        grid=(ch // ch_block,),
        in_specs=[
            pl.BlockSpec((ch_block, half_a, size_b), lambda i: (i, 0, 0)),
            blk_spec,
            blk_spec,
            pl.BlockSpec((ch_block, 1, size_b), lambda i: (i, 0, 0)),
        ] + [full(t) for t in tabs],
        out_specs=pl.BlockSpec((ch_block, half_a, size_b), lambda i: (i, 0, 0)),
        out_shape=jax.ShapeDtypeStruct((ch, half_a, size_b), jnp.bfloat16),
    )(x, *spectrum, g, *tabs)
    return out.reshape(ch, length)


def _proj_body(f_ref, q_ref, w_ref, s_ref, o_ref):
    gated = (q_ref[...].astype(jnp.float32) * f_ref[...].astype(jnp.float32)).astype(jnp.bfloat16)
    rows_major = gated.astype(jnp.float32).T.astype(jnp.bfloat16)
    acc = None
    for b in range(w_ref.shape[0] // BLK):
        part = jnp.dot(rows_major[:, b * BLK : (b + 1) * BLK], w_ref[b * BLK : (b + 1) * BLK, :],
                       preferred_element_type=jnp.float32) * s_ref[b : b + 1, :]
        acc = part if acc is None else acc + part
    o_ref[0] = acc.astype(jnp.bfloat16)


def project(filtered_home, q_cols, out_values, scale_cols, n_pieces):
    chans, rows = filtered_home.shape
    width = out_values.shape[1] // n_pieces
    return pl.pallas_call(
        _proj_body,
        grid=(n_pieces,),
        in_specs=[
            pl.BlockSpec((chans, rows), lambda j: (0, 0)),
            pl.BlockSpec((chans, rows), lambda j: (0, 0)),
            pl.BlockSpec((chans, width), lambda j: (0, j)),
            pl.BlockSpec((scale_cols.shape[0], width), lambda j: (0, j)),
        ],
        out_specs=pl.BlockSpec((1, rows, width), lambda j: (j, 0, 0)),
        out_shape=jax.ShapeDtypeStruct((n_pieces, rows, width), jnp.bfloat16),
    )(filtered_home, q_cols, out_values, scale_cols)


def multiply_round(left_arr, right_arr):
    return (left_arr.astype(jnp.float32) * right_arr.astype(jnp.float32)).astype(jnp.bfloat16)


def local(projected, feat_weight, long_filter, skip_gain, out_values, out_scales):
    groups = lax.axis_size("seq")
    tok_rows = projected.shape[1]
    local_ch = projected.shape[2]
    length = tok_rows * groups
    rim_width = KS - 1
    prior_rows = passed_along(projected[:, tok_rows - rim_width :, :], "seq", 1)
    q_feat, gated_kv = featurize_kv(projected, prior_rows, feat_weight)
    tabs = conv_tables(2 * length // 256, 256)
    spectrum = filter_spectrum(long_filter, tabs)
    kv_owned = lax.all_to_all(gated_kv, "seq", split_axis=0, concat_axis=1, tiled=True)
    filtered = long_conv(kv_owned, spectrum, skip_gain, tabs)
    filtered_home = lax.all_to_all(filtered, "seq", split_axis=1, concat_axis=0, tiled=True)
    n_tensor = lax.axis_size("tensor")
    scale_cols = jnp.repeat(out_scales, BLK, axis=1)
    pieces = project(filtered_home, q_feat, out_values, scale_cols, n_tensor)
    gathered = lax.all_to_all(pieces, "tensor", 0, 0, tiled=True)
    return jnp.sum(gathered.astype(jnp.float32), axis=0).astype(jnp.bfloat16)


def solution(mesh):
    return jax.shard_map(
        local,
        mesh=mesh,
        in_specs=(
            P(None, "seq", "tensor"),
            P(None, None, "tensor"),
            P(("tensor", "seq"), None),
            P(("tensor", "seq")),
            P("tensor", None),
            P("tensor", None),
        ),
        out_specs=P("seq", "tensor"),
        check_vma=False,
    )
```

```python
import math

import jax
import jax.numpy as jnp
from jax import lax
from jax.sharding import PartitionSpec as P
from jax.experimental import pallas as pl
from jax.experimental.pallas import tpu as pltpu

KS = 7
BLK = 128


TRIPLE = lax.Precision.HIGH


def passed_along(x, axis, by):
    size = lax.axis_size(axis)
    pairs = [(i, i + by) for i in range(size) if 0 <= i + by < size]
    return lax.ppermute(x, axis, pairs)


def split_length(whole):
    for candidate in range(2, whole + 1, 2):
        if whole % candidate == 0 and candidate * candidate >= whole:
            return (candidate, whole // candidate)
    return (whole, 1)


def angle_pair(row_count, col_count, period):
    row_ids = lax.broadcasted_iota(jnp.int32, (row_count, col_count), 0)
    col_ids = lax.broadcasted_iota(jnp.int32, (row_count, col_count), 1)
    angles = (row_ids * col_ids % period).astype(jnp.float32) * (2.0 * math.pi / period)
    return (jnp.cos(angles), jnp.sin(angles))


def make_tables(length):
    whole = 2 * length
    size_a, size_b = split_length(whole)
    return (
        angle_pair(size_a, size_a, size_a),
        angle_pair(size_b, size_b, size_b),
        angle_pair(size_a, size_b, whole),
        size_a,
        size_b,
    )


def right_mul(signal, matrix):
    return jnp.einsum("ckn,nm->ckm", signal, matrix, precision=TRIPLE)


def forward(signal, tables):
    (cos_a, sin_a), (cos_b, sin_b), (cos_t, sin_t), size_a, size_b = tables
    half_a = size_a // 2
    blocks = signal.reshape(signal.shape[0], half_a, size_b)
    real_a = jnp.einsum("kn,cnb->ckb", cos_a[:, :half_a], blocks, precision=TRIPLE)
    imag_a = -jnp.einsum("kn,cnb->ckb", sin_a[:, :half_a], blocks, precision=TRIPLE)
    real_t = real_a * cos_t + imag_a * sin_t
    imag_t = imag_a * cos_t - real_a * sin_t
    real_f = right_mul(real_t, cos_b) + right_mul(imag_t, sin_b)
    imag_f = right_mul(imag_t, cos_b) - right_mul(real_t, sin_b)
    return (real_f, imag_f)


def inverse(real_f, imag_f, tables):
    (cos_a, sin_a), (cos_b, sin_b), (cos_t, sin_t), size_a, size_b = tables
    half_a = size_a // 2
    real_z = right_mul(real_f, cos_b) - right_mul(imag_f, sin_b)
    imag_z = right_mul(imag_f, cos_b) + right_mul(real_f, sin_b)
    real_w = real_z * cos_t - imag_z * sin_t
    imag_w = imag_z * cos_t + real_z * sin_t
    out_half = jnp.einsum("nk,ckb->cnb", cos_a[:half_a, :], real_w, precision=TRIPLE) - jnp.einsum(
        "nk,ckb->cnb", sin_a[:half_a, :], imag_w, precision=TRIPLE
    )
    return out_half.reshape(out_half.shape[0], half_a * size_b) * (1.0 / (size_a * size_b))


def long_mix(gated_kv, spectrum, own_gain, tables):
    kv_values = gated_kv.astype(jnp.float32)
    real_u, imag_u = forward(kv_values, tables)
    real_h, imag_h = spectrum
    real_p = real_u * real_h - imag_u * imag_h
    imag_p = real_u * imag_h + imag_u * real_h
    convolved = inverse(real_p, imag_p, tables)
    return (convolved + own_gain[:, None] * kv_values).astype(jnp.bfloat16)


def featurize(extended, weights, length):
    tap_count = weights.shape[1]
    running = jnp.zeros(extended.shape[:1] + (length,) + extended.shape[2:], jnp.float32)
    for lag_idx in range(tap_count):
        offset = tap_count - 1 - lag_idx
        running = running + weights[:, lag_idx, None, :] * extended[
            :, offset : offset + length, :
        ].astype(jnp.float32)
    return running.astype(jnp.bfloat16)


def _feat_body(proj_ref, prior_ref, w_ref, q_ref, kv_ref, ext_ref):
    rows = proj_ref.shape[1]
    feats = []
    for a in range(3):
        ext_ref[0:2, :] = jnp.zeros((2, ext_ref.shape[1]), jnp.float32)
        ext_ref[2:8, :] = prior_ref[a].astype(jnp.float32)
        ext_ref[8 : 8 + rows, :] = proj_ref[a].astype(jnp.float32)
        acc = jnp.zeros((rows, ext_ref.shape[1]), jnp.float32)
        for j in range(KS):
            acc = acc + w_ref[a, j : j + 1, :] * ext_ref[8 - j : 8 - j + rows, :]
        feats.append(acc.astype(jnp.bfloat16))
    q_ref[...] = feats[0].astype(jnp.float32).T.astype(jnp.bfloat16)
    kv = feats[1].astype(jnp.float32) * feats[2].astype(jnp.float32)
    kv_ref[...] = kv.astype(jnp.bfloat16).astype(jnp.float32).T.astype(jnp.bfloat16)

def featurize_kv(projected, prior, weights, lane_block=128, interpret=False):
    _, rows, chans = projected.shape
    grid = (chans // lane_block,)
    return pl.pallas_call(
        _feat_body,
        grid=grid,
        in_specs=[
            pl.BlockSpec((3, rows, lane_block), lambda i: (0, 0, i)),
            pl.BlockSpec((3, KS - 1, lane_block), lambda i: (0, 0, i)),
            pl.BlockSpec((3, KS, lane_block), lambda i: (0, 0, i)),
        ],
        out_specs=[
            pl.BlockSpec((lane_block, rows), lambda i: (i, 0)),
            pl.BlockSpec((lane_block, rows), lambda i: (i, 0)),
        ],
        out_shape=[jax.ShapeDtypeStruct((chans, rows), jnp.bfloat16)] * 2,
        scratch_shapes=[pltpu.VMEM((rows + 8, lane_block), jnp.float32)],
        interpret=interpret,
    )(projected, prior, weights)


def _split(a):
    hi = a.astype(jnp.bfloat16)
    return hi, (a - hi.astype(jnp.float32)).astype(jnp.bfloat16)


def _mm(a, b):
    return jnp.dot(a, b, preferred_element_type=jnp.float32)


def _left3(t_hi, t_lo, v):
    v_hi, v_lo = _split(v)
    return _mm(t_hi, v_hi) + _mm(t_lo, v_hi) + _mm(t_hi, v_lo)


def _right3(v, t_hi, t_lo):
    v_hi, v_lo = _split(v)
    return _mm(v_hi, t_hi) + _mm(v_lo, t_hi) + _mm(v_hi, t_lo)


def _spectrum(a_re, a_im, ct, st, cb_h, cb_l, sb_h, sb_l):
    rows = ct.shape[0]
    t_re = a_re * ct + a_im * st
    t_im = a_im * ct - a_re * st
    stacked = jnp.concatenate([t_re, t_im], axis=0)
    r_c = _right3(stacked, cb_h, cb_l)
    r_s = _right3(stacked, sb_h, sb_l)
    return r_c[:rows] + r_s[rows:], r_c[rows:] - r_s[:rows]


def _filter_body(h_ref, ca_h, ca_l, sa_h, sa_l, cb_h, cb_l, sb_h, sb_l, ct_ref, st_ref, re_ref, im_ref):
    ct = ct_ref[...]
    st = st_ref[...]
    for c in range(h_ref.shape[0]):
        h = h_ref[c]
        a_re = _left3(ca_h[...], ca_l[...], h)
        a_im = -_left3(sa_h[...], sa_l[...], h)
        re_ref[c], im_ref[c] = _spectrum(a_re, a_im, ct, st, cb_h[...], cb_l[...], sb_h[...], sb_l[...])


def _conv_body(x_ref, fh_re_ref, fh_im_ref, g_ref, ca_h, ca_l, sa_h, sa_l, cb_h, cb_l, sb_h, sb_l,
               ct_ref, st_ref, inv_h, inv_l, o_ref):
    rows = ct_ref.shape[0]
    ct = ct_ref[...]
    st = st_ref[...]
    for c in range(x_ref.shape[0]):
        x_b = x_ref[c]
        a_re = _mm(ca_h[...], x_b) + _mm(ca_l[...], x_b)
        a_im = -(_mm(sa_h[...], x_b) + _mm(sa_l[...], x_b))
        fx_re, fx_im = _spectrum(a_re, a_im, ct, st, cb_h[...], cb_l[...], sb_h[...], sb_l[...])
        fh_re = fh_re_ref[c]
        fh_im = fh_im_ref[c]
        p_re = fx_re * fh_re - fx_im * fh_im
        p_im = fx_re * fh_im + fx_im * fh_re
        stacked = jnp.concatenate([p_re, p_im], axis=0)
        q_c = _right3(stacked, cb_h[...], cb_l[...])
        q_s = _right3(stacked, sb_h[...], sb_l[...])
        z_re = q_c[:rows] - q_s[rows:]
        z_im = q_c[rows:] + q_s[:rows]
        w_re = z_re * ct - z_im * st
        w_im = z_im * ct + z_re * st
        out = _left3(inv_h[...], inv_l[...], jnp.concatenate([w_re, w_im], axis=0))
        x_f = x_b.astype(jnp.float32)
        o_ref[c] = (out * (1.0 / (rows * ct_ref.shape[1])) + g_ref[c] * x_f).astype(jnp.bfloat16)


def conv_tables(size_a, size_b):
    whole = size_a * size_b
    half_a = size_a // 2

    def pair(r, c, period):
        ri = lax.broadcasted_iota(jnp.int32, (r, c), 0)
        ci = lax.broadcasted_iota(jnp.int32, (r, c), 1)
        ang = (ri * ci % period).astype(jnp.float32) * (2.0 * math.pi / period)
        return jnp.cos(ang), jnp.sin(ang)

    cos_a, sin_a = pair(size_a, half_a, size_a)
    cos_b, sin_b = pair(size_b, size_b, size_b)
    cos_t, sin_t = pair(size_a, size_b, whole)
    inv = jnp.concatenate([cos_a.T, -sin_a.T], axis=1)
    return (*_split(cos_a), *_split(sin_a), *_split(cos_b), *_split(sin_b), cos_t, sin_t, *_split(inv))


def filter_spectrum(filt, tabs, ch_block=2, size_b=256):
    ch, length = filt.shape
    half_a = length // size_b
    size_a = 2 * half_a
    h = filt.reshape(ch, half_a, size_b)
    full = lambda t: pl.BlockSpec(t.shape, lambda i: (0,) * t.ndim)
    blk_out = pl.BlockSpec((ch_block, size_a, size_b), lambda i: (i, 0, 0))
    return pl.pallas_call(
        _filter_body,
        grid=(ch // ch_block,),
        in_specs=[pl.BlockSpec((ch_block, half_a, size_b), lambda i: (i, 0, 0))]
        + [full(t) for t in tabs[:10]],
        out_specs=[blk_out, blk_out],
        out_shape=[jax.ShapeDtypeStruct((ch, size_a, size_b), jnp.float32)] * 2,
    )(h, *tabs[:10])


def long_conv(kv, spectrum, gain, tabs, ch_block=2, size_b=256):
    ch, length = kv.shape
    half_a = length // size_b
    size_a = 2 * half_a
    x = kv.reshape(ch, half_a, size_b)
    g = jnp.broadcast_to(gain[:, None, None], (ch, 1, size_b))
    full = lambda t: pl.BlockSpec(t.shape, lambda i: (0,) * t.ndim)
    blk_spec = pl.BlockSpec((ch_block, size_a, size_b), lambda i: (i, 0, 0))
    out = pl.pallas_call(
        _conv_body,
        grid=(ch // ch_block,),
        in_specs=[
            pl.BlockSpec((ch_block, half_a, size_b), lambda i: (i, 0, 0)),
            blk_spec,
            blk_spec,
            pl.BlockSpec((ch_block, 1, size_b), lambda i: (i, 0, 0)),
        ] + [full(t) for t in tabs],
        out_specs=pl.BlockSpec((ch_block, half_a, size_b), lambda i: (i, 0, 0)),
        out_shape=jax.ShapeDtypeStruct((ch, half_a, size_b), jnp.bfloat16),
    )(x, *spectrum, g, *tabs)
    return out.reshape(ch, length)


def _proj_body(f_ref, q_ref, w_ref, s_ref, o_ref, g_scr):
    @pl.when(pl.program_id(0) == 0)
    def _():
        gated = (q_ref[...].astype(jnp.float32) * f_ref[...].astype(jnp.float32)).astype(jnp.bfloat16)
        g_scr[...] = gated.astype(jnp.float32).T.astype(jnp.bfloat16)

    width = o_ref.shape[2]
    for p in range(o_ref.shape[0]):
        acc = None
        for b in range(w_ref.shape[0] // BLK):
            part = jnp.dot(g_scr[:, b * BLK : (b + 1) * BLK],
                           w_ref[b * BLK : (b + 1) * BLK, p * width : (p + 1) * width],
                           preferred_element_type=jnp.float32) * s_ref[b : b + 1, p * width : (p + 1) * width]
            acc = part if acc is None else acc + part
        o_ref[p] = acc.astype(jnp.bfloat16)


def project(filtered_home, q_cols, out_values, scale_cols, n_pieces, steps=2):
    chans, rows = filtered_home.shape
    width = out_values.shape[1] // n_pieces
    per_step = n_pieces // steps
    return pl.pallas_call(
        _proj_body,
        grid=(steps,),
        in_specs=[
            pl.BlockSpec((chans, rows), lambda j: (0, 0)),
            pl.BlockSpec((chans, rows), lambda j: (0, 0)),
            pl.BlockSpec((chans, width * per_step), lambda j: (0, j)),
            pl.BlockSpec((scale_cols.shape[0], width * per_step), lambda j: (0, j)),
        ],
        out_specs=pl.BlockSpec((per_step, rows, width), lambda j: (j, 0, 0)),
        out_shape=jax.ShapeDtypeStruct((n_pieces, rows, width), jnp.bfloat16),
        scratch_shapes=[pltpu.VMEM((rows, chans), jnp.bfloat16)],
    )(filtered_home, q_cols, out_values, scale_cols)


def multiply_round(left_arr, right_arr):
    return (left_arr.astype(jnp.float32) * right_arr.astype(jnp.float32)).astype(jnp.bfloat16)


def local(projected, feat_weight, long_filter, skip_gain, out_values, out_scales):
    groups = lax.axis_size("seq")
    tok_rows = projected.shape[1]
    local_ch = projected.shape[2]
    length = tok_rows * groups
    rim_width = KS - 1
    prior_rows = passed_along(projected[:, tok_rows - rim_width :, :], "seq", 1)
    q_feat, gated_kv = featurize_kv(projected, prior_rows, feat_weight)
    tabs = conv_tables(2 * length // 256, 256)
    spectrum = filter_spectrum(long_filter, tabs)
    kv_owned = lax.all_to_all(gated_kv, "seq", split_axis=0, concat_axis=1, tiled=True)
    filtered = long_conv(kv_owned, spectrum, skip_gain, tabs)
    filtered_home = lax.all_to_all(filtered, "seq", split_axis=1, concat_axis=0, tiled=True)
    n_tensor = lax.axis_size("tensor")
    scale_cols = jnp.repeat(out_scales, BLK, axis=1)
    pieces = project(filtered_home, q_feat, out_values, scale_cols, n_tensor)
    gathered = lax.all_to_all(pieces, "tensor", 0, 0, tiled=True)
    return jnp.sum(gathered.astype(jnp.float32), axis=0).astype(jnp.bfloat16)


def solution(mesh):
    return jax.shard_map(
        local,
        mesh=mesh,
        in_specs=(
            P(None, "seq", "tensor"),
            P(None, None, "tensor"),
            P(("tensor", "seq"), None),
            P(("tensor", "seq")),
            P("tensor", None),
            P("tensor", None),
        ),
        out_specs=P("seq", "tensor"),
        check_vma=False,
    )
```

```python
import math

import jax
import jax.numpy as jnp
from jax import lax
from jax.sharding import PartitionSpec as P
from jax.experimental import pallas as pl
from jax.experimental.pallas import tpu as pltpu

KS = 7
BLK = 128


TRIPLE = lax.Precision.HIGH


def passed_along(x, axis, by):
    size = lax.axis_size(axis)
    pairs = [(i, i + by) for i in range(size) if 0 <= i + by < size]
    return lax.ppermute(x, axis, pairs)


def split_length(whole):
    for candidate in range(2, whole + 1, 2):
        if whole % candidate == 0 and candidate * candidate >= whole:
            return (candidate, whole // candidate)
    return (whole, 1)


def angle_pair(row_count, col_count, period):
    row_ids = lax.broadcasted_iota(jnp.int32, (row_count, col_count), 0)
    col_ids = lax.broadcasted_iota(jnp.int32, (row_count, col_count), 1)
    angles = (row_ids * col_ids % period).astype(jnp.float32) * (2.0 * math.pi / period)
    return (jnp.cos(angles), jnp.sin(angles))


def make_tables(length):
    whole = 2 * length
    size_a, size_b = split_length(whole)
    return (
        angle_pair(size_a, size_a, size_a),
        angle_pair(size_b, size_b, size_b),
        angle_pair(size_a, size_b, whole),
        size_a,
        size_b,
    )


def right_mul(signal, matrix):
    return jnp.einsum("ckn,nm->ckm", signal, matrix, precision=TRIPLE)


def forward(signal, tables):
    (cos_a, sin_a), (cos_b, sin_b), (cos_t, sin_t), size_a, size_b = tables
    half_a = size_a // 2
    blocks = signal.reshape(signal.shape[0], half_a, size_b)
    real_a = jnp.einsum("kn,cnb->ckb", cos_a[:, :half_a], blocks, precision=TRIPLE)
    imag_a = -jnp.einsum("kn,cnb->ckb", sin_a[:, :half_a], blocks, precision=TRIPLE)
    real_t = real_a * cos_t + imag_a * sin_t
    imag_t = imag_a * cos_t - real_a * sin_t
    real_f = right_mul(real_t, cos_b) + right_mul(imag_t, sin_b)
    imag_f = right_mul(imag_t, cos_b) - right_mul(real_t, sin_b)
    return (real_f, imag_f)


def inverse(real_f, imag_f, tables):
    (cos_a, sin_a), (cos_b, sin_b), (cos_t, sin_t), size_a, size_b = tables
    half_a = size_a // 2
    real_z = right_mul(real_f, cos_b) - right_mul(imag_f, sin_b)
    imag_z = right_mul(imag_f, cos_b) + right_mul(real_f, sin_b)
    real_w = real_z * cos_t - imag_z * sin_t
    imag_w = imag_z * cos_t + real_z * sin_t
    out_half = jnp.einsum("nk,ckb->cnb", cos_a[:half_a, :], real_w, precision=TRIPLE) - jnp.einsum(
        "nk,ckb->cnb", sin_a[:half_a, :], imag_w, precision=TRIPLE
    )
    return out_half.reshape(out_half.shape[0], half_a * size_b) * (1.0 / (size_a * size_b))


def long_mix(gated_kv, spectrum, own_gain, tables):
    kv_values = gated_kv.astype(jnp.float32)
    real_u, imag_u = forward(kv_values, tables)
    real_h, imag_h = spectrum
    real_p = real_u * real_h - imag_u * imag_h
    imag_p = real_u * imag_h + imag_u * real_h
    convolved = inverse(real_p, imag_p, tables)
    return (convolved + own_gain[:, None] * kv_values).astype(jnp.bfloat16)


def featurize(extended, weights, length):
    tap_count = weights.shape[1]
    running = jnp.zeros(extended.shape[:1] + (length,) + extended.shape[2:], jnp.float32)
    for lag_idx in range(tap_count):
        offset = tap_count - 1 - lag_idx
        running = running + weights[:, lag_idx, None, :] * extended[
            :, offset : offset + length, :
        ].astype(jnp.float32)
    return running.astype(jnp.bfloat16)


def _feat_body(proj_ref, prior_ref, w_ref, q_ref, kv_ref, ext_ref):
    rows = proj_ref.shape[1]
    feats = []
    for a in range(3):
        ext_ref[0:2, :] = jnp.zeros((2, ext_ref.shape[1]), jnp.float32)
        ext_ref[2:8, :] = prior_ref[a].astype(jnp.float32)
        ext_ref[8 : 8 + rows, :] = proj_ref[a].astype(jnp.float32)
        acc = jnp.zeros((rows, ext_ref.shape[1]), jnp.float32)
        for j in range(KS):
            acc = acc + w_ref[a, j : j + 1, :] * ext_ref[8 - j : 8 - j + rows, :]
        feats.append(acc.astype(jnp.bfloat16))
    q_ref[...] = feats[0].astype(jnp.float32).T.astype(jnp.bfloat16)
    kv = feats[1].astype(jnp.float32) * feats[2].astype(jnp.float32)
    kv_ref[...] = kv.astype(jnp.bfloat16).astype(jnp.float32).T.astype(jnp.bfloat16)

def featurize_kv(projected, prior, weights, lane_block=128, interpret=False):
    _, rows, chans = projected.shape
    grid = (chans // lane_block,)
    return pl.pallas_call(
        _feat_body,
        grid=grid,
        in_specs=[
            pl.BlockSpec((3, rows, lane_block), lambda i: (0, 0, i)),
            pl.BlockSpec((3, KS - 1, lane_block), lambda i: (0, 0, i)),
            pl.BlockSpec((3, KS, lane_block), lambda i: (0, 0, i)),
        ],
        out_specs=[
            pl.BlockSpec((lane_block, rows), lambda i: (i, 0)),
            pl.BlockSpec((lane_block, rows), lambda i: (i, 0)),
        ],
        out_shape=[jax.ShapeDtypeStruct((chans, rows), jnp.bfloat16)] * 2,
        scratch_shapes=[pltpu.VMEM((rows + 8, lane_block), jnp.float32)],
        interpret=interpret,
    )(projected, prior, weights)


def _split(a):
    hi = a.astype(jnp.bfloat16)
    return hi, (a - hi.astype(jnp.float32)).astype(jnp.bfloat16)


def _mm(a, b):
    return jnp.dot(a, b, preferred_element_type=jnp.float32)


def _left3(t_hi, t_lo, v):
    v_hi, v_lo = _split(v)
    return _mm(t_hi, v_hi) + _mm(t_lo, v_hi) + _mm(t_hi, v_lo)


def _right3(v, t_hi, t_lo):
    v_hi, v_lo = _split(v)
    return _mm(v_hi, t_hi) + _mm(v_lo, t_hi) + _mm(v_hi, t_lo)


def _spectrum(a_re, a_im, ct, st, cbsb_h, cbsb_l):
    rows, width = ct.shape
    t_re = a_re * ct + a_im * st
    t_im = a_im * ct - a_re * st
    r = _right3(jnp.concatenate([t_re, t_im], axis=0), cbsb_h, cbsb_l)
    f_re = r[:rows, :width] + r[rows:, width:]
    f_im = r[rows:, :width] - r[:rows, width:]
    return f_re, f_im


def _filter_body(h_ref, casa_h, casa_l, cbsb_h, cbsb_l, ct_ref, st_ref, re_ref, im_ref):
    ct = ct_ref[...]
    st = st_ref[...]
    rows = ct.shape[0]
    for c in range(h_ref.shape[0]):
        a = _left3(casa_h[...], casa_l[...], h_ref[c])
        re_ref[c], im_ref[c] = _spectrum(a[:rows], -a[rows:], ct, st, cbsb_h[...], cbsb_l[...])


def _conv_body(x_ref, fh_re_ref, fh_im_ref, g_ref, casa_h, casa_l, cbsb_h, cbsb_l,
               ct_ref, st_ref, ctw_ref, stw_ref, inv_h, inv_l, o_ref):
    ct = ct_ref[...]
    st = st_ref[...]
    rows, width = ct.shape
    chans = fh_re_ref.shape[0]
    x_b = x_ref[...]
    a = _mm(casa_h[...], x_b) + _mm(casa_l[...], x_b)
    ctw = ctw_ref[...]
    stw = stw_ref[...]
    a_re = a[:rows]
    a_im = -a[rows:]
    t_re = a_re * ctw + a_im * stw
    t_im = a_im * ctw - a_re * stw
    pieces = []
    for c in range(chans):
        pieces.append(t_re[:, c * width : (c + 1) * width])
        pieces.append(t_im[:, c * width : (c + 1) * width])
    r = _right3(jnp.concatenate(pieces, axis=0), cbsb_h[...], cbsb_l[...])
    prods = []
    for c in range(chans):
        lo = 2 * rows * c
        f_re = r[lo : lo + rows, :width] + r[lo + rows : lo + 2 * rows, width:]
        f_im = r[lo + rows : lo + 2 * rows, :width] - r[lo : lo + rows, width:]
        fh_re = fh_re_ref[c]
        fh_im = fh_im_ref[c]
        prods.append(f_re * fh_re - f_im * fh_im)
        prods.append(f_re * fh_im + f_im * fh_re)
    q = _right3(jnp.concatenate(prods, axis=0), cbsb_h[...], cbsb_l[...])
    cols = []
    for c in range(chans):
        lo = 2 * rows * c
        z_re = q[lo : lo + rows, :width] - q[lo + rows : lo + 2 * rows, width:]
        z_im = q[lo + rows : lo + 2 * rows, :width] + q[lo : lo + rows, width:]
        w_re = z_re * ct - z_im * st
        w_im = z_im * ct + z_re * st
        cols.append(jnp.concatenate([w_re, w_im], axis=0))
    out = _left3(inv_h[...], inv_l[...], jnp.concatenate(cols, axis=1))
    x_f = x_b.astype(jnp.float32)
    o_ref[...] = (out * (1.0 / (rows * width)) + g_ref[...] * x_f).astype(jnp.bfloat16)


def conv_tables(size_a, size_b):
    whole = size_a * size_b
    half_a = size_a // 2

    def pair(r, c, period):
        ri = lax.broadcasted_iota(jnp.int32, (r, c), 0)
        ci = lax.broadcasted_iota(jnp.int32, (r, c), 1)
        ang = (ri * ci % period).astype(jnp.float32) * (2.0 * math.pi / period)
        return jnp.cos(ang), jnp.sin(ang)

    cos_a, sin_a = pair(size_a, half_a, size_a)
    cos_b, sin_b = pair(size_b, size_b, size_b)
    cos_t, sin_t = pair(size_a, size_b, whole)
    inv = jnp.concatenate([cos_a.T, -sin_a.T], axis=1)
    casa = jnp.concatenate([cos_a, sin_a], axis=0)
    cbsb = jnp.concatenate([cos_b, sin_b], axis=1)
    return (*_split(casa), *_split(cbsb), cos_t, sin_t, *_split(inv))


def filter_spectrum(filt, tabs, ch_block=2, size_b=256):
    ch, length = filt.shape
    half_a = length // size_b
    size_a = 2 * half_a
    h = filt.reshape(ch, half_a, size_b)
    full = lambda t: pl.BlockSpec(t.shape, lambda i: (0,) * t.ndim)
    blk_out = pl.BlockSpec((ch_block, size_a, size_b), lambda i: (i, 0, 0))
    return pl.pallas_call(
        _filter_body,
        grid=(ch // ch_block,),
        in_specs=[pl.BlockSpec((ch_block, half_a, size_b), lambda i: (i, 0, 0))]
        + [full(t) for t in tabs[:6]],
        out_specs=[blk_out, blk_out],
        out_shape=[jax.ShapeDtypeStruct((ch, size_a, size_b), jnp.float32)] * 2,
    )(h, *tabs[:6])


def long_conv(x, spectrum, gain, tabs):
    blocks, lanes = x.shape
    ch = gain.shape[0]
    size_b = lanes // ch
    g = jnp.repeat(gain, size_b)[None, :]
    casa_h, casa_l, cbsb_h, cbsb_l, cos_t, sin_t, inv_h, inv_l = tabs
    ctw = jnp.tile(cos_t, (1, ch))
    stw = jnp.tile(sin_t, (1, ch))
    return pl.pallas_call(
        _conv_body,
        out_shape=jax.ShapeDtypeStruct((blocks, lanes), jnp.bfloat16),
    )(x, *spectrum, g, casa_h, casa_l, cbsb_h, cbsb_l, cos_t, sin_t, ctw, stw, inv_h, inv_l)


def _proj_body(f_ref, q_ref, w_ref, s_ref, o_ref, g_scr):
    @pl.when(pl.program_id(0) == 0)
    def _():
        gated = (q_ref[...].astype(jnp.float32) * f_ref[...].astype(jnp.float32)).astype(jnp.bfloat16)
        g_scr[...] = gated.astype(jnp.float32).T.astype(jnp.bfloat16)

    width = o_ref.shape[2]
    for p in range(o_ref.shape[0]):
        acc = None
        for b in range(w_ref.shape[0] // BLK):
            part = jnp.dot(g_scr[:, b * BLK : (b + 1) * BLK],
                           w_ref[b * BLK : (b + 1) * BLK, p * width : (p + 1) * width],
                           preferred_element_type=jnp.float32) * s_ref[b : b + 1, p * width : (p + 1) * width]
            acc = part if acc is None else acc + part
        o_ref[p] = acc.astype(jnp.bfloat16)


def project(filtered_home, q_cols, out_values, scale_cols, n_pieces, steps=2):
    chans, rows = filtered_home.shape
    width = out_values.shape[1] // n_pieces
    per_step = n_pieces // steps
    return pl.pallas_call(
        _proj_body,
        grid=(steps,),
        in_specs=[
            pl.BlockSpec((chans, rows), lambda j: (0, 0)),
            pl.BlockSpec((chans, rows), lambda j: (0, 0)),
            pl.BlockSpec((chans, width * per_step), lambda j: (0, j)),
            pl.BlockSpec((scale_cols.shape[0], width * per_step), lambda j: (0, j)),
        ],
        out_specs=pl.BlockSpec((per_step, rows, width), lambda j: (j, 0, 0)),
        out_shape=jax.ShapeDtypeStruct((n_pieces, rows, width), jnp.bfloat16),
        scratch_shapes=[pltpu.VMEM((rows, chans), jnp.bfloat16)],
    )(filtered_home, q_cols, out_values, scale_cols)


def multiply_round(left_arr, right_arr):
    return (left_arr.astype(jnp.float32) * right_arr.astype(jnp.float32)).astype(jnp.bfloat16)


def local(projected, feat_weight, long_filter, skip_gain, out_values, out_scales):
    groups = lax.axis_size("seq")
    tok_rows = projected.shape[1]
    local_ch = projected.shape[2]
    length = tok_rows * groups
    rim_width = KS - 1
    prior_rows = passed_along(projected[:, tok_rows - rim_width :, :], "seq", 1)
    q_feat, gated_kv = featurize_kv(projected, prior_rows, feat_weight)
    tabs = conv_tables(2 * length // 256, 256)
    spectrum = filter_spectrum(long_filter, tabs)
    kv_owned = lax.all_to_all(gated_kv.reshape(groups, -1, tok_rows), "seq", 0, 0, tiled=True)
    filtered = long_conv(kv_owned.reshape(groups, -1), spectrum, skip_gain, tabs)
    filtered_home = lax.all_to_all(filtered, "seq", 0, 0, tiled=True).reshape(local_ch, tok_rows)
    n_tensor = lax.axis_size("tensor")
    scale_cols = jnp.repeat(out_scales, BLK, axis=1)
    pieces = project(filtered_home, q_feat, out_values, scale_cols, n_tensor)
    gathered = lax.all_to_all(pieces, "tensor", 0, 0, tiled=True)
    return jnp.sum(gathered.astype(jnp.float32), axis=0).astype(jnp.bfloat16)


def solution(mesh):
    return jax.shard_map(
        local,
        mesh=mesh,
        in_specs=(
            P(None, "seq", "tensor"),
            P(None, None, "tensor"),
            P(("tensor", "seq"), None),
            P(("tensor", "seq")),
            P("tensor", None),
            P("tensor", None),
        ),
        out_specs=P("seq", "tensor"),
        check_vma=False,
    )
```

```python
import math

import jax
import jax.numpy as jnp
from jax import lax
from jax.sharding import PartitionSpec as P
from jax.experimental import pallas as pl
from jax.experimental.pallas import tpu as pltpu

KS = 7
BLK = 128


TRIPLE = lax.Precision.HIGH


def passed_along(x, axis, by):
    size = lax.axis_size(axis)
    pairs = [(i, i + by) for i in range(size) if 0 <= i + by < size]
    return lax.ppermute(x, axis, pairs)


def split_length(whole):
    for candidate in range(2, whole + 1, 2):
        if whole % candidate == 0 and candidate * candidate >= whole:
            return (candidate, whole // candidate)
    return (whole, 1)


def angle_pair(row_count, col_count, period):
    row_ids = lax.broadcasted_iota(jnp.int32, (row_count, col_count), 0)
    col_ids = lax.broadcasted_iota(jnp.int32, (row_count, col_count), 1)
    angles = (row_ids * col_ids % period).astype(jnp.float32) * (2.0 * math.pi / period)
    return (jnp.cos(angles), jnp.sin(angles))


def make_tables(length):
    whole = 2 * length
    size_a, size_b = split_length(whole)
    return (
        angle_pair(size_a, size_a, size_a),
        angle_pair(size_b, size_b, size_b),
        angle_pair(size_a, size_b, whole),
        size_a,
        size_b,
    )


def right_mul(signal, matrix):
    return jnp.einsum("ckn,nm->ckm", signal, matrix, precision=TRIPLE)


def forward(signal, tables):
    (cos_a, sin_a), (cos_b, sin_b), (cos_t, sin_t), size_a, size_b = tables
    half_a = size_a // 2
    blocks = signal.reshape(signal.shape[0], half_a, size_b)
    real_a = jnp.einsum("kn,cnb->ckb", cos_a[:, :half_a], blocks, precision=TRIPLE)
    imag_a = -jnp.einsum("kn,cnb->ckb", sin_a[:, :half_a], blocks, precision=TRIPLE)
    real_t = real_a * cos_t + imag_a * sin_t
    imag_t = imag_a * cos_t - real_a * sin_t
    real_f = right_mul(real_t, cos_b) + right_mul(imag_t, sin_b)
    imag_f = right_mul(imag_t, cos_b) - right_mul(real_t, sin_b)
    return (real_f, imag_f)


def inverse(real_f, imag_f, tables):
    (cos_a, sin_a), (cos_b, sin_b), (cos_t, sin_t), size_a, size_b = tables
    half_a = size_a // 2
    real_z = right_mul(real_f, cos_b) - right_mul(imag_f, sin_b)
    imag_z = right_mul(imag_f, cos_b) + right_mul(real_f, sin_b)
    real_w = real_z * cos_t - imag_z * sin_t
    imag_w = imag_z * cos_t + real_z * sin_t
    out_half = jnp.einsum("nk,ckb->cnb", cos_a[:half_a, :], real_w, precision=TRIPLE) - jnp.einsum(
        "nk,ckb->cnb", sin_a[:half_a, :], imag_w, precision=TRIPLE
    )
    return out_half.reshape(out_half.shape[0], half_a * size_b) * (1.0 / (size_a * size_b))


def long_mix(gated_kv, spectrum, own_gain, tables):
    kv_values = gated_kv.astype(jnp.float32)
    real_u, imag_u = forward(kv_values, tables)
    real_h, imag_h = spectrum
    real_p = real_u * real_h - imag_u * imag_h
    imag_p = real_u * imag_h + imag_u * real_h
    convolved = inverse(real_p, imag_p, tables)
    return (convolved + own_gain[:, None] * kv_values).astype(jnp.bfloat16)


def featurize(extended, weights, length):
    tap_count = weights.shape[1]
    running = jnp.zeros(extended.shape[:1] + (length,) + extended.shape[2:], jnp.float32)
    for lag_idx in range(tap_count):
        offset = tap_count - 1 - lag_idx
        running = running + weights[:, lag_idx, None, :] * extended[
            :, offset : offset + length, :
        ].astype(jnp.float32)
    return running.astype(jnp.bfloat16)


def _feat_body(proj_ref, prior_ref, w_ref, q_ref, kv_ref, ext_ref):
    rows = proj_ref.shape[1]
    feats = []
    for a in range(3):
        ext_ref[0:2, :] = jnp.zeros((2, ext_ref.shape[1]), jnp.float32)
        ext_ref[2:8, :] = prior_ref[a].astype(jnp.float32)
        ext_ref[8 : 8 + rows, :] = proj_ref[a].astype(jnp.float32)
        acc = jnp.zeros((rows, ext_ref.shape[1]), jnp.float32)
        for j in range(KS):
            acc = acc + w_ref[a, j : j + 1, :] * ext_ref[8 - j : 8 - j + rows, :]
        feats.append(acc.astype(jnp.bfloat16))
    q_ref[...] = feats[0].astype(jnp.float32).T.astype(jnp.bfloat16)
    kv = feats[1].astype(jnp.float32) * feats[2].astype(jnp.float32)
    kv_ref[...] = kv.astype(jnp.bfloat16).astype(jnp.float32).T.astype(jnp.bfloat16)

def featurize_kv(projected, prior, weights, lane_block=128, interpret=False):
    _, rows, chans = projected.shape
    grid = (chans // lane_block,)
    return pl.pallas_call(
        _feat_body,
        grid=grid,
        in_specs=[
            pl.BlockSpec((3, rows, lane_block), lambda i: (0, 0, i)),
            pl.BlockSpec((3, KS - 1, lane_block), lambda i: (0, 0, i)),
            pl.BlockSpec((3, KS, lane_block), lambda i: (0, 0, i)),
        ],
        out_specs=[
            pl.BlockSpec((lane_block, rows), lambda i: (i, 0)),
            pl.BlockSpec((lane_block, rows), lambda i: (i, 0)),
        ],
        out_shape=[jax.ShapeDtypeStruct((chans, rows), jnp.bfloat16)] * 2,
        scratch_shapes=[pltpu.VMEM((rows + 8, lane_block), jnp.float32)],
        interpret=interpret,
    )(projected, prior, weights)


def _split(a):
    hi = a.astype(jnp.bfloat16)
    return hi, (a - hi.astype(jnp.float32)).astype(jnp.bfloat16)


def _mm(a, b):
    return jnp.dot(a, b, preferred_element_type=jnp.float32)


def _left3(t_hi, t_lo, v):
    v_hi, v_lo = _split(v)
    return _mm(t_hi, v_hi) + _mm(t_lo, v_hi) + _mm(t_hi, v_lo)


def _right3(v, t_hi, t_lo):
    v_hi, v_lo = _split(v)
    return _mm(v_hi, t_hi) + _mm(v_lo, t_hi) + _mm(v_hi, t_lo)


def _spectrum(a_re, a_im, ct, st, cbsb_h, cbsb_l):
    rows, width = ct.shape
    t_re = a_re * ct + a_im * st
    t_im = a_im * ct - a_re * st
    r = _right3(jnp.concatenate([t_re, t_im], axis=0), cbsb_h, cbsb_l)
    f_re = r[:rows, :width] + r[rows:, width:]
    f_im = r[rows:, :width] - r[:rows, width:]
    return f_re, f_im


def _filter_body(h_ref, casa_h, casa_l, cbsb_h, cbsb_l, ct_ref, st_ref, re_ref, im_ref):
    ct = ct_ref[...]
    st = st_ref[...]
    rows = ct.shape[0]
    for c in range(h_ref.shape[0]):
        a = _left3(casa_h[...], casa_l[...], h_ref[c])
        re_ref[c], im_ref[c] = _spectrum(a[:rows], -a[rows:], ct, st, cbsb_h[...], cbsb_l[...])


def _conv_body(x_ref, fh_re_ref, fh_im_ref, g_ref, casa_h, casa_l, cbsb_h, cbsb_l,
               ct_ref, st_ref, inv_h, inv_l, o_ref):
    ct = ct_ref[...]
    st = st_ref[...]
    rows, width = ct.shape
    chans = fh_re_ref.shape[0]
    x_b = x_ref[...]
    a = _mm(casa_h[...], x_b) + _mm(casa_l[...], x_b)
    pieces = []
    for c in range(chans):
        a_re = a[:rows, c * width : (c + 1) * width]
        a_im = -a[rows:, c * width : (c + 1) * width]
        pieces.append(a_re * ct + a_im * st)
        pieces.append(a_im * ct - a_re * st)
    r = _right3(jnp.concatenate(pieces, axis=0), cbsb_h[...], cbsb_l[...])
    prods = []
    for c in range(chans):
        lo = 2 * rows * c
        f_re = r[lo : lo + rows, :width] + r[lo + rows : lo + 2 * rows, width:]
        f_im = r[lo + rows : lo + 2 * rows, :width] - r[lo : lo + rows, width:]
        fh_re = fh_re_ref[c]
        fh_im = fh_im_ref[c]
        prods.append(f_re * fh_re - f_im * fh_im)
        prods.append(f_re * fh_im + f_im * fh_re)
    q = _right3(jnp.concatenate(prods, axis=0), cbsb_h[...], cbsb_l[...])
    cols = []
    for c in range(chans):
        lo = 2 * rows * c
        z_re = q[lo : lo + rows, :width] - q[lo + rows : lo + 2 * rows, width:]
        z_im = q[lo + rows : lo + 2 * rows, :width] + q[lo : lo + rows, width:]
        w_re = z_re * ct - z_im * st
        w_im = z_im * ct + z_re * st
        cols.append(jnp.concatenate([w_re, w_im], axis=0))
    out = _left3(inv_h[...], inv_l[...], jnp.concatenate(cols, axis=1))
    x_f = x_b.astype(jnp.float32)
    o_ref[...] = (out * (1.0 / (rows * width)) + g_ref[...] * x_f).astype(jnp.bfloat16)


def conv_tables(size_a, size_b):
    whole = size_a * size_b
    half_a = size_a // 2

    def pair(r, c, period):
        ri = lax.broadcasted_iota(jnp.int32, (r, c), 0)
        ci = lax.broadcasted_iota(jnp.int32, (r, c), 1)
        ang = (ri * ci % period).astype(jnp.float32) * (2.0 * math.pi / period)
        return jnp.cos(ang), jnp.sin(ang)

    cos_a, sin_a = pair(size_a, half_a, size_a)
    cos_b, sin_b = pair(size_b, size_b, size_b)
    cos_t, sin_t = pair(size_a, size_b, whole)
    inv = jnp.concatenate([cos_a.T, -sin_a.T], axis=1)
    casa = jnp.concatenate([cos_a, sin_a], axis=0)
    cbsb = jnp.concatenate([cos_b, sin_b], axis=1)
    return (*_split(casa), *_split(cbsb), cos_t, sin_t, *_split(inv))


def filter_spectrum(filt, tabs, ch_block=2, size_b=256):
    ch, length = filt.shape
    half_a = length // size_b
    size_a = 2 * half_a
    h = filt.reshape(ch, half_a, size_b)
    full = lambda t: pl.BlockSpec(t.shape, lambda i: (0,) * t.ndim)
    blk_out = pl.BlockSpec((ch_block, size_a, size_b), lambda i: (i, 0, 0))
    return pl.pallas_call(
        _filter_body,
        grid=(ch // ch_block,),
        in_specs=[pl.BlockSpec((ch_block, half_a, size_b), lambda i: (i, 0, 0))]
        + [full(t) for t in tabs[:6]],
        out_specs=[blk_out, blk_out],
        out_shape=[jax.ShapeDtypeStruct((ch, size_a, size_b), jnp.float32)] * 2,
    )(h, *tabs[:6])


def long_conv(x, spectrum, gain, tabs):
    blocks, lanes = x.shape
    ch = gain.shape[0]
    size_b = lanes // ch
    g = jnp.repeat(gain, size_b)[None, :]
    casa_h, casa_l, cbsb_h, cbsb_l, cos_t, sin_t, inv_h, inv_l = tabs
    return pl.pallas_call(
        _conv_body,
        out_shape=jax.ShapeDtypeStruct((blocks, lanes), jnp.bfloat16),
    )(x, *spectrum, g, casa_h, casa_l, cbsb_h, cbsb_l, cos_t, sin_t, inv_h, inv_l)


def _proj_body(f_ref, q_ref, w_ref, s_ref, o_ref, g_scr):
    @pl.when(pl.program_id(0) == 0)
    def _():
        gated = (q_ref[...].astype(jnp.float32) * f_ref[...].astype(jnp.float32)).astype(jnp.bfloat16)
        g_scr[...] = gated.astype(jnp.float32).T.astype(jnp.bfloat16)

    width = o_ref.shape[2]
    for p in range(o_ref.shape[0]):
        acc = None
        for b in range(w_ref.shape[0] // BLK):
            part = jnp.dot(g_scr[:, b * BLK : (b + 1) * BLK],
                           w_ref[b * BLK : (b + 1) * BLK, p * width : (p + 1) * width],
                           preferred_element_type=jnp.float32) * s_ref[b : b + 1, p * width : (p + 1) * width]
            acc = part if acc is None else acc + part
        o_ref[p] = acc.astype(jnp.bfloat16)


def project(filtered_home, q_cols, out_values, scale_cols, n_pieces, steps=2):
    chans, rows = filtered_home.shape
    width = out_values.shape[1] // n_pieces
    per_step = n_pieces // steps
    return pl.pallas_call(
        _proj_body,
        grid=(steps,),
        in_specs=[
            pl.BlockSpec((chans, rows), lambda j: (0, 0)),
            pl.BlockSpec((chans, rows), lambda j: (0, 0)),
            pl.BlockSpec((chans, width * per_step), lambda j: (0, j)),
            pl.BlockSpec((scale_cols.shape[0], width * per_step), lambda j: (0, j)),
        ],
        out_specs=pl.BlockSpec((per_step, rows, width), lambda j: (j, 0, 0)),
        out_shape=jax.ShapeDtypeStruct((n_pieces, rows, width), jnp.bfloat16),
        scratch_shapes=[pltpu.VMEM((rows, chans), jnp.bfloat16)],
    )(filtered_home, q_cols, out_values, scale_cols)


def multiply_round(left_arr, right_arr):
    return (left_arr.astype(jnp.float32) * right_arr.astype(jnp.float32)).astype(jnp.bfloat16)


def local(projected, feat_weight, long_filter, skip_gain, out_values, out_scales):
    groups = lax.axis_size("seq")
    tok_rows = projected.shape[1]
    local_ch = projected.shape[2]
    length = tok_rows * groups
    rim_width = KS - 1
    prior_rows = passed_along(projected[:, tok_rows - rim_width :, :], "seq", 1)
    q_feat, gated_kv = featurize_kv(projected, prior_rows, feat_weight)
    tabs = conv_tables(2 * length // 256, 256)
    spectrum = filter_spectrum(long_filter, tabs)
    kv_owned = lax.all_to_all(gated_kv.reshape(groups, -1, tok_rows), "seq", 0, 0, tiled=True)
    filtered = long_conv(kv_owned.reshape(groups, -1), spectrum, skip_gain, tabs)
    filtered = filtered.reshape(groups, -1, tok_rows)
    filtered_home = lax.all_to_all(filtered, "seq", 0, 0, tiled=True).reshape(local_ch, tok_rows)
    n_tensor = lax.axis_size("tensor")
    scale_cols = jnp.repeat(out_scales, BLK, axis=1)
    pieces = project(filtered_home, q_feat, out_values, scale_cols, n_tensor)
    gathered = lax.all_to_all(pieces, "tensor", 0, 0, tiled=True)
    return jnp.sum(gathered.astype(jnp.float32), axis=0).astype(jnp.bfloat16)


def solution(mesh):
    return jax.shard_map(
        local,
        mesh=mesh,
        in_specs=(
            P(None, "seq", "tensor"),
            P(None, None, "tensor"),
            P(("tensor", "seq"), None),
            P(("tensor", "seq")),
            P("tensor", None),
            P("tensor", None),
        ),
        out_specs=P("seq", "tensor"),
        check_vma=False,
    )
```

```python
import math

import jax
import jax.numpy as jnp
from jax import lax
from jax.sharding import PartitionSpec as P
from jax.experimental import pallas as pl
from jax.experimental.pallas import tpu as pltpu

KS = 7
BLK = 128


TRIPLE = lax.Precision.HIGH


def passed_along(x, axis, by):
    size = lax.axis_size(axis)
    pairs = [(i, i + by) for i in range(size) if 0 <= i + by < size]
    return lax.ppermute(x, axis, pairs)


def split_length(whole):
    for candidate in range(2, whole + 1, 2):
        if whole % candidate == 0 and candidate * candidate >= whole:
            return (candidate, whole // candidate)
    return (whole, 1)


def angle_pair(row_count, col_count, period):
    row_ids = lax.broadcasted_iota(jnp.int32, (row_count, col_count), 0)
    col_ids = lax.broadcasted_iota(jnp.int32, (row_count, col_count), 1)
    angles = (row_ids * col_ids % period).astype(jnp.float32) * (2.0 * math.pi / period)
    return (jnp.cos(angles), jnp.sin(angles))


def make_tables(length):
    whole = 2 * length
    size_a, size_b = split_length(whole)
    return (
        angle_pair(size_a, size_a, size_a),
        angle_pair(size_b, size_b, size_b),
        angle_pair(size_a, size_b, whole),
        size_a,
        size_b,
    )


def right_mul(signal, matrix):
    return jnp.einsum("ckn,nm->ckm", signal, matrix, precision=TRIPLE)


def forward(signal, tables):
    (cos_a, sin_a), (cos_b, sin_b), (cos_t, sin_t), size_a, size_b = tables
    half_a = size_a // 2
    blocks = signal.reshape(signal.shape[0], half_a, size_b)
    real_a = jnp.einsum("kn,cnb->ckb", cos_a[:, :half_a], blocks, precision=TRIPLE)
    imag_a = -jnp.einsum("kn,cnb->ckb", sin_a[:, :half_a], blocks, precision=TRIPLE)
    real_t = real_a * cos_t + imag_a * sin_t
    imag_t = imag_a * cos_t - real_a * sin_t
    real_f = right_mul(real_t, cos_b) + right_mul(imag_t, sin_b)
    imag_f = right_mul(imag_t, cos_b) - right_mul(real_t, sin_b)
    return (real_f, imag_f)


def inverse(real_f, imag_f, tables):
    (cos_a, sin_a), (cos_b, sin_b), (cos_t, sin_t), size_a, size_b = tables
    half_a = size_a // 2
    real_z = right_mul(real_f, cos_b) - right_mul(imag_f, sin_b)
    imag_z = right_mul(imag_f, cos_b) + right_mul(real_f, sin_b)
    real_w = real_z * cos_t - imag_z * sin_t
    imag_w = imag_z * cos_t + real_z * sin_t
    out_half = jnp.einsum("nk,ckb->cnb", cos_a[:half_a, :], real_w, precision=TRIPLE) - jnp.einsum(
        "nk,ckb->cnb", sin_a[:half_a, :], imag_w, precision=TRIPLE
    )
    return out_half.reshape(out_half.shape[0], half_a * size_b) * (1.0 / (size_a * size_b))


def long_mix(gated_kv, spectrum, own_gain, tables):
    kv_values = gated_kv.astype(jnp.float32)
    real_u, imag_u = forward(kv_values, tables)
    real_h, imag_h = spectrum
    real_p = real_u * real_h - imag_u * imag_h
    imag_p = real_u * imag_h + imag_u * real_h
    convolved = inverse(real_p, imag_p, tables)
    return (convolved + own_gain[:, None] * kv_values).astype(jnp.bfloat16)


def featurize(extended, weights, length):
    tap_count = weights.shape[1]
    running = jnp.zeros(extended.shape[:1] + (length,) + extended.shape[2:], jnp.float32)
    for lag_idx in range(tap_count):
        offset = tap_count - 1 - lag_idx
        running = running + weights[:, lag_idx, None, :] * extended[
            :, offset : offset + length, :
        ].astype(jnp.float32)
    return running.astype(jnp.bfloat16)


def _feat_body(proj_ref, prior_ref, w_ref, q_ref, kv_ref, ext_ref):
    rows = proj_ref.shape[1]
    feats = []
    for a in range(3):
        ext_ref[0:2, :] = jnp.zeros((2, ext_ref.shape[1]), jnp.float32)
        ext_ref[2:8, :] = prior_ref[a].astype(jnp.float32)
        ext_ref[8 : 8 + rows, :] = proj_ref[a].astype(jnp.float32)
        acc = jnp.zeros((rows, ext_ref.shape[1]), jnp.float32)
        for j in range(KS):
            acc = acc + w_ref[a, j : j + 1, :] * ext_ref[8 - j : 8 - j + rows, :]
        feats.append(acc.astype(jnp.bfloat16))
    q_ref[...] = feats[0].astype(jnp.float32).T.astype(jnp.bfloat16)
    kv = feats[1].astype(jnp.float32) * feats[2].astype(jnp.float32)
    kv_ref[...] = kv.astype(jnp.bfloat16).astype(jnp.float32).T.astype(jnp.bfloat16)

def featurize_kv(projected, prior, weights, lane_block=128, interpret=False):
    _, rows, chans = projected.shape
    grid = (chans // lane_block,)
    return pl.pallas_call(
        _feat_body,
        grid=grid,
        in_specs=[
            pl.BlockSpec((3, rows, lane_block), lambda i: (0, 0, i)),
            pl.BlockSpec((3, KS - 1, lane_block), lambda i: (0, 0, i)),
            pl.BlockSpec((3, KS, lane_block), lambda i: (0, 0, i)),
        ],
        out_specs=[
            pl.BlockSpec((lane_block, rows), lambda i: (i, 0)),
            pl.BlockSpec((lane_block, rows), lambda i: (i, 0)),
        ],
        out_shape=[jax.ShapeDtypeStruct((chans, rows), jnp.bfloat16)] * 2,
        scratch_shapes=[pltpu.VMEM((rows + 8, lane_block), jnp.float32)],
        interpret=interpret,
    )(projected, prior, weights)


def _split(a):
    hi = a.astype(jnp.bfloat16)
    return hi, (a - hi.astype(jnp.float32)).astype(jnp.bfloat16)


def _mm(a, b):
    return jnp.dot(a, b, preferred_element_type=jnp.float32)


def _left3(t_hi, t_lo, v):
    v_hi, v_lo = _split(v)
    return _mm(t_hi, v_hi) + _mm(t_lo, v_hi) + _mm(t_hi, v_lo)


def _right3(v, t_hi, t_lo):
    v_hi, v_lo = _split(v)
    return _mm(v_hi, t_hi) + _mm(v_lo, t_hi) + _mm(v_hi, t_lo)


def _spectrum(a_re, a_im, ct, st, cbsb_h, cbsb_l):
    rows, width = ct.shape
    t_re = a_re * ct + a_im * st
    t_im = a_im * ct - a_re * st
    r = _right3(jnp.concatenate([t_re, t_im], axis=0), cbsb_h, cbsb_l)
    f_re = r[:rows, :width] + r[rows:, width:]
    f_im = r[rows:, :width] - r[:rows, width:]
    return f_re, f_im


def _filter_body(h_ref, casa_h, casa_l, cbsb_h, cbsb_l, ct_ref, st_ref, re_ref, im_ref):
    ct = ct_ref[...]
    st = st_ref[...]
    rows = ct.shape[0]
    for c in range(h_ref.shape[0]):
        a = _left3(casa_h[...], casa_l[...], h_ref[c])
        re_ref[c], im_ref[c] = _spectrum(a[:rows], -a[rows:], ct, st, cbsb_h[...], cbsb_l[...])


def _conv_body(x_ref, fh_re_ref, fh_im_ref, g_ref, casa_h, casa_l, cbsb_h, cbsb_l,
               ct_ref, st_ref, inv_h, inv_l, o_ref):
    ct = ct_ref[...]
    st = st_ref[...]
    rows, width = ct.shape
    chans = fh_re_ref.shape[0]
    x_b = jnp.concatenate([x_ref[:, c, :] for c in range(chans)], axis=1)
    a = _mm(casa_h[...], x_b) + _mm(casa_l[...], x_b)
    pieces = []
    for c in range(chans):
        a_re = a[:rows, c * width : (c + 1) * width]
        a_im = -a[rows:, c * width : (c + 1) * width]
        pieces.append(a_re * ct + a_im * st)
        pieces.append(a_im * ct - a_re * st)
    r = _right3(jnp.concatenate(pieces, axis=0), cbsb_h[...], cbsb_l[...])
    prods = []
    for c in range(chans):
        lo = 2 * rows * c
        f_re = r[lo : lo + rows, :width] + r[lo + rows : lo + 2 * rows, width:]
        f_im = r[lo + rows : lo + 2 * rows, :width] - r[lo : lo + rows, width:]
        fh_re = fh_re_ref[c]
        fh_im = fh_im_ref[c]
        prods.append(f_re * fh_re - f_im * fh_im)
        prods.append(f_re * fh_im + f_im * fh_re)
    q = _right3(jnp.concatenate(prods, axis=0), cbsb_h[...], cbsb_l[...])
    cols = []
    for c in range(chans):
        lo = 2 * rows * c
        z_re = q[lo : lo + rows, :width] - q[lo + rows : lo + 2 * rows, width:]
        z_im = q[lo + rows : lo + 2 * rows, :width] + q[lo : lo + rows, width:]
        w_re = z_re * ct - z_im * st
        w_im = z_im * ct + z_re * st
        cols.append(jnp.concatenate([w_re, w_im], axis=0))
    out = _left3(inv_h[...], inv_l[...], jnp.concatenate(cols, axis=1))
    res = (out * (1.0 / (rows * width)) + g_ref[...] * x_b.astype(jnp.float32)).astype(jnp.bfloat16)
    for c in range(chans):
        o_ref[:, c, :] = res[:, c * width : (c + 1) * width]


def conv_tables(size_a, size_b):
    whole = size_a * size_b
    half_a = size_a // 2

    def pair(r, c, period):
        ri = lax.broadcasted_iota(jnp.int32, (r, c), 0)
        ci = lax.broadcasted_iota(jnp.int32, (r, c), 1)
        ang = (ri * ci % period).astype(jnp.float32) * (2.0 * math.pi / period)
        return jnp.cos(ang), jnp.sin(ang)

    cos_a, sin_a = pair(size_a, half_a, size_a)
    cos_b, sin_b = pair(size_b, size_b, size_b)
    cos_t, sin_t = pair(size_a, size_b, whole)
    inv = jnp.concatenate([cos_a.T, -sin_a.T], axis=1)
    casa = jnp.concatenate([cos_a, sin_a], axis=0)
    cbsb = jnp.concatenate([cos_b, sin_b], axis=1)
    return (*_split(casa), *_split(cbsb), cos_t, sin_t, *_split(inv))


def filter_spectrum(filt, tabs, ch_block=2, size_b=256):
    ch, length = filt.shape
    half_a = length // size_b
    size_a = 2 * half_a
    h = filt.reshape(ch, half_a, size_b)
    full = lambda t: pl.BlockSpec(t.shape, lambda i: (0,) * t.ndim)
    blk_out = pl.BlockSpec((ch_block, size_a, size_b), lambda i: (i, 0, 0))
    return pl.pallas_call(
        _filter_body,
        grid=(ch // ch_block,),
        in_specs=[pl.BlockSpec((ch_block, half_a, size_b), lambda i: (i, 0, 0))]
        + [full(t) for t in tabs[:6]],
        out_specs=[blk_out, blk_out],
        out_shape=[jax.ShapeDtypeStruct((ch, size_a, size_b), jnp.float32)] * 2,
    )(h, *tabs[:6])


def long_conv(x, spectrum, gain, tabs):
    blocks, ch, size_b = x.shape
    g = jnp.repeat(gain, size_b)[None, :]
    casa_h, casa_l, cbsb_h, cbsb_l, cos_t, sin_t, inv_h, inv_l = tabs
    return pl.pallas_call(
        _conv_body,
        out_shape=jax.ShapeDtypeStruct((blocks, ch, size_b), jnp.bfloat16),
    )(x, *spectrum, g, casa_h, casa_l, cbsb_h, cbsb_l, cos_t, sin_t, inv_h, inv_l)


def _proj_body(f_ref, q_ref, w_ref, s_ref, o_ref, g_scr):
    @pl.when(pl.program_id(0) == 0)
    def _():
        gated = (q_ref[...].astype(jnp.float32) * f_ref[...].astype(jnp.float32)).astype(jnp.bfloat16)
        g_scr[...] = gated.astype(jnp.float32).T.astype(jnp.bfloat16)

    width = o_ref.shape[2]
    for p in range(o_ref.shape[0]):
        acc = None
        for b in range(w_ref.shape[0] // BLK):
            part = jnp.dot(g_scr[:, b * BLK : (b + 1) * BLK],
                           w_ref[b * BLK : (b + 1) * BLK, p * width : (p + 1) * width],
                           preferred_element_type=jnp.float32) * s_ref[b : b + 1, p * width : (p + 1) * width]
            acc = part if acc is None else acc + part
        o_ref[p] = acc.astype(jnp.bfloat16)


def project(filtered_home, q_cols, out_values, scale_cols, n_pieces, steps=2):
    chans, rows = filtered_home.shape
    width = out_values.shape[1] // n_pieces
    per_step = n_pieces // steps
    return pl.pallas_call(
        _proj_body,
        grid=(steps,),
        in_specs=[
            pl.BlockSpec((chans, rows), lambda j: (0, 0)),
            pl.BlockSpec((chans, rows), lambda j: (0, 0)),
            pl.BlockSpec((chans, width * per_step), lambda j: (0, j)),
            pl.BlockSpec((scale_cols.shape[0], width * per_step), lambda j: (0, j)),
        ],
        out_specs=pl.BlockSpec((per_step, rows, width), lambda j: (j, 0, 0)),
        out_shape=jax.ShapeDtypeStruct((n_pieces, rows, width), jnp.bfloat16),
        scratch_shapes=[pltpu.VMEM((rows, chans), jnp.bfloat16)],
    )(filtered_home, q_cols, out_values, scale_cols)


def multiply_round(left_arr, right_arr):
    return (left_arr.astype(jnp.float32) * right_arr.astype(jnp.float32)).astype(jnp.bfloat16)


def local(projected, feat_weight, long_filter, skip_gain, out_values, out_scales):
    groups = lax.axis_size("seq")
    tok_rows = projected.shape[1]
    local_ch = projected.shape[2]
    length = tok_rows * groups
    rim_width = KS - 1
    prior_rows = passed_along(projected[:, tok_rows - rim_width :, :], "seq", 1)
    q_feat, gated_kv = featurize_kv(projected, prior_rows, feat_weight)
    tabs = conv_tables(2 * length // 256, 256)
    spectrum = filter_spectrum(long_filter, tabs)
    kv_owned = lax.all_to_all(gated_kv.reshape(groups, -1, tok_rows), "seq", 0, 0, tiled=True)
    filtered = long_conv(kv_owned, spectrum, skip_gain, tabs)
    filtered_home = lax.all_to_all(filtered, "seq", 0, 0, tiled=True).reshape(local_ch, tok_rows)
    n_tensor = lax.axis_size("tensor")
    scale_cols = jnp.repeat(out_scales, BLK, axis=1)
    pieces = project(filtered_home, q_feat, out_values, scale_cols, n_tensor)
    gathered = lax.all_to_all(pieces, "tensor", 0, 0, tiled=True)
    return jnp.sum(gathered.astype(jnp.float32), axis=0).astype(jnp.bfloat16)


def solution(mesh):
    return jax.shard_map(
        local,
        mesh=mesh,
        in_specs=(
            P(None, "seq", "tensor"),
            P(None, None, "tensor"),
            P(("tensor", "seq"), None),
            P(("tensor", "seq")),
            P("tensor", None),
            P("tensor", None),
        ),
        out_specs=P("seq", "tensor"),
        check_vma=False,
    )
```

```python
import math

import jax
import jax.numpy as jnp
from jax import lax
from jax.sharding import PartitionSpec as P
from jax.experimental import pallas as pl
from jax.experimental.pallas import tpu as pltpu

KS = 7
BLK = 128


TRIPLE = lax.Precision.HIGH


def passed_along(x, axis, by):
    size = lax.axis_size(axis)
    pairs = [(i, i + by) for i in range(size) if 0 <= i + by < size]
    return lax.ppermute(x, axis, pairs)


def split_length(whole):
    for candidate in range(2, whole + 1, 2):
        if whole % candidate == 0 and candidate * candidate >= whole:
            return (candidate, whole // candidate)
    return (whole, 1)


def angle_pair(row_count, col_count, period):
    row_ids = lax.broadcasted_iota(jnp.int32, (row_count, col_count), 0)
    col_ids = lax.broadcasted_iota(jnp.int32, (row_count, col_count), 1)
    angles = (row_ids * col_ids % period).astype(jnp.float32) * (2.0 * math.pi / period)
    return (jnp.cos(angles), jnp.sin(angles))


def make_tables(length):
    whole = 2 * length
    size_a, size_b = split_length(whole)
    return (
        angle_pair(size_a, size_a, size_a),
        angle_pair(size_b, size_b, size_b),
        angle_pair(size_a, size_b, whole),
        size_a,
        size_b,
    )


def right_mul(signal, matrix):
    return jnp.einsum("ckn,nm->ckm", signal, matrix, precision=TRIPLE)


def forward(signal, tables):
    (cos_a, sin_a), (cos_b, sin_b), (cos_t, sin_t), size_a, size_b = tables
    half_a = size_a // 2
    blocks = signal.reshape(signal.shape[0], half_a, size_b)
    real_a = jnp.einsum("kn,cnb->ckb", cos_a[:, :half_a], blocks, precision=TRIPLE)
    imag_a = -jnp.einsum("kn,cnb->ckb", sin_a[:, :half_a], blocks, precision=TRIPLE)
    real_t = real_a * cos_t + imag_a * sin_t
    imag_t = imag_a * cos_t - real_a * sin_t
    real_f = right_mul(real_t, cos_b) + right_mul(imag_t, sin_b)
    imag_f = right_mul(imag_t, cos_b) - right_mul(real_t, sin_b)
    return (real_f, imag_f)


def inverse(real_f, imag_f, tables):
    (cos_a, sin_a), (cos_b, sin_b), (cos_t, sin_t), size_a, size_b = tables
    half_a = size_a // 2
    real_z = right_mul(real_f, cos_b) - right_mul(imag_f, sin_b)
    imag_z = right_mul(imag_f, cos_b) + right_mul(real_f, sin_b)
    real_w = real_z * cos_t - imag_z * sin_t
    imag_w = imag_z * cos_t + real_z * sin_t
    out_half = jnp.einsum("nk,ckb->cnb", cos_a[:half_a, :], real_w, precision=TRIPLE) - jnp.einsum(
        "nk,ckb->cnb", sin_a[:half_a, :], imag_w, precision=TRIPLE
    )
    return out_half.reshape(out_half.shape[0], half_a * size_b) * (1.0 / (size_a * size_b))


def long_mix(gated_kv, spectrum, own_gain, tables):
    kv_values = gated_kv.astype(jnp.float32)
    real_u, imag_u = forward(kv_values, tables)
    real_h, imag_h = spectrum
    real_p = real_u * real_h - imag_u * imag_h
    imag_p = real_u * imag_h + imag_u * real_h
    convolved = inverse(real_p, imag_p, tables)
    return (convolved + own_gain[:, None] * kv_values).astype(jnp.bfloat16)


def featurize(extended, weights, length):
    tap_count = weights.shape[1]
    running = jnp.zeros(extended.shape[:1] + (length,) + extended.shape[2:], jnp.float32)
    for lag_idx in range(tap_count):
        offset = tap_count - 1 - lag_idx
        running = running + weights[:, lag_idx, None, :] * extended[
            :, offset : offset + length, :
        ].astype(jnp.float32)
    return running.astype(jnp.bfloat16)


def _feat_body(proj_ref, prior_ref, w_ref, q_ref, kv_ref, ext_ref):
    rows = proj_ref.shape[1]
    feats = []
    for a in range(3):
        ext_ref[0:2, :] = jnp.zeros((2, ext_ref.shape[1]), jnp.float32)
        ext_ref[2:8, :] = prior_ref[a].astype(jnp.float32)
        ext_ref[8 : 8 + rows, :] = proj_ref[a].astype(jnp.float32)
        acc = jnp.zeros((rows, ext_ref.shape[1]), jnp.float32)
        for j in range(KS):
            acc = acc + w_ref[a, j : j + 1, :] * ext_ref[8 - j : 8 - j + rows, :]
        feats.append(acc.astype(jnp.bfloat16))
    q_ref[...] = feats[0].astype(jnp.float32).T.astype(jnp.bfloat16)
    kv = feats[1].astype(jnp.float32) * feats[2].astype(jnp.float32)
    kv_ref[...] = kv.astype(jnp.bfloat16).astype(jnp.float32).T.astype(jnp.bfloat16)

def featurize_kv(projected, prior, weights, lane_block=128, interpret=False):
    _, rows, chans = projected.shape
    grid = (chans // lane_block,)
    return pl.pallas_call(
        _feat_body,
        grid=grid,
        in_specs=[
            pl.BlockSpec((3, rows, lane_block), lambda i: (0, 0, i)),
            pl.BlockSpec((3, KS - 1, lane_block), lambda i: (0, 0, i)),
            pl.BlockSpec((3, KS, lane_block), lambda i: (0, 0, i)),
        ],
        out_specs=[
            pl.BlockSpec((lane_block, rows), lambda i: (i, 0)),
            pl.BlockSpec((lane_block, rows), lambda i: (i, 0)),
        ],
        out_shape=[jax.ShapeDtypeStruct((chans, rows), jnp.bfloat16)] * 2,
        scratch_shapes=[pltpu.VMEM((rows + 8, lane_block), jnp.float32)],
        interpret=interpret,
    )(projected, prior, weights)


def _split(a):
    hi = a.astype(jnp.bfloat16)
    return hi, (a - hi.astype(jnp.float32)).astype(jnp.bfloat16)


def _mm(a, b):
    return jnp.dot(a, b, preferred_element_type=jnp.float32)


def _left3(t_hi, t_lo, v):
    v_hi, v_lo = _split(v)
    return _mm(t_hi, v_hi) + _mm(t_lo, v_hi) + _mm(t_hi, v_lo)


def _right3(v, t_hi, t_lo):
    v_hi, v_lo = _split(v)
    return _mm(v_hi, t_hi) + _mm(v_lo, t_hi) + _mm(v_hi, t_lo)


def _right2(v, t_hi, t_lo):
    v_hi = v.astype(jnp.bfloat16)
    return _mm(v_hi, t_hi) + _mm(v_hi, t_lo)


def _spectrum(a_re, a_im, ct, st, cbsb_h, cbsb_l):
    rows, width = ct.shape
    t_re = a_re * ct + a_im * st
    t_im = a_im * ct - a_re * st
    r = _right3(jnp.concatenate([t_re, t_im], axis=0), cbsb_h, cbsb_l)
    f_re = r[:rows, :width] + r[rows:, width:]
    f_im = r[rows:, :width] - r[:rows, width:]
    return f_re, f_im


def _filter_body(h_ref, casa_h, casa_l, cbsb_h, cbsb_l, ct_ref, st_ref, re_ref, im_ref):
    ct = ct_ref[...]
    st = st_ref[...]
    rows = ct.shape[0]
    for c in range(h_ref.shape[0]):
        a = _left3(casa_h[...], casa_l[...], h_ref[c])
        re_ref[c], im_ref[c] = _spectrum(a[:rows], -a[rows:], ct, st, cbsb_h[...], cbsb_l[...])


def _conv_body(x_ref, fh_re_ref, fh_im_ref, g_ref, casa_h, casa_l, cbsb_h, cbsb_l,
               ct_ref, st_ref, inv_h, inv_l, o_ref):
    ct = ct_ref[...]
    st = st_ref[...]
    rows, width = ct.shape
    chans = fh_re_ref.shape[0]
    x_b = jnp.concatenate([x_ref[:, c, :] for c in range(chans)], axis=1)
    a = _mm(casa_h[...], x_b) + _mm(casa_l[...], x_b)
    pieces = []
    for c in range(chans):
        a_re = a[:rows, c * width : (c + 1) * width]
        a_im = -a[rows:, c * width : (c + 1) * width]
        pieces.append(a_re * ct + a_im * st)
        pieces.append(a_im * ct - a_re * st)
    r = _right2(jnp.concatenate(pieces, axis=0), cbsb_h[...], cbsb_l[...])
    prods = []
    for c in range(chans):
        lo = 2 * rows * c
        f_re = r[lo : lo + rows, :width] + r[lo + rows : lo + 2 * rows, width:]
        f_im = r[lo + rows : lo + 2 * rows, :width] - r[lo : lo + rows, width:]
        fh_re = fh_re_ref[c]
        fh_im = fh_im_ref[c]
        prods.append(f_re * fh_re - f_im * fh_im)
        prods.append(f_re * fh_im + f_im * fh_re)
    q = _right2(jnp.concatenate(prods, axis=0), cbsb_h[...], cbsb_l[...])
    cols = []
    for c in range(chans):
        lo = 2 * rows * c
        z_re = q[lo : lo + rows, :width] - q[lo + rows : lo + 2 * rows, width:]
        z_im = q[lo + rows : lo + 2 * rows, :width] + q[lo : lo + rows, width:]
        w_re = z_re * ct - z_im * st
        w_im = z_im * ct + z_re * st
        cols.append(jnp.concatenate([w_re, w_im], axis=0))
    out = _left3(inv_h[...], inv_l[...], jnp.concatenate(cols, axis=1))
    res = (out * (1.0 / (rows * width)) + g_ref[...] * x_b.astype(jnp.float32)).astype(jnp.bfloat16)
    for c in range(chans):
        o_ref[:, c, :] = res[:, c * width : (c + 1) * width]


def conv_tables(size_a, size_b):
    whole = size_a * size_b
    half_a = size_a // 2

    def pair(r, c, period):
        ri = lax.broadcasted_iota(jnp.int32, (r, c), 0)
        ci = lax.broadcasted_iota(jnp.int32, (r, c), 1)
        ang = (ri * ci % period).astype(jnp.float32) * (2.0 * math.pi / period)
        return jnp.cos(ang), jnp.sin(ang)

    cos_a, sin_a = pair(size_a, half_a, size_a)
    cos_b, sin_b = pair(size_b, size_b, size_b)
    cos_t, sin_t = pair(size_a, size_b, whole)
    inv = jnp.concatenate([cos_a.T, -sin_a.T], axis=1)
    casa = jnp.concatenate([cos_a, sin_a], axis=0)
    cbsb = jnp.concatenate([cos_b, sin_b], axis=1)
    return (*_split(casa), *_split(cbsb), cos_t, sin_t, *_split(inv))


def filter_spectrum(filt, tabs, ch_block=2, size_b=256):
    ch, length = filt.shape
    half_a = length // size_b
    size_a = 2 * half_a
    h = filt.reshape(ch, half_a, size_b)
    full = lambda t: pl.BlockSpec(t.shape, lambda i: (0,) * t.ndim)
    blk_out = pl.BlockSpec((ch_block, size_a, size_b), lambda i: (i, 0, 0))
    return pl.pallas_call(
        _filter_body,
        grid=(ch // ch_block,),
        in_specs=[pl.BlockSpec((ch_block, half_a, size_b), lambda i: (i, 0, 0))]
        + [full(t) for t in tabs[:6]],
        out_specs=[blk_out, blk_out],
        out_shape=[jax.ShapeDtypeStruct((ch, size_a, size_b), jnp.float32)] * 2,
    )(h, *tabs[:6])


def long_conv(x, spectrum, gain, tabs):
    blocks, ch, size_b = x.shape
    g = jnp.repeat(gain, size_b)[None, :]
    casa_h, casa_l, cbsb_h, cbsb_l, cos_t, sin_t, inv_h, inv_l = tabs
    return pl.pallas_call(
        _conv_body,
        out_shape=jax.ShapeDtypeStruct((blocks, ch, size_b), jnp.bfloat16),
    )(x, *spectrum, g, casa_h, casa_l, cbsb_h, cbsb_l, cos_t, sin_t, inv_h, inv_l)


def _proj_body(f_ref, q_ref, w_ref, s_ref, o_ref, g_scr):
    @pl.when(pl.program_id(0) == 0)
    def _():
        gated = (q_ref[...].astype(jnp.float32) * f_ref[...].astype(jnp.float32)).astype(jnp.bfloat16)
        g_scr[...] = gated.astype(jnp.float32).T.astype(jnp.bfloat16)

    width = o_ref.shape[2]
    for p in range(o_ref.shape[0]):
        acc = None
        for b in range(w_ref.shape[0] // BLK):
            part = jnp.dot(g_scr[:, b * BLK : (b + 1) * BLK],
                           w_ref[b * BLK : (b + 1) * BLK, p * width : (p + 1) * width],
                           preferred_element_type=jnp.float32) * s_ref[b : b + 1, p * width : (p + 1) * width]
            acc = part if acc is None else acc + part
        o_ref[p] = acc.astype(jnp.bfloat16)


def project(filtered_home, q_cols, out_values, scale_cols, n_pieces, steps=2):
    chans, rows = filtered_home.shape
    width = out_values.shape[1] // n_pieces
    per_step = n_pieces // steps
    return pl.pallas_call(
        _proj_body,
        grid=(steps,),
        in_specs=[
            pl.BlockSpec((chans, rows), lambda j: (0, 0)),
            pl.BlockSpec((chans, rows), lambda j: (0, 0)),
            pl.BlockSpec((chans, width * per_step), lambda j: (0, j)),
            pl.BlockSpec((scale_cols.shape[0], width * per_step), lambda j: (0, j)),
        ],
        out_specs=pl.BlockSpec((per_step, rows, width), lambda j: (j, 0, 0)),
        out_shape=jax.ShapeDtypeStruct((n_pieces, rows, width), jnp.bfloat16),
        scratch_shapes=[pltpu.VMEM((rows, chans), jnp.bfloat16)],
    )(filtered_home, q_cols, out_values, scale_cols)


def multiply_round(left_arr, right_arr):
    return (left_arr.astype(jnp.float32) * right_arr.astype(jnp.float32)).astype(jnp.bfloat16)


def local(projected, feat_weight, long_filter, skip_gain, out_values, out_scales):
    groups = lax.axis_size("seq")
    tok_rows = projected.shape[1]
    local_ch = projected.shape[2]
    length = tok_rows * groups
    rim_width = KS - 1
    prior_rows = passed_along(projected[:, tok_rows - rim_width :, :], "seq", 1)
    q_feat, gated_kv = featurize_kv(projected, prior_rows, feat_weight)
    tabs = conv_tables(2 * length // 256, 256)
    spectrum = filter_spectrum(long_filter, tabs)
    kv_owned = lax.all_to_all(gated_kv.reshape(groups, -1, tok_rows), "seq", 0, 0, tiled=True)
    filtered = long_conv(kv_owned, spectrum, skip_gain, tabs)
    filtered_home = lax.all_to_all(filtered, "seq", 0, 0, tiled=True).reshape(local_ch, tok_rows)
    n_tensor = lax.axis_size("tensor")
    scale_cols = jnp.repeat(out_scales, BLK, axis=1)
    pieces = project(filtered_home, q_feat, out_values, scale_cols, n_tensor)
    gathered = lax.all_to_all(pieces, "tensor", 0, 0, tiled=True)
    return jnp.sum(gathered.astype(jnp.float32), axis=0).astype(jnp.bfloat16)


def solution(mesh):
    return jax.shard_map(
        local,
        mesh=mesh,
        in_specs=(
            P(None, "seq", "tensor"),
            P(None, None, "tensor"),
            P(("tensor", "seq"), None),
            P(("tensor", "seq")),
            P("tensor", None),
            P("tensor", None),
        ),
        out_specs=P("seq", "tensor"),
        check_vma=False,
    )
```

```python
import math

import jax
import jax.numpy as jnp
from jax import lax
from jax.sharding import PartitionSpec as P
from jax.experimental import pallas as pl
from jax.experimental.pallas import tpu as pltpu

KS = 7
BLK = 128


TRIPLE = lax.Precision.HIGH


def passed_along(x, axis, by):
    size = lax.axis_size(axis)
    pairs = [(i, i + by) for i in range(size) if 0 <= i + by < size]
    return lax.ppermute(x, axis, pairs)


def split_length(whole):
    for candidate in range(2, whole + 1, 2):
        if whole % candidate == 0 and candidate * candidate >= whole:
            return (candidate, whole // candidate)
    return (whole, 1)


def angle_pair(row_count, col_count, period):
    row_ids = lax.broadcasted_iota(jnp.int32, (row_count, col_count), 0)
    col_ids = lax.broadcasted_iota(jnp.int32, (row_count, col_count), 1)
    angles = (row_ids * col_ids % period).astype(jnp.float32) * (2.0 * math.pi / period)
    return (jnp.cos(angles), jnp.sin(angles))


def make_tables(length):
    whole = 2 * length
    size_a, size_b = split_length(whole)
    return (
        angle_pair(size_a, size_a, size_a),
        angle_pair(size_b, size_b, size_b),
        angle_pair(size_a, size_b, whole),
        size_a,
        size_b,
    )


def right_mul(signal, matrix):
    return jnp.einsum("ckn,nm->ckm", signal, matrix, precision=TRIPLE)


def forward(signal, tables):
    (cos_a, sin_a), (cos_b, sin_b), (cos_t, sin_t), size_a, size_b = tables
    half_a = size_a // 2
    blocks = signal.reshape(signal.shape[0], half_a, size_b)
    real_a = jnp.einsum("kn,cnb->ckb", cos_a[:, :half_a], blocks, precision=TRIPLE)
    imag_a = -jnp.einsum("kn,cnb->ckb", sin_a[:, :half_a], blocks, precision=TRIPLE)
    real_t = real_a * cos_t + imag_a * sin_t
    imag_t = imag_a * cos_t - real_a * sin_t
    real_f = right_mul(real_t, cos_b) + right_mul(imag_t, sin_b)
    imag_f = right_mul(imag_t, cos_b) - right_mul(real_t, sin_b)
    return (real_f, imag_f)


def inverse(real_f, imag_f, tables):
    (cos_a, sin_a), (cos_b, sin_b), (cos_t, sin_t), size_a, size_b = tables
    half_a = size_a // 2
    real_z = right_mul(real_f, cos_b) - right_mul(imag_f, sin_b)
    imag_z = right_mul(imag_f, cos_b) + right_mul(real_f, sin_b)
    real_w = real_z * cos_t - imag_z * sin_t
    imag_w = imag_z * cos_t + real_z * sin_t
    out_half = jnp.einsum("nk,ckb->cnb", cos_a[:half_a, :], real_w, precision=TRIPLE) - jnp.einsum(
        "nk,ckb->cnb", sin_a[:half_a, :], imag_w, precision=TRIPLE
    )
    return out_half.reshape(out_half.shape[0], half_a * size_b) * (1.0 / (size_a * size_b))


def long_mix(gated_kv, spectrum, own_gain, tables):
    kv_values = gated_kv.astype(jnp.float32)
    real_u, imag_u = forward(kv_values, tables)
    real_h, imag_h = spectrum
    real_p = real_u * real_h - imag_u * imag_h
    imag_p = real_u * imag_h + imag_u * real_h
    convolved = inverse(real_p, imag_p, tables)
    return (convolved + own_gain[:, None] * kv_values).astype(jnp.bfloat16)


def featurize(extended, weights, length):
    tap_count = weights.shape[1]
    running = jnp.zeros(extended.shape[:1] + (length,) + extended.shape[2:], jnp.float32)
    for lag_idx in range(tap_count):
        offset = tap_count - 1 - lag_idx
        running = running + weights[:, lag_idx, None, :] * extended[
            :, offset : offset + length, :
        ].astype(jnp.float32)
    return running.astype(jnp.bfloat16)


def _feat_body(proj_ref, prior_ref, w_ref, q_ref, kv_ref, ext_ref):
    rows = proj_ref.shape[1]
    feats = []
    for a in range(3):
        ext_ref[0:2, :] = jnp.zeros((2, ext_ref.shape[1]), jnp.float32)
        ext_ref[2:8, :] = prior_ref[a].astype(jnp.float32)
        ext_ref[8 : 8 + rows, :] = proj_ref[a].astype(jnp.float32)
        acc = jnp.zeros((rows, ext_ref.shape[1]), jnp.float32)
        for j in range(KS):
            acc = acc + w_ref[a, j : j + 1, :] * ext_ref[8 - j : 8 - j + rows, :]
        feats.append(acc.astype(jnp.bfloat16))
    q_ref[...] = feats[0].astype(jnp.float32).T.astype(jnp.bfloat16)
    kv = feats[1].astype(jnp.float32) * feats[2].astype(jnp.float32)
    kv_ref[...] = kv.astype(jnp.bfloat16).astype(jnp.float32).T.astype(jnp.bfloat16)

def featurize_kv(projected, prior, weights, lane_block=128, interpret=False):
    _, rows, chans = projected.shape
    grid = (chans // lane_block,)
    return pl.pallas_call(
        _feat_body,
        grid=grid,
        in_specs=[
            pl.BlockSpec((3, rows, lane_block), lambda i: (0, 0, i)),
            pl.BlockSpec((3, KS - 1, lane_block), lambda i: (0, 0, i)),
            pl.BlockSpec((3, KS, lane_block), lambda i: (0, 0, i)),
        ],
        out_specs=[
            pl.BlockSpec((lane_block, rows), lambda i: (i, 0)),
            pl.BlockSpec((lane_block, rows), lambda i: (i, 0)),
        ],
        out_shape=[jax.ShapeDtypeStruct((chans, rows), jnp.bfloat16)] * 2,
        scratch_shapes=[pltpu.VMEM((rows + 8, lane_block), jnp.float32)],
        interpret=interpret,
    )(projected, prior, weights)


def _split(a):
    hi = a.astype(jnp.bfloat16)
    return hi, (a - hi.astype(jnp.float32)).astype(jnp.bfloat16)


def _mm(a, b):
    return jnp.dot(a, b, preferred_element_type=jnp.float32)


def _left3(t_hi, t_lo, v):
    v_hi, v_lo = _split(v)
    return _mm(t_hi, v_hi) + _mm(t_lo, v_hi) + _mm(t_hi, v_lo)


def _right3(v, t_hi, t_lo):
    v_hi, v_lo = _split(v)
    return _mm(v_hi, t_hi) + _mm(v_lo, t_hi) + _mm(v_hi, t_lo)


def _right2(v, t_hi, t_lo):
    v_hi = v.astype(jnp.bfloat16)
    return _mm(v_hi, t_hi) + _mm(v_hi, t_lo)


def _spectrum(a_re, a_im, ct, st, cbsb_h, cbsb_l):
    rows, width = ct.shape
    t_re = a_re * ct + a_im * st
    t_im = a_im * ct - a_re * st
    r = _right3(jnp.concatenate([t_re, t_im], axis=0), cbsb_h, cbsb_l)
    f_re = r[:rows, :width] + r[rows:, width:]
    f_im = r[rows:, :width] - r[:rows, width:]
    return f_re, f_im


def _filter_body(h_ref, casa_h, casa_l, cbsb_h, cbsb_l, ct_ref, st_ref, re_ref, im_ref):
    ct = ct_ref[...]
    st = st_ref[...]
    rows = ct.shape[0]
    for c in range(h_ref.shape[0]):
        a = _left3(casa_h[...], casa_l[...], h_ref[c])
        re_ref[c], im_ref[c] = _spectrum(a[:rows], -a[rows:], ct, st, cbsb_h[...], cbsb_l[...])


def _conv_body(x_ref, fh_re_ref, fh_im_ref, g_ref, casa_h, casa_l, cbsb_h, cbsb_l,
               ct_ref, st_ref, inv_h, inv_l, o_ref):
    ct = ct_ref[...]
    st = st_ref[...]
    rows, width = ct.shape
    chans = fh_re_ref.shape[0]
    x_b = jnp.concatenate([x_ref[:, c, :] for c in range(chans)], axis=1)
    a = _mm(casa_h[...], x_b) + _mm(casa_l[...], x_b)
    pieces = []
    for c in range(chans):
        a_re = a[:rows, c * width : (c + 1) * width]
        a_im = -a[rows:, c * width : (c + 1) * width]
        pieces.append(a_re * ct + a_im * st)
        pieces.append(a_im * ct - a_re * st)
    r = _right2(jnp.concatenate(pieces, axis=0), cbsb_h[...], cbsb_l[...])
    prods = []
    for c in range(chans):
        lo = 2 * rows * c
        f_re = r[lo : lo + rows, :width] + r[lo + rows : lo + 2 * rows, width:]
        f_im = r[lo + rows : lo + 2 * rows, :width] - r[lo : lo + rows, width:]
        fh_re = fh_re_ref[c]
        fh_im = fh_im_ref[c]
        prods.append(f_re * fh_re - f_im * fh_im)
        prods.append(f_re * fh_im + f_im * fh_re)
    q = _right2(jnp.concatenate(prods, axis=0), cbsb_h[...], cbsb_l[...])
    cols = []
    for c in range(chans):
        lo = 2 * rows * c
        z_re = q[lo : lo + rows, :width] - q[lo + rows : lo + 2 * rows, width:]
        z_im = q[lo + rows : lo + 2 * rows, :width] + q[lo : lo + rows, width:]
        w_re = z_re * ct - z_im * st
        w_im = z_im * ct + z_re * st
        cols.append(jnp.concatenate([w_re, w_im], axis=0))
    out = _left3(inv_h[...], inv_l[...], jnp.concatenate(cols, axis=1))
    res = (out * (1.0 / (rows * width)) + g_ref[...] * x_b.astype(jnp.float32)).astype(jnp.bfloat16)
    for c in range(chans):
        o_ref[:, c, :] = res[:, c * width : (c + 1) * width]


def conv_tables(size_a, size_b):
    whole = size_a * size_b
    half_a = size_a // 2

    def pair(r, c, period):
        ri = lax.broadcasted_iota(jnp.int32, (r, c), 0)
        ci = lax.broadcasted_iota(jnp.int32, (r, c), 1)
        ang = (ri * ci % period).astype(jnp.float32) * (2.0 * math.pi / period)
        return jnp.cos(ang), jnp.sin(ang)

    cos_a, sin_a = pair(size_a, half_a, size_a)
    cos_b, sin_b = pair(size_b, size_b, size_b)
    cos_t, sin_t = pair(size_a, size_b, whole)
    inv = jnp.concatenate([cos_a.T, -sin_a.T], axis=1)
    casa = jnp.concatenate([cos_a, sin_a], axis=0)
    cbsb = jnp.concatenate([cos_b, sin_b], axis=1)
    return (*_split(casa), *_split(cbsb), cos_t, sin_t, *_split(inv))


def filter_spectrum(filt, tabs, ch_block=2, size_b=256):
    ch, length = filt.shape
    half_a = length // size_b
    size_a = 2 * half_a
    h = filt.reshape(ch, half_a, size_b)
    full = lambda t: pl.BlockSpec(t.shape, lambda i: (0,) * t.ndim)
    blk_out = pl.BlockSpec((ch_block, size_a, size_b), lambda i: (i, 0, 0))
    return pl.pallas_call(
        _filter_body,
        grid=(ch // ch_block,),
        in_specs=[pl.BlockSpec((ch_block, half_a, size_b), lambda i: (i, 0, 0))]
        + [full(t) for t in tabs[:6]],
        out_specs=[blk_out, blk_out],
        out_shape=[jax.ShapeDtypeStruct((ch, size_a, size_b), jnp.float32)] * 2,
    )(h, *tabs[:6])


def long_conv(x, spectrum, gain, tabs):
    blocks, ch, size_b = x.shape
    g = jnp.repeat(gain, size_b)[None, :]
    casa_h, casa_l, cbsb_h, cbsb_l, cos_t, sin_t, inv_h, inv_l = tabs
    return pl.pallas_call(
        _conv_body,
        out_shape=jax.ShapeDtypeStruct((blocks, ch, size_b), jnp.bfloat16),
    )(x, *spectrum, g, casa_h, casa_l, cbsb_h, cbsb_l, cos_t, sin_t, inv_h, inv_l)


def _proj_body(f_ref, q_ref, w_ref, s_ref, o_ref, g_scr):
    @pl.when(pl.program_id(0) == 0)
    def _():
        gated = (q_ref[...].astype(jnp.float32) * f_ref[...].astype(jnp.float32)).astype(jnp.bfloat16)
        g_scr[...] = gated.astype(jnp.float32).T.astype(jnp.bfloat16)

    width = o_ref.shape[2]
    for p in range(o_ref.shape[0]):
        acc = None
        for b in range(w_ref.shape[0] // BLK):
            part = jnp.dot(g_scr[:, b * BLK : (b + 1) * BLK],
                           w_ref[b * BLK : (b + 1) * BLK, p * width : (p + 1) * width],
                           preferred_element_type=jnp.float32) * s_ref[b : b + 1, p * width : (p + 1) * width]
            acc = part if acc is None else acc + part
        o_ref[p] = acc.astype(jnp.bfloat16)


def project(filtered_home, q_cols, out_values, scale_cols, n_pieces, steps=2):
    chans, rows = filtered_home.shape
    width = out_values.shape[1] // n_pieces
    per_step = n_pieces // steps
    return pl.pallas_call(
        _proj_body,
        grid=(steps,),
        in_specs=[
            pl.BlockSpec((chans, rows), lambda j: (0, 0)),
            pl.BlockSpec((chans, rows), lambda j: (0, 0)),
            pl.BlockSpec((chans, width * per_step), lambda j: (0, j)),
            pl.BlockSpec((scale_cols.shape[0], width * per_step), lambda j: (0, j)),
        ],
        out_specs=pl.BlockSpec((per_step, rows, width), lambda j: (j, 0, 0)),
        out_shape=jax.ShapeDtypeStruct((n_pieces, rows, width), jnp.bfloat16),
        scratch_shapes=[pltpu.VMEM((rows, chans), jnp.bfloat16)],
    )(filtered_home, q_cols, out_values, scale_cols)


def multiply_round(left_arr, right_arr):
    return (left_arr.astype(jnp.float32) * right_arr.astype(jnp.float32)).astype(jnp.bfloat16)


def local(projected, feat_weight, long_filter, skip_gain, out_values, out_scales):
    groups = lax.axis_size("seq")
    tok_rows = projected.shape[1]
    local_ch = projected.shape[2]
    length = tok_rows * groups
    rim_width = KS - 1
    prior_rows = passed_along(projected[:, tok_rows - rim_width :, :], "seq", 1)
    q_feat, gated_kv = featurize_kv(projected, prior_rows, feat_weight)
    gated_kv, long_filter, skip_gain = lax.optimization_barrier((gated_kv, long_filter, skip_gain))
    tabs = conv_tables(2 * length // 256, 256)
    spectrum = filter_spectrum(long_filter, tabs)
    kv_owned = lax.all_to_all(gated_kv.reshape(groups, -1, tok_rows), "seq", 0, 0, tiled=True)
    filtered = long_conv(kv_owned, spectrum, skip_gain, tabs)
    filtered_home = lax.all_to_all(filtered, "seq", 0, 0, tiled=True).reshape(local_ch, tok_rows)
    n_tensor = lax.axis_size("tensor")
    scale_cols = jnp.repeat(out_scales, BLK, axis=1)
    pieces = project(filtered_home, q_feat, out_values, scale_cols, n_tensor)
    gathered = lax.all_to_all(pieces, "tensor", 0, 0, tiled=True)
    return jnp.sum(gathered.astype(jnp.float32), axis=0).astype(jnp.bfloat16)


def solution(mesh):
    return jax.shard_map(
        local,
        mesh=mesh,
        in_specs=(
            P(None, "seq", "tensor"),
            P(None, None, "tensor"),
            P(("tensor", "seq"), None),
            P(("tensor", "seq")),
            P("tensor", None),
            P("tensor", None),
        ),
        out_specs=P("seq", "tensor"),
        check_vma=False,
    )
```

```python
import math

import jax
import jax.numpy as jnp
from jax import lax
from jax.sharding import PartitionSpec as P
from jax.experimental import pallas as pl
from jax.experimental.pallas import tpu as pltpu

KS = 7
BLK = 128


TRIPLE = lax.Precision.HIGH


def passed_along(x, axis, by):
    size = lax.axis_size(axis)
    pairs = [(i, i + by) for i in range(size) if 0 <= i + by < size]
    return lax.ppermute(x, axis, pairs)


def split_length(whole):
    for candidate in range(2, whole + 1, 2):
        if whole % candidate == 0 and candidate * candidate >= whole:
            return (candidate, whole // candidate)
    return (whole, 1)


def angle_pair(row_count, col_count, period):
    row_ids = lax.broadcasted_iota(jnp.int32, (row_count, col_count), 0)
    col_ids = lax.broadcasted_iota(jnp.int32, (row_count, col_count), 1)
    angles = (row_ids * col_ids % period).astype(jnp.float32) * (2.0 * math.pi / period)
    return (jnp.cos(angles), jnp.sin(angles))


def make_tables(length):
    whole = 2 * length
    size_a, size_b = split_length(whole)
    return (
        angle_pair(size_a, size_a, size_a),
        angle_pair(size_b, size_b, size_b),
        angle_pair(size_a, size_b, whole),
        size_a,
        size_b,
    )


def right_mul(signal, matrix):
    return jnp.einsum("ckn,nm->ckm", signal, matrix, precision=TRIPLE)


def forward(signal, tables):
    (cos_a, sin_a), (cos_b, sin_b), (cos_t, sin_t), size_a, size_b = tables
    half_a = size_a // 2
    blocks = signal.reshape(signal.shape[0], half_a, size_b)
    real_a = jnp.einsum("kn,cnb->ckb", cos_a[:, :half_a], blocks, precision=TRIPLE)
    imag_a = -jnp.einsum("kn,cnb->ckb", sin_a[:, :half_a], blocks, precision=TRIPLE)
    real_t = real_a * cos_t + imag_a * sin_t
    imag_t = imag_a * cos_t - real_a * sin_t
    real_f = right_mul(real_t, cos_b) + right_mul(imag_t, sin_b)
    imag_f = right_mul(imag_t, cos_b) - right_mul(real_t, sin_b)
    return (real_f, imag_f)


def inverse(real_f, imag_f, tables):
    (cos_a, sin_a), (cos_b, sin_b), (cos_t, sin_t), size_a, size_b = tables
    half_a = size_a // 2
    real_z = right_mul(real_f, cos_b) - right_mul(imag_f, sin_b)
    imag_z = right_mul(imag_f, cos_b) + right_mul(real_f, sin_b)
    real_w = real_z * cos_t - imag_z * sin_t
    imag_w = imag_z * cos_t + real_z * sin_t
    out_half = jnp.einsum("nk,ckb->cnb", cos_a[:half_a, :], real_w, precision=TRIPLE) - jnp.einsum(
        "nk,ckb->cnb", sin_a[:half_a, :], imag_w, precision=TRIPLE
    )
    return out_half.reshape(out_half.shape[0], half_a * size_b) * (1.0 / (size_a * size_b))


def long_mix(gated_kv, spectrum, own_gain, tables):
    kv_values = gated_kv.astype(jnp.float32)
    real_u, imag_u = forward(kv_values, tables)
    real_h, imag_h = spectrum
    real_p = real_u * real_h - imag_u * imag_h
    imag_p = real_u * imag_h + imag_u * real_h
    convolved = inverse(real_p, imag_p, tables)
    return (convolved + own_gain[:, None] * kv_values).astype(jnp.bfloat16)


def featurize(extended, weights, length):
    tap_count = weights.shape[1]
    running = jnp.zeros(extended.shape[:1] + (length,) + extended.shape[2:], jnp.float32)
    for lag_idx in range(tap_count):
        offset = tap_count - 1 - lag_idx
        running = running + weights[:, lag_idx, None, :] * extended[
            :, offset : offset + length, :
        ].astype(jnp.float32)
    return running.astype(jnp.bfloat16)


def _feat_body(proj_ref, prior_ref, w_ref, q_ref, kv_ref, ext_ref):
    rows = proj_ref.shape[1]
    feats = []
    for a in range(3):
        ext_ref[0:2, :] = jnp.zeros((2, ext_ref.shape[1]), jnp.float32)
        ext_ref[2:8, :] = prior_ref[a].astype(jnp.float32)
        ext_ref[8 : 8 + rows, :] = proj_ref[a].astype(jnp.float32)
        acc = jnp.zeros((rows, ext_ref.shape[1]), jnp.float32)
        for j in range(KS):
            acc = acc + w_ref[a, j : j + 1, :] * ext_ref[8 - j : 8 - j + rows, :]
        feats.append(acc.astype(jnp.bfloat16))
    q_ref[...] = feats[0].astype(jnp.float32).T.astype(jnp.bfloat16)
    kv = feats[1].astype(jnp.float32) * feats[2].astype(jnp.float32)
    kv_ref[...] = kv.astype(jnp.bfloat16).astype(jnp.float32).T.astype(jnp.bfloat16)

def featurize_kv(projected, prior, weights, lane_block=128, interpret=False):
    _, rows, chans = projected.shape
    grid = (chans // lane_block,)
    return pl.pallas_call(
        _feat_body,
        grid=grid,
        in_specs=[
            pl.BlockSpec((3, rows, lane_block), lambda i: (0, 0, i)),
            pl.BlockSpec((3, KS - 1, lane_block), lambda i: (0, 0, i)),
            pl.BlockSpec((3, KS, lane_block), lambda i: (0, 0, i)),
        ],
        out_specs=[
            pl.BlockSpec((lane_block, rows), lambda i: (i, 0)),
            pl.BlockSpec((lane_block, rows), lambda i: (i, 0)),
        ],
        out_shape=[jax.ShapeDtypeStruct((chans, rows), jnp.bfloat16)] * 2,
        scratch_shapes=[pltpu.VMEM((rows + 8, lane_block), jnp.float32)],
        interpret=interpret,
    )(projected, prior, weights)


def _split(a):
    hi = a.astype(jnp.bfloat16)
    return hi, (a - hi.astype(jnp.float32)).astype(jnp.bfloat16)


def _mm(a, b):
    return jnp.dot(a, b, preferred_element_type=jnp.float32)


def _left3(t_hi, t_lo, v):
    v_hi, v_lo = _split(v)
    return _mm(t_hi, v_hi) + _mm(t_lo, v_hi) + _mm(t_hi, v_lo)


def _right3(v, t_hi, t_lo):
    v_hi, v_lo = _split(v)
    return _mm(v_hi, t_hi) + _mm(v_lo, t_hi) + _mm(v_hi, t_lo)


def _left2(t_hi, t_lo, v):
    v_hi = v.astype(jnp.bfloat16)
    return _mm(t_hi, v_hi) + _mm(t_lo, v_hi)


def _right2(v, t_hi, t_lo):
    v_hi = v.astype(jnp.bfloat16)
    return _mm(v_hi, t_hi) + _mm(v_hi, t_lo)


def _spectrum(a_re, a_im, ct, st, cbsb_h, cbsb_l):
    rows, width = ct.shape
    t_re = a_re * ct + a_im * st
    t_im = a_im * ct - a_re * st
    r = _right3(jnp.concatenate([t_re, t_im], axis=0), cbsb_h, cbsb_l)
    f_re = r[:rows, :width] + r[rows:, width:]
    f_im = r[rows:, :width] - r[:rows, width:]
    return f_re, f_im


def _filter_body(h_ref, casa_h, casa_l, cbsb_h, cbsb_l, ct_ref, st_ref, re_ref, im_ref):
    ct = ct_ref[...]
    st = st_ref[...]
    rows = ct.shape[0]
    for c in range(h_ref.shape[0]):
        a = _left3(casa_h[...], casa_l[...], h_ref[c])
        re_ref[c], im_ref[c] = _spectrum(a[:rows], -a[rows:], ct, st, cbsb_h[...], cbsb_l[...])


def _conv_body(x_ref, fh_re_ref, fh_im_ref, g_ref, casa_h, casa_l, cbsb_h, cbsb_l,
               ct_ref, st_ref, inv_h, inv_l, o_ref):
    ct = ct_ref[...]
    st = st_ref[...]
    rows, width = ct.shape
    chans = fh_re_ref.shape[0]
    x_b = jnp.concatenate([x_ref[:, c, :] for c in range(chans)], axis=1)
    a = _mm(casa_h[...], x_b) + _mm(casa_l[...], x_b)
    pieces = []
    for c in range(chans):
        a_re = a[:rows, c * width : (c + 1) * width]
        a_im = -a[rows:, c * width : (c + 1) * width]
        pieces.append(a_re * ct + a_im * st)
        pieces.append(a_im * ct - a_re * st)
    r = _right2(jnp.concatenate(pieces, axis=0), cbsb_h[...], cbsb_l[...])
    prods = []
    for c in range(chans):
        lo = 2 * rows * c
        f_re = r[lo : lo + rows, :width] + r[lo + rows : lo + 2 * rows, width:]
        f_im = r[lo + rows : lo + 2 * rows, :width] - r[lo : lo + rows, width:]
        fh_re = fh_re_ref[c]
        fh_im = fh_im_ref[c]
        prods.append(f_re * fh_re - f_im * fh_im)
        prods.append(f_re * fh_im + f_im * fh_re)
    q = _right2(jnp.concatenate(prods, axis=0), cbsb_h[...], cbsb_l[...])
    cols = []
    for c in range(chans):
        lo = 2 * rows * c
        z_re = q[lo : lo + rows, :width] - q[lo + rows : lo + 2 * rows, width:]
        z_im = q[lo + rows : lo + 2 * rows, :width] + q[lo : lo + rows, width:]
        w_re = z_re * ct - z_im * st
        w_im = z_im * ct + z_re * st
        cols.append(jnp.concatenate([w_re, w_im], axis=0))
    out = _left2(inv_h[...], inv_l[...], jnp.concatenate(cols, axis=1))
    res = (out * (1.0 / (rows * width)) + g_ref[...] * x_b.astype(jnp.float32)).astype(jnp.bfloat16)
    for c in range(chans):
        o_ref[:, c, :] = res[:, c * width : (c + 1) * width]


def conv_tables(size_a, size_b):
    whole = size_a * size_b
    half_a = size_a // 2

    def pair(r, c, period):
        ri = lax.broadcasted_iota(jnp.int32, (r, c), 0)
        ci = lax.broadcasted_iota(jnp.int32, (r, c), 1)
        ang = (ri * ci % period).astype(jnp.float32) * (2.0 * math.pi / period)
        return jnp.cos(ang), jnp.sin(ang)

    cos_a, sin_a = pair(size_a, half_a, size_a)
    cos_b, sin_b = pair(size_b, size_b, size_b)
    cos_t, sin_t = pair(size_a, size_b, whole)
    inv = jnp.concatenate([cos_a.T, -sin_a.T], axis=1)
    casa = jnp.concatenate([cos_a, sin_a], axis=0)
    cbsb = jnp.concatenate([cos_b, sin_b], axis=1)
    return (*_split(casa), *_split(cbsb), cos_t, sin_t, *_split(inv))


def filter_spectrum(filt, tabs, ch_block=2, size_b=256):
    ch, length = filt.shape
    half_a = length // size_b
    size_a = 2 * half_a
    h = filt.reshape(ch, half_a, size_b)
    full = lambda t: pl.BlockSpec(t.shape, lambda i: (0,) * t.ndim)
    blk_out = pl.BlockSpec((ch_block, size_a, size_b), lambda i: (i, 0, 0))
    return pl.pallas_call(
        _filter_body,
        grid=(ch // ch_block,),
        in_specs=[pl.BlockSpec((ch_block, half_a, size_b), lambda i: (i, 0, 0))]
        + [full(t) for t in tabs[:6]],
        out_specs=[blk_out, blk_out],
        out_shape=[jax.ShapeDtypeStruct((ch, size_a, size_b), jnp.float32)] * 2,
    )(h, *tabs[:6])


def long_conv(x, spectrum, gain, tabs):
    blocks, ch, size_b = x.shape
    g = jnp.repeat(gain, size_b)[None, :]
    casa_h, casa_l, cbsb_h, cbsb_l, cos_t, sin_t, inv_h, inv_l = tabs
    return pl.pallas_call(
        _conv_body,
        out_shape=jax.ShapeDtypeStruct((blocks, ch, size_b), jnp.bfloat16),
    )(x, *spectrum, g, casa_h, casa_l, cbsb_h, cbsb_l, cos_t, sin_t, inv_h, inv_l)


def _proj_body(f_ref, q_ref, w_ref, s_ref, o_ref, g_scr):
    @pl.when(pl.program_id(0) == 0)
    def _():
        gated = (q_ref[...].astype(jnp.float32) * f_ref[...].astype(jnp.float32)).astype(jnp.bfloat16)
        g_scr[...] = gated.astype(jnp.float32).T.astype(jnp.bfloat16)

    width = o_ref.shape[2]
    for p in range(o_ref.shape[0]):
        acc = None
        for b in range(w_ref.shape[0] // BLK):
            part = jnp.dot(g_scr[:, b * BLK : (b + 1) * BLK],
                           w_ref[b * BLK : (b + 1) * BLK, p * width : (p + 1) * width],
                           preferred_element_type=jnp.float32) * s_ref[b : b + 1, p * width : (p + 1) * width]
            acc = part if acc is None else acc + part
        o_ref[p] = acc.astype(jnp.bfloat16)


def project(filtered_home, q_cols, out_values, scale_cols, n_pieces, steps=2):
    chans, rows = filtered_home.shape
    width = out_values.shape[1] // n_pieces
    per_step = n_pieces // steps
    return pl.pallas_call(
        _proj_body,
        grid=(steps,),
        in_specs=[
            pl.BlockSpec((chans, rows), lambda j: (0, 0)),
            pl.BlockSpec((chans, rows), lambda j: (0, 0)),
            pl.BlockSpec((chans, width * per_step), lambda j: (0, j)),
            pl.BlockSpec((scale_cols.shape[0], width * per_step), lambda j: (0, j)),
        ],
        out_specs=pl.BlockSpec((per_step, rows, width), lambda j: (j, 0, 0)),
        out_shape=jax.ShapeDtypeStruct((n_pieces, rows, width), jnp.bfloat16),
        scratch_shapes=[pltpu.VMEM((rows, chans), jnp.bfloat16)],
    )(filtered_home, q_cols, out_values, scale_cols)


def multiply_round(left_arr, right_arr):
    return (left_arr.astype(jnp.float32) * right_arr.astype(jnp.float32)).astype(jnp.bfloat16)


def local(projected, feat_weight, long_filter, skip_gain, out_values, out_scales):
    groups = lax.axis_size("seq")
    tok_rows = projected.shape[1]
    local_ch = projected.shape[2]
    length = tok_rows * groups
    rim_width = KS - 1
    prior_rows = passed_along(projected[:, tok_rows - rim_width :, :], "seq", 1)
    q_feat, gated_kv = featurize_kv(projected, prior_rows, feat_weight)
    tabs = conv_tables(2 * length // 256, 256)
    spectrum = filter_spectrum(long_filter, tabs)
    kv_owned = lax.all_to_all(gated_kv.reshape(groups, -1, tok_rows), "seq", 0, 0, tiled=True)
    filtered = long_conv(kv_owned, spectrum, skip_gain, tabs)
    filtered_home = lax.all_to_all(filtered, "seq", 0, 0, tiled=True).reshape(local_ch, tok_rows)
    n_tensor = lax.axis_size("tensor")
    scale_cols = jnp.repeat(out_scales, BLK, axis=1)
    pieces = project(filtered_home, q_feat, out_values, scale_cols, n_tensor)
    gathered = lax.all_to_all(pieces, "tensor", 0, 0, tiled=True)
    return jnp.sum(gathered.astype(jnp.float32), axis=0).astype(jnp.bfloat16)


def solution(mesh):
    return jax.shard_map(
        local,
        mesh=mesh,
        in_specs=(
            P(None, "seq", "tensor"),
            P(None, None, "tensor"),
            P(("tensor", "seq"), None),
            P(("tensor", "seq")),
            P("tensor", None),
            P("tensor", None),
        ),
        out_specs=P("seq", "tensor"),
        check_vma=False,
    )
```

```python
import math

import jax
import jax.numpy as jnp
from jax import lax
from jax.sharding import PartitionSpec as P
from jax.experimental import pallas as pl
from jax.experimental.pallas import tpu as pltpu

KS = 7
BLK = 128


TRIPLE = lax.Precision.HIGH


def passed_along(x, axis, by):
    size = lax.axis_size(axis)
    pairs = [(i, i + by) for i in range(size) if 0 <= i + by < size]
    return lax.ppermute(x, axis, pairs)


def split_length(whole):
    for candidate in range(2, whole + 1, 2):
        if whole % candidate == 0 and candidate * candidate >= whole:
            return (candidate, whole // candidate)
    return (whole, 1)


def angle_pair(row_count, col_count, period):
    row_ids = lax.broadcasted_iota(jnp.int32, (row_count, col_count), 0)
    col_ids = lax.broadcasted_iota(jnp.int32, (row_count, col_count), 1)
    angles = (row_ids * col_ids % period).astype(jnp.float32) * (2.0 * math.pi / period)
    return (jnp.cos(angles), jnp.sin(angles))


def make_tables(length):
    whole = 2 * length
    size_a, size_b = split_length(whole)
    return (
        angle_pair(size_a, size_a, size_a),
        angle_pair(size_b, size_b, size_b),
        angle_pair(size_a, size_b, whole),
        size_a,
        size_b,
    )


def right_mul(signal, matrix):
    return jnp.einsum("ckn,nm->ckm", signal, matrix, precision=TRIPLE)


def forward(signal, tables):
    (cos_a, sin_a), (cos_b, sin_b), (cos_t, sin_t), size_a, size_b = tables
    half_a = size_a // 2
    blocks = signal.reshape(signal.shape[0], half_a, size_b)
    real_a = jnp.einsum("kn,cnb->ckb", cos_a[:, :half_a], blocks, precision=TRIPLE)
    imag_a = -jnp.einsum("kn,cnb->ckb", sin_a[:, :half_a], blocks, precision=TRIPLE)
    real_t = real_a * cos_t + imag_a * sin_t
    imag_t = imag_a * cos_t - real_a * sin_t
    real_f = right_mul(real_t, cos_b) + right_mul(imag_t, sin_b)
    imag_f = right_mul(imag_t, cos_b) - right_mul(real_t, sin_b)
    return (real_f, imag_f)


def inverse(real_f, imag_f, tables):
    (cos_a, sin_a), (cos_b, sin_b), (cos_t, sin_t), size_a, size_b = tables
    half_a = size_a // 2
    real_z = right_mul(real_f, cos_b) - right_mul(imag_f, sin_b)
    imag_z = right_mul(imag_f, cos_b) + right_mul(real_f, sin_b)
    real_w = real_z * cos_t - imag_z * sin_t
    imag_w = imag_z * cos_t + real_z * sin_t
    out_half = jnp.einsum("nk,ckb->cnb", cos_a[:half_a, :], real_w, precision=TRIPLE) - jnp.einsum(
        "nk,ckb->cnb", sin_a[:half_a, :], imag_w, precision=TRIPLE
    )
    return out_half.reshape(out_half.shape[0], half_a * size_b) * (1.0 / (size_a * size_b))


def long_mix(gated_kv, spectrum, own_gain, tables):
    kv_values = gated_kv.astype(jnp.float32)
    real_u, imag_u = forward(kv_values, tables)
    real_h, imag_h = spectrum
    real_p = real_u * real_h - imag_u * imag_h
    imag_p = real_u * imag_h + imag_u * real_h
    convolved = inverse(real_p, imag_p, tables)
    return (convolved + own_gain[:, None] * kv_values).astype(jnp.bfloat16)


def featurize(extended, weights, length):
    tap_count = weights.shape[1]
    running = jnp.zeros(extended.shape[:1] + (length,) + extended.shape[2:], jnp.float32)
    for lag_idx in range(tap_count):
        offset = tap_count - 1 - lag_idx
        running = running + weights[:, lag_idx, None, :] * extended[
            :, offset : offset + length, :
        ].astype(jnp.float32)
    return running.astype(jnp.bfloat16)


def _feat_body(proj_ref, prior_ref, w_ref, q_ref, kv_ref, ext_ref):
    rows = proj_ref.shape[1]
    feats = []
    for a in range(3):
        ext_ref[0:2, :] = jnp.zeros((2, ext_ref.shape[1]), jnp.float32)
        ext_ref[2:8, :] = prior_ref[a].astype(jnp.float32)
        ext_ref[8 : 8 + rows, :] = proj_ref[a].astype(jnp.float32)
        acc = jnp.zeros((rows, ext_ref.shape[1]), jnp.float32)
        for j in range(KS):
            acc = acc + w_ref[a, j : j + 1, :] * ext_ref[8 - j : 8 - j + rows, :]
        feats.append(acc.astype(jnp.bfloat16))
    q_ref[...] = feats[0].astype(jnp.float32).T.astype(jnp.bfloat16)
    kv = feats[1].astype(jnp.float32) * feats[2].astype(jnp.float32)
    kv_ref[...] = kv.astype(jnp.bfloat16).astype(jnp.float32).T.astype(jnp.bfloat16)

def featurize_kv(projected, prior, weights, lane_block=128, interpret=False):
    _, rows, chans = projected.shape
    grid = (chans // lane_block,)
    return pl.pallas_call(
        _feat_body,
        grid=grid,
        in_specs=[
            pl.BlockSpec((3, rows, lane_block), lambda i: (0, 0, i)),
            pl.BlockSpec((3, KS - 1, lane_block), lambda i: (0, 0, i)),
            pl.BlockSpec((3, KS, lane_block), lambda i: (0, 0, i)),
        ],
        out_specs=[
            pl.BlockSpec((lane_block, rows), lambda i: (i, 0)),
            pl.BlockSpec((lane_block, rows), lambda i: (i, 0)),
        ],
        out_shape=[jax.ShapeDtypeStruct((chans, rows), jnp.bfloat16)] * 2,
        scratch_shapes=[pltpu.VMEM((rows + 8, lane_block), jnp.float32)],
        interpret=interpret,
    )(projected, prior, weights)


def _split(a):
    hi = a.astype(jnp.bfloat16)
    return hi, (a - hi.astype(jnp.float32)).astype(jnp.bfloat16)


def _mm(a, b):
    return jnp.dot(a, b, preferred_element_type=jnp.float32)


def _left3(t_hi, t_lo, v):
    v_hi, v_lo = _split(v)
    return _mm(t_hi, v_hi) + _mm(t_lo, v_hi) + _mm(t_hi, v_lo)


def _right3(v, t_hi, t_lo):
    v_hi, v_lo = _split(v)
    return _mm(v_hi, t_hi) + _mm(v_lo, t_hi) + _mm(v_hi, t_lo)


def _right2(v, t_hi, t_lo):
    v_hi = v.astype(jnp.bfloat16)
    return _mm(v_hi, t_hi) + _mm(v_hi, t_lo)


def _spectrum(a_re, a_im, ct, st, cbsb_h, cbsb_l):
    rows, width = ct.shape
    t_re = a_re * ct + a_im * st
    t_im = a_im * ct - a_re * st
    r = _right3(jnp.concatenate([t_re, t_im], axis=0), cbsb_h, cbsb_l)
    f_re = r[:rows, :width] + r[rows:, width:]
    f_im = r[rows:, :width] - r[:rows, width:]
    return f_re, f_im


def _filter_body(h_ref, casa_h, casa_l, cbsb_h, cbsb_l, ct_ref, st_ref, re_ref, im_ref):
    ct = ct_ref[...]
    st = st_ref[...]
    rows = ct.shape[0]
    for c in range(h_ref.shape[0]):
        a = _left3(casa_h[...], casa_l[...], h_ref[c])
        re_ref[c], im_ref[c] = _spectrum(a[:rows], -a[rows:], ct, st, cbsb_h[...], cbsb_l[...])


def _conv_body(x_ref, fh_re_ref, fh_im_ref, g_ref, casa_h, casa_l, cbsb_h, cbsb_l,
               ct_ref, st_ref, inv_h, inv_l, o_ref):
    ct = ct_ref[...]
    st = st_ref[...]
    rows, width = ct.shape
    chans = fh_re_ref.shape[0]
    x_b = jnp.concatenate([x_ref[:, c, :] for c in range(chans)], axis=1)
    a = _mm(casa_h[...], x_b) + _mm(casa_l[...], x_b)
    pieces = []
    for c in range(chans):
        a_re = a[:rows, c * width : (c + 1) * width]
        a_im = -a[rows:, c * width : (c + 1) * width]
        pieces.append(a_re * ct + a_im * st)
        pieces.append(a_im * ct - a_re * st)
    r = _right2(jnp.concatenate(pieces, axis=0), cbsb_h[...], cbsb_l[...])
    prods = []
    for c in range(chans):
        lo = 2 * rows * c
        f_re = r[lo : lo + rows, :width] + r[lo + rows : lo + 2 * rows, width:]
        f_im = r[lo + rows : lo + 2 * rows, :width] - r[lo : lo + rows, width:]
        fh_re = fh_re_ref[c]
        fh_im = fh_im_ref[c]
        prods.append(f_re * fh_re - f_im * fh_im)
        prods.append(f_re * fh_im + f_im * fh_re)
    q = _right2(jnp.concatenate(prods, axis=0), cbsb_h[...], cbsb_l[...])
    cols = []
    for c in range(chans):
        lo = 2 * rows * c
        z_re = q[lo : lo + rows, :width] - q[lo + rows : lo + 2 * rows, width:]
        z_im = q[lo + rows : lo + 2 * rows, :width] + q[lo : lo + rows, width:]
        w_re = z_re * ct - z_im * st
        w_im = z_im * ct + z_re * st
        cols.append(jnp.concatenate([w_re, w_im], axis=0))
    out = _left3(inv_h[...], inv_l[...], jnp.concatenate(cols, axis=1))
    res = (out * (1.0 / (rows * width)) + g_ref[...] * x_b.astype(jnp.float32)).astype(jnp.bfloat16)
    for c in range(chans):
        o_ref[:, c, :] = res[:, c * width : (c + 1) * width]


def conv_tables(size_a, size_b):
    whole = size_a * size_b
    half_a = size_a // 2

    def pair(r, c, period):
        ri = lax.broadcasted_iota(jnp.int32, (r, c), 0)
        ci = lax.broadcasted_iota(jnp.int32, (r, c), 1)
        ang = (ri * ci % period).astype(jnp.float32) * (2.0 * math.pi / period)
        return jnp.cos(ang), jnp.sin(ang)

    cos_a, sin_a = pair(size_a, half_a, size_a)
    cos_b, sin_b = pair(size_b, size_b, size_b)
    cos_t, sin_t = pair(size_a, size_b, whole)
    inv = jnp.concatenate([cos_a.T, -sin_a.T], axis=1)
    casa = jnp.concatenate([cos_a, sin_a], axis=0)
    cbsb = jnp.concatenate([cos_b, sin_b], axis=1)
    return (*_split(casa), *_split(cbsb), cos_t, sin_t, *_split(inv))


def filter_spectrum(filt, tabs, ch_block=2, size_b=256):
    ch, length = filt.shape
    half_a = length // size_b
    size_a = 2 * half_a
    h = filt.reshape(ch, half_a, size_b)
    full = lambda t: pl.BlockSpec(t.shape, lambda i: (0,) * t.ndim)
    blk_out = pl.BlockSpec((ch_block, size_a, size_b), lambda i: (i, 0, 0))
    return pl.pallas_call(
        _filter_body,
        grid=(ch // ch_block,),
        in_specs=[pl.BlockSpec((ch_block, half_a, size_b), lambda i: (i, 0, 0))]
        + [full(t) for t in tabs[:6]],
        out_specs=[blk_out, blk_out],
        out_shape=[jax.ShapeDtypeStruct((ch, size_a, size_b), jnp.float32)] * 2,
    )(h, *tabs[:6])


def long_conv(x, spectrum, gain, tabs):
    blocks, ch, size_b = x.shape
    g = jnp.repeat(gain, size_b)[None, :]
    casa_h, casa_l, cbsb_h, cbsb_l, cos_t, sin_t, inv_h, inv_l = tabs
    return pl.pallas_call(
        _conv_body,
        out_shape=jax.ShapeDtypeStruct((blocks, ch, size_b), jnp.bfloat16),
    )(x, *spectrum, g, casa_h, casa_l, cbsb_h, cbsb_l, cos_t, sin_t, inv_h, inv_l)


def _proj_body(f_ref, q_ref, w_ref, s_ref, o_ref, g_scr):
    @pl.when(pl.program_id(0) == 0)
    def _():
        gated = (q_ref[...].astype(jnp.float32) * f_ref[...].astype(jnp.float32)).astype(jnp.bfloat16)
        g_scr[...] = gated.astype(jnp.float32).T.astype(jnp.bfloat16)

    width = o_ref.shape[2]
    for p in range(o_ref.shape[0]):
        acc = None
        for b in range(w_ref.shape[0] // BLK):
            part = jnp.dot(g_scr[:, b * BLK : (b + 1) * BLK],
                           w_ref[b * BLK : (b + 1) * BLK, p * width : (p + 1) * width],
                           preferred_element_type=jnp.float32) * s_ref[b : b + 1, p * width : (p + 1) * width]
            acc = part if acc is None else acc + part
        o_ref[p] = acc.astype(jnp.bfloat16)


def project(filtered_home, q_cols, out_values, scale_cols, n_pieces, steps=2):
    chans, rows = filtered_home.shape
    width = out_values.shape[1] // n_pieces
    per_step = n_pieces // steps
    return pl.pallas_call(
        _proj_body,
        grid=(steps,),
        in_specs=[
            pl.BlockSpec((chans, rows), lambda j: (0, 0)),
            pl.BlockSpec((chans, rows), lambda j: (0, 0)),
            pl.BlockSpec((chans, width * per_step), lambda j: (0, j)),
            pl.BlockSpec((scale_cols.shape[0], width * per_step), lambda j: (0, j)),
        ],
        out_specs=pl.BlockSpec((per_step, rows, width), lambda j: (j, 0, 0)),
        out_shape=jax.ShapeDtypeStruct((n_pieces, rows, width), jnp.bfloat16),
        scratch_shapes=[pltpu.VMEM((rows, chans), jnp.bfloat16)],
    )(filtered_home, q_cols, out_values, scale_cols)


def multiply_round(left_arr, right_arr):
    return (left_arr.astype(jnp.float32) * right_arr.astype(jnp.float32)).astype(jnp.bfloat16)


def local(projected, feat_weight, long_filter, skip_gain, out_values, out_scales):
    groups = lax.axis_size("seq")
    tok_rows = projected.shape[1]
    local_ch = projected.shape[2]
    length = tok_rows * groups
    rim_width = KS - 1
    prior_rows = passed_along(projected[:, tok_rows - rim_width :, :], "seq", 1)
    q_feat, gated_kv = featurize_kv(projected, prior_rows, feat_weight)
    tabs = conv_tables(2 * length // 256, 256)
    spectrum = filter_spectrum(long_filter, tabs)
    kv_owned = lax.all_to_all(gated_kv.reshape(groups, -1, tok_rows), "seq", 0, 0, tiled=True)
    filtered = long_conv(kv_owned, spectrum, skip_gain, tabs)
    filtered_home = lax.all_to_all(filtered, "seq", 0, 0, tiled=True).reshape(local_ch, tok_rows)
    n_tensor = lax.axis_size("tensor")
    scale_cols = jnp.repeat(out_scales, BLK, axis=1)
    half = tok_rows // 2
    outs = []
    for h in range(2):
        cols = slice(h * half, (h + 1) * half)
        pieces = project(filtered_home[:, cols], q_feat[:, cols], out_values, scale_cols, n_tensor)
        gathered = lax.all_to_all(pieces, "tensor", 0, 0, tiled=True)
        outs.append(jnp.sum(gathered.astype(jnp.float32), axis=0).astype(jnp.bfloat16))
    return jnp.concatenate(outs, axis=0)


def solution(mesh):
    return jax.shard_map(
        local,
        mesh=mesh,
        in_specs=(
            P(None, "seq", "tensor"),
            P(None, None, "tensor"),
            P(("tensor", "seq"), None),
            P(("tensor", "seq")),
            P("tensor", None),
            P("tensor", None),
        ),
        out_specs=P("seq", "tensor"),
        check_vma=False,
    )
```

```python
import math

import jax
import jax.numpy as jnp
from jax import lax
from jax.sharding import PartitionSpec as P
from jax.experimental import pallas as pl
from jax.experimental.pallas import tpu as pltpu

KS = 7
BLK = 128


TRIPLE = lax.Precision.HIGH


def passed_along(x, axis, by):
    size = lax.axis_size(axis)
    pairs = [(i, i + by) for i in range(size) if 0 <= i + by < size]
    return lax.ppermute(x, axis, pairs)


def split_length(whole):
    for candidate in range(2, whole + 1, 2):
        if whole % candidate == 0 and candidate * candidate >= whole:
            return (candidate, whole // candidate)
    return (whole, 1)


def angle_pair(row_count, col_count, period):
    row_ids = lax.broadcasted_iota(jnp.int32, (row_count, col_count), 0)
    col_ids = lax.broadcasted_iota(jnp.int32, (row_count, col_count), 1)
    angles = (row_ids * col_ids % period).astype(jnp.float32) * (2.0 * math.pi / period)
    return (jnp.cos(angles), jnp.sin(angles))


def make_tables(length):
    whole = 2 * length
    size_a, size_b = split_length(whole)
    return (
        angle_pair(size_a, size_a, size_a),
        angle_pair(size_b, size_b, size_b),
        angle_pair(size_a, size_b, whole),
        size_a,
        size_b,
    )


def right_mul(signal, matrix):
    return jnp.einsum("ckn,nm->ckm", signal, matrix, precision=TRIPLE)


def forward(signal, tables):
    (cos_a, sin_a), (cos_b, sin_b), (cos_t, sin_t), size_a, size_b = tables
    half_a = size_a // 2
    blocks = signal.reshape(signal.shape[0], half_a, size_b)
    real_a = jnp.einsum("kn,cnb->ckb", cos_a[:, :half_a], blocks, precision=TRIPLE)
    imag_a = -jnp.einsum("kn,cnb->ckb", sin_a[:, :half_a], blocks, precision=TRIPLE)
    real_t = real_a * cos_t + imag_a * sin_t
    imag_t = imag_a * cos_t - real_a * sin_t
    real_f = right_mul(real_t, cos_b) + right_mul(imag_t, sin_b)
    imag_f = right_mul(imag_t, cos_b) - right_mul(real_t, sin_b)
    return (real_f, imag_f)


def inverse(real_f, imag_f, tables):
    (cos_a, sin_a), (cos_b, sin_b), (cos_t, sin_t), size_a, size_b = tables
    half_a = size_a // 2
    real_z = right_mul(real_f, cos_b) - right_mul(imag_f, sin_b)
    imag_z = right_mul(imag_f, cos_b) + right_mul(real_f, sin_b)
    real_w = real_z * cos_t - imag_z * sin_t
    imag_w = imag_z * cos_t + real_z * sin_t
    out_half = jnp.einsum("nk,ckb->cnb", cos_a[:half_a, :], real_w, precision=TRIPLE) - jnp.einsum(
        "nk,ckb->cnb", sin_a[:half_a, :], imag_w, precision=TRIPLE
    )
    return out_half.reshape(out_half.shape[0], half_a * size_b) * (1.0 / (size_a * size_b))


def long_mix(gated_kv, spectrum, own_gain, tables):
    kv_values = gated_kv.astype(jnp.float32)
    real_u, imag_u = forward(kv_values, tables)
    real_h, imag_h = spectrum
    real_p = real_u * real_h - imag_u * imag_h
    imag_p = real_u * imag_h + imag_u * real_h
    convolved = inverse(real_p, imag_p, tables)
    return (convolved + own_gain[:, None] * kv_values).astype(jnp.bfloat16)


def featurize(extended, weights, length):
    tap_count = weights.shape[1]
    running = jnp.zeros(extended.shape[:1] + (length,) + extended.shape[2:], jnp.float32)
    for lag_idx in range(tap_count):
        offset = tap_count - 1 - lag_idx
        running = running + weights[:, lag_idx, None, :] * extended[
            :, offset : offset + length, :
        ].astype(jnp.float32)
    return running.astype(jnp.bfloat16)


def _feat_body(proj_ref, prior_ref, w_ref, q_ref, kv_ref, ext_ref):
    rows = proj_ref.shape[1]
    feats = []
    for a in range(3):
        ext_ref[0:2, :] = jnp.zeros((2, ext_ref.shape[1]), jnp.float32)
        ext_ref[2:8, :] = prior_ref[a].astype(jnp.float32)
        ext_ref[8 : 8 + rows, :] = proj_ref[a].astype(jnp.float32)
        acc = jnp.zeros((rows, ext_ref.shape[1]), jnp.float32)
        for j in range(KS):
            acc = acc + w_ref[a, j : j + 1, :] * ext_ref[8 - j : 8 - j + rows, :]
        feats.append(acc.astype(jnp.bfloat16))
    q_ref[...] = feats[0].astype(jnp.float32).T.astype(jnp.bfloat16)
    kv = feats[1].astype(jnp.float32) * feats[2].astype(jnp.float32)
    kv_ref[...] = kv.astype(jnp.bfloat16).astype(jnp.float32).T.astype(jnp.bfloat16)

def featurize_kv(projected, prior, weights, lane_block=128, interpret=False):
    _, rows, chans = projected.shape
    grid = (chans // lane_block,)
    return pl.pallas_call(
        _feat_body,
        grid=grid,
        in_specs=[
            pl.BlockSpec((3, rows, lane_block), lambda i: (0, 0, i)),
            pl.BlockSpec((3, KS - 1, lane_block), lambda i: (0, 0, i)),
            pl.BlockSpec((3, KS, lane_block), lambda i: (0, 0, i)),
        ],
        out_specs=[
            pl.BlockSpec((lane_block, rows), lambda i: (i, 0)),
            pl.BlockSpec((lane_block, rows), lambda i: (i, 0)),
        ],
        out_shape=[jax.ShapeDtypeStruct((chans, rows), jnp.bfloat16)] * 2,
        scratch_shapes=[pltpu.VMEM((rows + 8, lane_block), jnp.float32)],
        interpret=interpret,
    )(projected, prior, weights)


def _split(a):
    hi = a.astype(jnp.bfloat16)
    return hi, (a - hi.astype(jnp.float32)).astype(jnp.bfloat16)


def _mm(a, b):
    return jnp.dot(a, b, preferred_element_type=jnp.float32)


def _left3(t_hi, t_lo, v):
    v_hi, v_lo = _split(v)
    return _mm(t_hi, v_hi) + _mm(t_lo, v_hi) + _mm(t_hi, v_lo)


def _right3(v, t_hi, t_lo):
    v_hi, v_lo = _split(v)
    return _mm(v_hi, t_hi) + _mm(v_lo, t_hi) + _mm(v_hi, t_lo)


def _right2(v, t_hi, t_lo):
    v_hi = v.astype(jnp.bfloat16)
    return _mm(v_hi, t_hi) + _mm(v_hi, t_lo)


def _spectrum(a_re, a_im, ct, st, cbsb_h, cbsb_l):
    rows, width = ct.shape
    t_re = a_re * ct + a_im * st
    t_im = a_im * ct - a_re * st
    r = _right3(jnp.concatenate([t_re, t_im], axis=0), cbsb_h, cbsb_l)
    f_re = r[:rows, :width] + r[rows:, width:]
    f_im = r[rows:, :width] - r[:rows, width:]
    return f_re, f_im


def _filter_body(h_ref, casa_h, casa_l, cbsb_h, cbsb_l, ct_ref, st_ref, re_ref, im_ref):
    ct = ct_ref[...]
    st = st_ref[...]
    rows = ct.shape[0]
    for c in range(h_ref.shape[0]):
        a = _left3(casa_h[...], casa_l[...], h_ref[c])
        re_ref[c], im_ref[c] = _spectrum(a[:rows], -a[rows:], ct, st, cbsb_h[...], cbsb_l[...])


def _conv_half(first, x_ref, fh_re_ref, fh_im_ref, g_ref, casa_h, casa_l, cbsb_h, cbsb_l,
               ct_ref, st_ref, inv_h, inv_l, o_ref):
    ct = ct_ref[...]
    st = st_ref[...]
    rows, width = ct.shape
    chans = fh_re_ref.shape[0]
    chan_ids = range(first, first + chans)
    x_b = jnp.concatenate([x_ref[:, c, :] for c in chan_ids], axis=1)
    a = _mm(casa_h[...], x_b) + _mm(casa_l[...], x_b)
    pieces = []
    for c in range(chans):
        a_re = a[:rows, c * width : (c + 1) * width]
        a_im = -a[rows:, c * width : (c + 1) * width]
        pieces.append(a_re * ct + a_im * st)
        pieces.append(a_im * ct - a_re * st)
    r = _right2(jnp.concatenate(pieces, axis=0), cbsb_h[...], cbsb_l[...])
    prods = []
    for c in range(chans):
        lo = 2 * rows * c
        f_re = r[lo : lo + rows, :width] + r[lo + rows : lo + 2 * rows, width:]
        f_im = r[lo + rows : lo + 2 * rows, :width] - r[lo : lo + rows, width:]
        fh_re = fh_re_ref[c]
        fh_im = fh_im_ref[c]
        prods.append(f_re * fh_re - f_im * fh_im)
        prods.append(f_re * fh_im + f_im * fh_re)
    q = _right2(jnp.concatenate(prods, axis=0), cbsb_h[...], cbsb_l[...])
    cols = []
    for c in range(chans):
        lo = 2 * rows * c
        z_re = q[lo : lo + rows, :width] - q[lo + rows : lo + 2 * rows, width:]
        z_im = q[lo + rows : lo + 2 * rows, :width] + q[lo : lo + rows, width:]
        w_re = z_re * ct - z_im * st
        w_im = z_im * ct + z_re * st
        cols.append(jnp.concatenate([w_re, w_im], axis=0))
    out = _left3(inv_h[...], inv_l[...], jnp.concatenate(cols, axis=1))
    res = (out * (1.0 / (rows * width)) + g_ref[:, first * width : (first + chans) * width] * x_b.astype(jnp.float32)).astype(jnp.bfloat16)
    for c in range(chans):
        o_ref[:, first + c, :] = res[:, c * width : (c + 1) * width]


def _conv_body(*refs):
    half = refs[1].shape[0]
    for step in range(2):
        pl.when(pl.program_id(0) == step)(lambda step=step: _conv_half(step * half, *refs))


def conv_tables(size_a, size_b):
    whole = size_a * size_b
    half_a = size_a // 2

    def pair(r, c, period):
        ri = lax.broadcasted_iota(jnp.int32, (r, c), 0)
        ci = lax.broadcasted_iota(jnp.int32, (r, c), 1)
        ang = (ri * ci % period).astype(jnp.float32) * (2.0 * math.pi / period)
        return jnp.cos(ang), jnp.sin(ang)

    cos_a, sin_a = pair(size_a, half_a, size_a)
    cos_b, sin_b = pair(size_b, size_b, size_b)
    cos_t, sin_t = pair(size_a, size_b, whole)
    inv = jnp.concatenate([cos_a.T, -sin_a.T], axis=1)
    casa = jnp.concatenate([cos_a, sin_a], axis=0)
    cbsb = jnp.concatenate([cos_b, sin_b], axis=1)
    return (*_split(casa), *_split(cbsb), cos_t, sin_t, *_split(inv))


def filter_spectrum(filt, tabs, ch_block=2, size_b=256):
    ch, length = filt.shape
    half_a = length // size_b
    size_a = 2 * half_a
    h = filt.reshape(ch, half_a, size_b)
    full = lambda t: pl.BlockSpec(t.shape, lambda i: (0,) * t.ndim)
    blk_out = pl.BlockSpec((ch_block, size_a, size_b), lambda i: (i, 0, 0))
    return pl.pallas_call(
        _filter_body,
        grid=(ch // ch_block,),
        in_specs=[pl.BlockSpec((ch_block, half_a, size_b), lambda i: (i, 0, 0))]
        + [full(t) for t in tabs[:6]],
        out_specs=[blk_out, blk_out],
        out_shape=[jax.ShapeDtypeStruct((ch, size_a, size_b), jnp.float32)] * 2,
    )(h, *tabs[:6])


def long_conv(x, spectrum, gain, tabs):
    blocks, ch, size_b = x.shape
    g = jnp.repeat(gain, size_b)[None, :]
    casa_h, casa_l, cbsb_h, cbsb_l, cos_t, sin_t, inv_h, inv_l = tabs
    tables = (casa_h, casa_l, cbsb_h, cbsb_l, cos_t, sin_t, inv_h, inv_l)
    full = lambda t: pl.BlockSpec(t.shape, lambda i: (0,) * t.ndim)
    half = pl.BlockSpec((ch // 2,) + spectrum[0].shape[1:], lambda i: (i, 0, 0))
    return pl.pallas_call(
        _conv_body,
        grid=(2,),
        in_specs=[full(x), half, half, full(g)] + [full(t) for t in tables],
        out_specs=pl.BlockSpec((blocks, ch, size_b), lambda i: (0, 0, 0)),
        out_shape=jax.ShapeDtypeStruct((blocks, ch, size_b), jnp.bfloat16),
    )(x, *spectrum, g, *tables)


def _proj_body(f_ref, q_ref, w_ref, s_ref, o_ref, g_scr):
    @pl.when(pl.program_id(0) == 0)
    def _():
        gated = (q_ref[...].astype(jnp.float32) * f_ref[...].astype(jnp.float32)).astype(jnp.bfloat16)
        g_scr[...] = gated.astype(jnp.float32).T.astype(jnp.bfloat16)

    width = o_ref.shape[2]
    for p in range(o_ref.shape[0]):
        acc = None
        for b in range(w_ref.shape[0] // BLK):
            part = jnp.dot(g_scr[:, b * BLK : (b + 1) * BLK],
                           w_ref[b * BLK : (b + 1) * BLK, p * width : (p + 1) * width],
                           preferred_element_type=jnp.float32) * s_ref[b : b + 1, p * width : (p + 1) * width]
            acc = part if acc is None else acc + part
        o_ref[p] = acc.astype(jnp.bfloat16)


def project(filtered_home, q_cols, out_values, scale_cols, n_pieces, steps=2):
    chans, rows = filtered_home.shape
    width = out_values.shape[1] // n_pieces
    per_step = n_pieces // steps
    return pl.pallas_call(
        _proj_body,
        grid=(steps,),
        in_specs=[
            pl.BlockSpec((chans, rows), lambda j: (0, 0)),
            pl.BlockSpec((chans, rows), lambda j: (0, 0)),
            pl.BlockSpec((chans, width * per_step), lambda j: (0, j)),
            pl.BlockSpec((scale_cols.shape[0], width * per_step), lambda j: (0, j)),
        ],
        out_specs=pl.BlockSpec((per_step, rows, width), lambda j: (j, 0, 0)),
        out_shape=jax.ShapeDtypeStruct((n_pieces, rows, width), jnp.bfloat16),
        scratch_shapes=[pltpu.VMEM((rows, chans), jnp.bfloat16)],
    )(filtered_home, q_cols, out_values, scale_cols)


def multiply_round(left_arr, right_arr):
    return (left_arr.astype(jnp.float32) * right_arr.astype(jnp.float32)).astype(jnp.bfloat16)


def local(projected, feat_weight, long_filter, skip_gain, out_values, out_scales):
    groups = lax.axis_size("seq")
    tok_rows = projected.shape[1]
    local_ch = projected.shape[2]
    length = tok_rows * groups
    rim_width = KS - 1
    prior_rows = passed_along(projected[:, tok_rows - rim_width :, :], "seq", 1)
    q_feat, gated_kv = featurize_kv(projected, prior_rows, feat_weight)
    tabs = conv_tables(2 * length // 256, 256)
    spectrum = filter_spectrum(long_filter, tabs)
    kv_owned = lax.all_to_all(gated_kv.reshape(groups, -1, tok_rows), "seq", 0, 0, tiled=True)
    filtered = long_conv(kv_owned, spectrum, skip_gain, tabs)
    filtered_home = lax.all_to_all(filtered, "seq", 0, 0, tiled=True).reshape(local_ch, tok_rows)
    n_tensor = lax.axis_size("tensor")
    scale_cols = jnp.repeat(out_scales, BLK, axis=1)
    pieces = project(filtered_home, q_feat, out_values, scale_cols, n_tensor)
    gathered = lax.all_to_all(pieces, "tensor", 0, 0, tiled=True)
    return jnp.sum(gathered.astype(jnp.float32), axis=0).astype(jnp.bfloat16)


def solution(mesh):
    return jax.shard_map(
        local,
        mesh=mesh,
        in_specs=(
            P(None, "seq", "tensor"),
            P(None, None, "tensor"),
            P(("tensor", "seq"), None),
            P(("tensor", "seq")),
            P("tensor", None),
            P("tensor", None),
        ),
        out_specs=P("seq", "tensor"),
        check_vma=False,
    )
```

```python
import math

import jax
import jax.numpy as jnp
from jax import lax
from jax.sharding import PartitionSpec as P
from jax.experimental import pallas as pl
from jax.experimental.pallas import tpu as pltpu

KS = 7
BLK = 128


TRIPLE = lax.Precision.HIGH


def passed_along(x, axis, by):
    size = lax.axis_size(axis)
    pairs = [(i, i + by) for i in range(size) if 0 <= i + by < size]
    return lax.ppermute(x, axis, pairs)


def split_length(whole):
    for candidate in range(2, whole + 1, 2):
        if whole % candidate == 0 and candidate * candidate >= whole:
            return (candidate, whole // candidate)
    return (whole, 1)


def angle_pair(row_count, col_count, period):
    row_ids = lax.broadcasted_iota(jnp.int32, (row_count, col_count), 0)
    col_ids = lax.broadcasted_iota(jnp.int32, (row_count, col_count), 1)
    angles = (row_ids * col_ids % period).astype(jnp.float32) * (2.0 * math.pi / period)
    return (jnp.cos(angles), jnp.sin(angles))


def make_tables(length):
    whole = 2 * length
    size_a, size_b = split_length(whole)
    return (
        angle_pair(size_a, size_a, size_a),
        angle_pair(size_b, size_b, size_b),
        angle_pair(size_a, size_b, whole),
        size_a,
        size_b,
    )


def right_mul(signal, matrix):
    return jnp.einsum("ckn,nm->ckm", signal, matrix, precision=TRIPLE)


def forward(signal, tables):
    (cos_a, sin_a), (cos_b, sin_b), (cos_t, sin_t), size_a, size_b = tables
    half_a = size_a // 2
    blocks = signal.reshape(signal.shape[0], half_a, size_b)
    real_a = jnp.einsum("kn,cnb->ckb", cos_a[:, :half_a], blocks, precision=TRIPLE)
    imag_a = -jnp.einsum("kn,cnb->ckb", sin_a[:, :half_a], blocks, precision=TRIPLE)
    real_t = real_a * cos_t + imag_a * sin_t
    imag_t = imag_a * cos_t - real_a * sin_t
    real_f = right_mul(real_t, cos_b) + right_mul(imag_t, sin_b)
    imag_f = right_mul(imag_t, cos_b) - right_mul(real_t, sin_b)
    return (real_f, imag_f)


def inverse(real_f, imag_f, tables):
    (cos_a, sin_a), (cos_b, sin_b), (cos_t, sin_t), size_a, size_b = tables
    half_a = size_a // 2
    real_z = right_mul(real_f, cos_b) - right_mul(imag_f, sin_b)
    imag_z = right_mul(imag_f, cos_b) + right_mul(real_f, sin_b)
    real_w = real_z * cos_t - imag_z * sin_t
    imag_w = imag_z * cos_t + real_z * sin_t
    out_half = jnp.einsum("nk,ckb->cnb", cos_a[:half_a, :], real_w, precision=TRIPLE) - jnp.einsum(
        "nk,ckb->cnb", sin_a[:half_a, :], imag_w, precision=TRIPLE
    )
    return out_half.reshape(out_half.shape[0], half_a * size_b) * (1.0 / (size_a * size_b))


def long_mix(gated_kv, spectrum, own_gain, tables):
    kv_values = gated_kv.astype(jnp.float32)
    real_u, imag_u = forward(kv_values, tables)
    real_h, imag_h = spectrum
    real_p = real_u * real_h - imag_u * imag_h
    imag_p = real_u * imag_h + imag_u * real_h
    convolved = inverse(real_p, imag_p, tables)
    return (convolved + own_gain[:, None] * kv_values).astype(jnp.bfloat16)


def featurize(extended, weights, length):
    tap_count = weights.shape[1]
    running = jnp.zeros(extended.shape[:1] + (length,) + extended.shape[2:], jnp.float32)
    for lag_idx in range(tap_count):
        offset = tap_count - 1 - lag_idx
        running = running + weights[:, lag_idx, None, :] * extended[
            :, offset : offset + length, :
        ].astype(jnp.float32)
    return running.astype(jnp.bfloat16)


def _feat_body(proj_ref, prior_ref, w_ref, q_ref, kv_ref, ext_ref):
    rows = proj_ref.shape[1]
    feats = []
    for a in range(3):
        ext_ref[0:2, :] = jnp.zeros((2, ext_ref.shape[1]), jnp.float32)
        ext_ref[2:8, :] = prior_ref[a].astype(jnp.float32)
        ext_ref[8 : 8 + rows, :] = proj_ref[a].astype(jnp.float32)
        acc = jnp.zeros((rows, ext_ref.shape[1]), jnp.float32)
        for j in range(KS):
            acc = acc + w_ref[a, j : j + 1, :] * ext_ref[8 - j : 8 - j + rows, :]
        feats.append(acc.astype(jnp.bfloat16))
    q_ref[...] = feats[0].astype(jnp.float32).T.astype(jnp.bfloat16)
    kv = feats[1].astype(jnp.float32) * feats[2].astype(jnp.float32)
    kv_ref[...] = kv.astype(jnp.bfloat16).astype(jnp.float32).T.astype(jnp.bfloat16)

def featurize_kv(projected, prior, weights, lane_block=256, interpret=False):
    _, rows, chans = projected.shape
    grid = (chans // lane_block,)
    return pl.pallas_call(
        _feat_body,
        grid=grid,
        in_specs=[
            pl.BlockSpec((3, rows, lane_block), lambda i: (0, 0, i)),
            pl.BlockSpec((3, KS - 1, lane_block), lambda i: (0, 0, i)),
            pl.BlockSpec((3, KS, lane_block), lambda i: (0, 0, i)),
        ],
        out_specs=[
            pl.BlockSpec((lane_block, rows), lambda i: (i, 0)),
            pl.BlockSpec((lane_block, rows), lambda i: (i, 0)),
        ],
        out_shape=[jax.ShapeDtypeStruct((chans, rows), jnp.bfloat16)] * 2,
        scratch_shapes=[pltpu.VMEM((rows + 8, lane_block), jnp.float32)],
        interpret=interpret,
    )(projected, prior, weights)


def _split(a):
    hi = a.astype(jnp.bfloat16)
    return hi, (a - hi.astype(jnp.float32)).astype(jnp.bfloat16)


def _mm(a, b):
    return jnp.dot(a, b, preferred_element_type=jnp.float32)


def _left3(t_hi, t_lo, v):
    v_hi, v_lo = _split(v)
    return _mm(t_hi, v_hi) + _mm(t_lo, v_hi) + _mm(t_hi, v_lo)


def _right3(v, t_hi, t_lo):
    v_hi, v_lo = _split(v)
    return _mm(v_hi, t_hi) + _mm(v_lo, t_hi) + _mm(v_hi, t_lo)


def _right2(v, t_hi, t_lo):
    v_hi = v.astype(jnp.bfloat16)
    return _mm(v_hi, t_hi) + _mm(v_hi, t_lo)


def _spectrum(a_re, a_im, ct, st, cbsb_h, cbsb_l):
    rows, width = ct.shape
    t_re = a_re * ct + a_im * st
    t_im = a_im * ct - a_re * st
    r = _right3(jnp.concatenate([t_re, t_im], axis=0), cbsb_h, cbsb_l)
    f_re = r[:rows, :width] + r[rows:, width:]
    f_im = r[rows:, :width] - r[:rows, width:]
    return f_re, f_im


def _filter_body(h_ref, casa_h, casa_l, cbsb_h, cbsb_l, ct_ref, st_ref, re_ref, im_ref):
    ct = ct_ref[...]
    st = st_ref[...]
    rows = ct.shape[0]
    for c in range(h_ref.shape[0]):
        a = _left3(casa_h[...], casa_l[...], h_ref[c])
        re_ref[c], im_ref[c] = _spectrum(a[:rows], -a[rows:], ct, st, cbsb_h[...], cbsb_l[...])


def _conv_body(x_ref, fh_re_ref, fh_im_ref, g_ref, casa_h, casa_l, cbsb_h, cbsb_l,
               ct_ref, st_ref, inv_h, inv_l, o_ref):
    ct = ct_ref[...]
    st = st_ref[...]
    rows, width = ct.shape
    chans = fh_re_ref.shape[0]
    x_b = jnp.concatenate([x_ref[:, c, :] for c in range(chans)], axis=1)
    a = _mm(casa_h[...], x_b) + _mm(casa_l[...], x_b)
    pieces = []
    for c in range(chans):
        a_re = a[:rows, c * width : (c + 1) * width]
        a_im = -a[rows:, c * width : (c + 1) * width]
        pieces.append(a_re * ct + a_im * st)
        pieces.append(a_im * ct - a_re * st)
    r = _right2(jnp.concatenate(pieces, axis=0), cbsb_h[...], cbsb_l[...])
    prods = []
    for c in range(chans):
        lo = 2 * rows * c
        f_re = r[lo : lo + rows, :width] + r[lo + rows : lo + 2 * rows, width:]
        f_im = r[lo + rows : lo + 2 * rows, :width] - r[lo : lo + rows, width:]
        fh_re = fh_re_ref[c]
        fh_im = fh_im_ref[c]
        prods.append(f_re * fh_re - f_im * fh_im)
        prods.append(f_re * fh_im + f_im * fh_re)
    q = _right2(jnp.concatenate(prods, axis=0), cbsb_h[...], cbsb_l[...])
    cols = []
    for c in range(chans):
        lo = 2 * rows * c
        z_re = q[lo : lo + rows, :width] - q[lo + rows : lo + 2 * rows, width:]
        z_im = q[lo + rows : lo + 2 * rows, :width] + q[lo : lo + rows, width:]
        w_re = z_re * ct - z_im * st
        w_im = z_im * ct + z_re * st
        cols.append(jnp.concatenate([w_re, w_im], axis=0))
    out = _left3(inv_h[...], inv_l[...], jnp.concatenate(cols, axis=1))
    res = (out * (1.0 / (rows * width)) + g_ref[...] * x_b.astype(jnp.float32)).astype(jnp.bfloat16)
    for c in range(chans):
        o_ref[:, c, :] = res[:, c * width : (c + 1) * width]


def conv_tables(size_a, size_b):
    whole = size_a * size_b
    half_a = size_a // 2

    def pair(r, c, period):
        ri = lax.broadcasted_iota(jnp.int32, (r, c), 0)
        ci = lax.broadcasted_iota(jnp.int32, (r, c), 1)
        ang = (ri * ci % period).astype(jnp.float32) * (2.0 * math.pi / period)
        return jnp.cos(ang), jnp.sin(ang)

    cos_a, sin_a = pair(size_a, half_a, size_a)
    cos_b, sin_b = pair(size_b, size_b, size_b)
    cos_t, sin_t = pair(size_a, size_b, whole)
    inv = jnp.concatenate([cos_a.T, -sin_a.T], axis=1)
    casa = jnp.concatenate([cos_a, sin_a], axis=0)
    cbsb = jnp.concatenate([cos_b, sin_b], axis=1)
    return (*_split(casa), *_split(cbsb), cos_t, sin_t, *_split(inv))


def filter_spectrum(filt, tabs, ch_block=2, size_b=256):
    ch, length = filt.shape
    half_a = length // size_b
    size_a = 2 * half_a
    h = filt.reshape(ch, half_a, size_b)
    full = lambda t: pl.BlockSpec(t.shape, lambda i: (0,) * t.ndim)
    blk_out = pl.BlockSpec((ch_block, size_a, size_b), lambda i: (i, 0, 0))
    return pl.pallas_call(
        _filter_body,
        grid=(ch // ch_block,),
        in_specs=[pl.BlockSpec((ch_block, half_a, size_b), lambda i: (i, 0, 0))]
        + [full(t) for t in tabs[:6]],
        out_specs=[blk_out, blk_out],
        out_shape=[jax.ShapeDtypeStruct((ch, size_a, size_b), jnp.float32)] * 2,
    )(h, *tabs[:6])


def long_conv(x, spectrum, gain, tabs):
    blocks, ch, size_b = x.shape
    g = jnp.repeat(gain, size_b)[None, :]
    casa_h, casa_l, cbsb_h, cbsb_l, cos_t, sin_t, inv_h, inv_l = tabs
    return pl.pallas_call(
        _conv_body,
        out_shape=jax.ShapeDtypeStruct((blocks, ch, size_b), jnp.bfloat16),
    )(x, *spectrum, g, casa_h, casa_l, cbsb_h, cbsb_l, cos_t, sin_t, inv_h, inv_l)


def _proj_body(f_ref, q_ref, w_ref, s_ref, o_ref, g_scr):
    @pl.when(pl.program_id(0) == 0)
    def _():
        gated = (q_ref[...].astype(jnp.float32) * f_ref[...].astype(jnp.float32)).astype(jnp.bfloat16)
        g_scr[...] = gated.astype(jnp.float32).T.astype(jnp.bfloat16)

    width = o_ref.shape[2]
    for p in range(o_ref.shape[0]):
        acc = None
        for b in range(w_ref.shape[0] // BLK):
            part = jnp.dot(g_scr[:, b * BLK : (b + 1) * BLK],
                           w_ref[b * BLK : (b + 1) * BLK, p * width : (p + 1) * width],
                           preferred_element_type=jnp.float32) * s_ref[b : b + 1, p * width : (p + 1) * width]
            acc = part if acc is None else acc + part
        o_ref[p] = acc.astype(jnp.bfloat16)


def project(filtered_home, q_cols, out_values, scale_cols, n_pieces, steps=2):
    chans, rows = filtered_home.shape
    width = out_values.shape[1] // n_pieces
    per_step = n_pieces // steps
    return pl.pallas_call(
        _proj_body,
        grid=(steps,),
        in_specs=[
            pl.BlockSpec((chans, rows), lambda j: (0, 0)),
            pl.BlockSpec((chans, rows), lambda j: (0, 0)),
            pl.BlockSpec((chans, width * per_step), lambda j: (0, j)),
            pl.BlockSpec((scale_cols.shape[0], width * per_step), lambda j: (0, j)),
        ],
        out_specs=pl.BlockSpec((per_step, rows, width), lambda j: (j, 0, 0)),
        out_shape=jax.ShapeDtypeStruct((n_pieces, rows, width), jnp.bfloat16),
        scratch_shapes=[pltpu.VMEM((rows, chans), jnp.bfloat16)],
    )(filtered_home, q_cols, out_values, scale_cols)


def multiply_round(left_arr, right_arr):
    return (left_arr.astype(jnp.float32) * right_arr.astype(jnp.float32)).astype(jnp.bfloat16)


def local(projected, feat_weight, long_filter, skip_gain, out_values, out_scales):
    groups = lax.axis_size("seq")
    tok_rows = projected.shape[1]
    local_ch = projected.shape[2]
    length = tok_rows * groups
    rim_width = KS - 1
    prior_rows = passed_along(projected[:, tok_rows - rim_width :, :], "seq", 1)
    q_feat, gated_kv = featurize_kv(projected, prior_rows, feat_weight)
    tabs = conv_tables(2 * length // 256, 256)
    spectrum = filter_spectrum(long_filter, tabs)
    kv_owned = lax.all_to_all(gated_kv.reshape(groups, -1, tok_rows), "seq", 0, 0, tiled=True)
    filtered = long_conv(kv_owned, spectrum, skip_gain, tabs)
    filtered_home = lax.all_to_all(filtered, "seq", 0, 0, tiled=True).reshape(local_ch, tok_rows)
    n_tensor = lax.axis_size("tensor")
    scale_cols = jnp.repeat(out_scales, BLK, axis=1)
    pieces = project(filtered_home, q_feat, out_values, scale_cols, n_tensor)
    gathered = lax.all_to_all(pieces, "tensor", 0, 0, tiled=True)
    return jnp.sum(gathered.astype(jnp.float32), axis=0).astype(jnp.bfloat16)


def solution(mesh):
    return jax.shard_map(
        local,
        mesh=mesh,
        in_specs=(
            P(None, "seq", "tensor"),
            P(None, None, "tensor"),
            P(("tensor", "seq"), None),
            P(("tensor", "seq")),
            P("tensor", None),
            P("tensor", None),
        ),
        out_specs=P("seq", "tensor"),
        check_vma=False,
    )
```

```python
import math

import jax
import jax.numpy as jnp
from jax import lax
from jax.sharding import PartitionSpec as P
from jax.experimental import pallas as pl
from jax.experimental.pallas import tpu as pltpu

KS = 7
BLK = 128


TRIPLE = lax.Precision.HIGH


def passed_along(x, axis, by):
    size = lax.axis_size(axis)
    pairs = [(i, i + by) for i in range(size) if 0 <= i + by < size]
    return lax.ppermute(x, axis, pairs)


def split_length(whole):
    for candidate in range(2, whole + 1, 2):
        if whole % candidate == 0 and candidate * candidate >= whole:
            return (candidate, whole // candidate)
    return (whole, 1)


def angle_pair(row_count, col_count, period):
    row_ids = lax.broadcasted_iota(jnp.int32, (row_count, col_count), 0)
    col_ids = lax.broadcasted_iota(jnp.int32, (row_count, col_count), 1)
    angles = (row_ids * col_ids % period).astype(jnp.float32) * (2.0 * math.pi / period)
    return (jnp.cos(angles), jnp.sin(angles))


def make_tables(length):
    whole = 2 * length
    size_a, size_b = split_length(whole)
    return (
        angle_pair(size_a, size_a, size_a),
        angle_pair(size_b, size_b, size_b),
        angle_pair(size_a, size_b, whole),
        size_a,
        size_b,
    )


def right_mul(signal, matrix):
    return jnp.einsum("ckn,nm->ckm", signal, matrix, precision=TRIPLE)


def forward(signal, tables):
    (cos_a, sin_a), (cos_b, sin_b), (cos_t, sin_t), size_a, size_b = tables
    half_a = size_a // 2
    blocks = signal.reshape(signal.shape[0], half_a, size_b)
    real_a = jnp.einsum("kn,cnb->ckb", cos_a[:, :half_a], blocks, precision=TRIPLE)
    imag_a = -jnp.einsum("kn,cnb->ckb", sin_a[:, :half_a], blocks, precision=TRIPLE)
    real_t = real_a * cos_t + imag_a * sin_t
    imag_t = imag_a * cos_t - real_a * sin_t
    real_f = right_mul(real_t, cos_b) + right_mul(imag_t, sin_b)
    imag_f = right_mul(imag_t, cos_b) - right_mul(real_t, sin_b)
    return (real_f, imag_f)


def inverse(real_f, imag_f, tables):
    (cos_a, sin_a), (cos_b, sin_b), (cos_t, sin_t), size_a, size_b = tables
    half_a = size_a // 2
    real_z = right_mul(real_f, cos_b) - right_mul(imag_f, sin_b)
    imag_z = right_mul(imag_f, cos_b) + right_mul(real_f, sin_b)
    real_w = real_z * cos_t - imag_z * sin_t
    imag_w = imag_z * cos_t + real_z * sin_t
    out_half = jnp.einsum("nk,ckb->cnb", cos_a[:half_a, :], real_w, precision=TRIPLE) - jnp.einsum(
        "nk,ckb->cnb", sin_a[:half_a, :], imag_w, precision=TRIPLE
    )
    return out_half.reshape(out_half.shape[0], half_a * size_b) * (1.0 / (size_a * size_b))


def long_mix(gated_kv, spectrum, own_gain, tables):
    kv_values = gated_kv.astype(jnp.float32)
    real_u, imag_u = forward(kv_values, tables)
    real_h, imag_h = spectrum
    real_p = real_u * real_h - imag_u * imag_h
    imag_p = real_u * imag_h + imag_u * real_h
    convolved = inverse(real_p, imag_p, tables)
    return (convolved + own_gain[:, None] * kv_values).astype(jnp.bfloat16)


def featurize(extended, weights, length):
    tap_count = weights.shape[1]
    running = jnp.zeros(extended.shape[:1] + (length,) + extended.shape[2:], jnp.float32)
    for lag_idx in range(tap_count):
        offset = tap_count - 1 - lag_idx
        running = running + weights[:, lag_idx, None, :] * extended[
            :, offset : offset + length, :
        ].astype(jnp.float32)
    return running.astype(jnp.bfloat16)


def _feat_body(proj_ref, prior_ref, w_ref, q_ref, kv_ref, ext_ref):
    rows = proj_ref.shape[1]
    feats = []
    for a in range(3):
        ext_ref[0:2, :] = jnp.zeros((2, ext_ref.shape[1]), jnp.float32)
        ext_ref[2:8, :] = prior_ref[a].astype(jnp.float32)
        ext_ref[8 : 8 + rows, :] = proj_ref[a].astype(jnp.float32)
        acc = jnp.zeros((rows, ext_ref.shape[1]), jnp.float32)
        for j in range(KS):
            acc = acc + w_ref[a, j : j + 1, :] * ext_ref[8 - j : 8 - j + rows, :]
        feats.append(acc.astype(jnp.bfloat16))
    q_ref[...] = feats[0].astype(jnp.float32).T.astype(jnp.bfloat16)
    kv = feats[1].astype(jnp.float32) * feats[2].astype(jnp.float32)
    kv_ref[...] = kv.astype(jnp.bfloat16).astype(jnp.float32).T.astype(jnp.bfloat16)

def featurize_kv(projected, prior, weights, lane_block=512, interpret=False):
    _, rows, chans = projected.shape
    grid = (chans // lane_block,)
    return pl.pallas_call(
        _feat_body,
        grid=grid,
        in_specs=[
            pl.BlockSpec((3, rows, lane_block), lambda i: (0, 0, i)),
            pl.BlockSpec((3, KS - 1, lane_block), lambda i: (0, 0, i)),
            pl.BlockSpec((3, KS, lane_block), lambda i: (0, 0, i)),
        ],
        out_specs=[
            pl.BlockSpec((lane_block, rows), lambda i: (i, 0)),
            pl.BlockSpec((lane_block, rows), lambda i: (i, 0)),
        ],
        out_shape=[jax.ShapeDtypeStruct((chans, rows), jnp.bfloat16)] * 2,
        scratch_shapes=[pltpu.VMEM((rows + 8, lane_block), jnp.float32)],
        interpret=interpret,
    )(projected, prior, weights)


def _split(a):
    hi = a.astype(jnp.bfloat16)
    return hi, (a - hi.astype(jnp.float32)).astype(jnp.bfloat16)


def _mm(a, b):
    return jnp.dot(a, b, preferred_element_type=jnp.float32)


def _left3(t_hi, t_lo, v):
    v_hi, v_lo = _split(v)
    return _mm(t_hi, v_hi) + _mm(t_lo, v_hi) + _mm(t_hi, v_lo)


def _right3(v, t_hi, t_lo):
    v_hi, v_lo = _split(v)
    return _mm(v_hi, t_hi) + _mm(v_lo, t_hi) + _mm(v_hi, t_lo)


def _right2(v, t_hi, t_lo):
    v_hi = v.astype(jnp.bfloat16)
    return _mm(v_hi, t_hi) + _mm(v_hi, t_lo)


def _spectrum(a_re, a_im, ct, st, cbsb_h, cbsb_l):
    rows, width = ct.shape
    t_re = a_re * ct + a_im * st
    t_im = a_im * ct - a_re * st
    r = _right3(jnp.concatenate([t_re, t_im], axis=0), cbsb_h, cbsb_l)
    f_re = r[:rows, :width] + r[rows:, width:]
    f_im = r[rows:, :width] - r[:rows, width:]
    return f_re, f_im


def _filter_body(h_ref, casa_h, casa_l, cbsb_h, cbsb_l, ct_ref, st_ref, re_ref, im_ref):
    ct = ct_ref[...]
    st = st_ref[...]
    rows = ct.shape[0]
    for c in range(h_ref.shape[0]):
        a = _left3(casa_h[...], casa_l[...], h_ref[c])
        re_ref[c], im_ref[c] = _spectrum(a[:rows], -a[rows:], ct, st, cbsb_h[...], cbsb_l[...])


def _conv_body(x_ref, fh_re_ref, fh_im_ref, g_ref, casa_h, casa_l, cbsb_h, cbsb_l,
               ct_ref, st_ref, inv_h, inv_l, o_ref):
    ct = ct_ref[...]
    st = st_ref[...]
    rows, width = ct.shape
    chans = fh_re_ref.shape[0]
    x_b = jnp.concatenate([x_ref[:, c, :] for c in range(chans)], axis=1)
    a = _mm(casa_h[...], x_b) + _mm(casa_l[...], x_b)
    pieces = []
    for c in range(chans):
        a_re = a[:rows, c * width : (c + 1) * width]
        a_im = -a[rows:, c * width : (c + 1) * width]
        pieces.append(a_re * ct + a_im * st)
        pieces.append(a_im * ct - a_re * st)
    r = _right2(jnp.concatenate(pieces, axis=0), cbsb_h[...], cbsb_l[...])
    prods = []
    for c in range(chans):
        lo = 2 * rows * c
        f_re = r[lo : lo + rows, :width] + r[lo + rows : lo + 2 * rows, width:]
        f_im = r[lo + rows : lo + 2 * rows, :width] - r[lo : lo + rows, width:]
        fh_re = fh_re_ref[c]
        fh_im = fh_im_ref[c]
        prods.append(f_re * fh_re - f_im * fh_im)
        prods.append(f_re * fh_im + f_im * fh_re)
    q = _right2(jnp.concatenate(prods, axis=0), cbsb_h[...], cbsb_l[...])
    cols = []
    for c in range(chans):
        lo = 2 * rows * c
        z_re = q[lo : lo + rows, :width] - q[lo + rows : lo + 2 * rows, width:]
        z_im = q[lo + rows : lo + 2 * rows, :width] + q[lo : lo + rows, width:]
        w_re = z_re * ct - z_im * st
        w_im = z_im * ct + z_re * st
        cols.append(jnp.concatenate([w_re, w_im], axis=0))
    out = _left3(inv_h[...], inv_l[...], jnp.concatenate(cols, axis=1))
    res = (out * (1.0 / (rows * width)) + g_ref[...] * x_b.astype(jnp.float32)).astype(jnp.bfloat16)
    for c in range(chans):
        o_ref[:, c, :] = res[:, c * width : (c + 1) * width]


def conv_tables(size_a, size_b):
    whole = size_a * size_b
    half_a = size_a // 2

    def pair(r, c, period):
        ri = lax.broadcasted_iota(jnp.int32, (r, c), 0)
        ci = lax.broadcasted_iota(jnp.int32, (r, c), 1)
        ang = (ri * ci % period).astype(jnp.float32) * (2.0 * math.pi / period)
        return jnp.cos(ang), jnp.sin(ang)

    cos_a, sin_a = pair(size_a, half_a, size_a)
    cos_b, sin_b = pair(size_b, size_b, size_b)
    cos_t, sin_t = pair(size_a, size_b, whole)
    inv = jnp.concatenate([cos_a.T, -sin_a.T], axis=1)
    casa = jnp.concatenate([cos_a, sin_a], axis=0)
    cbsb = jnp.concatenate([cos_b, sin_b], axis=1)
    return (*_split(casa), *_split(cbsb), cos_t, sin_t, *_split(inv))


def filter_spectrum(filt, tabs, ch_block=2, size_b=256):
    ch, length = filt.shape
    half_a = length // size_b
    size_a = 2 * half_a
    h = filt.reshape(ch, half_a, size_b)
    full = lambda t: pl.BlockSpec(t.shape, lambda i: (0,) * t.ndim)
    blk_out = pl.BlockSpec((ch_block, size_a, size_b), lambda i: (i, 0, 0))
    return pl.pallas_call(
        _filter_body,
        grid=(ch // ch_block,),
        in_specs=[pl.BlockSpec((ch_block, half_a, size_b), lambda i: (i, 0, 0))]
        + [full(t) for t in tabs[:6]],
        out_specs=[blk_out, blk_out],
        out_shape=[jax.ShapeDtypeStruct((ch, size_a, size_b), jnp.float32)] * 2,
    )(h, *tabs[:6])


def long_conv(x, spectrum, gain, tabs):
    blocks, ch, size_b = x.shape
    g = jnp.repeat(gain, size_b)[None, :]
    casa_h, casa_l, cbsb_h, cbsb_l, cos_t, sin_t, inv_h, inv_l = tabs
    return pl.pallas_call(
        _conv_body,
        out_shape=jax.ShapeDtypeStruct((blocks, ch, size_b), jnp.bfloat16),
    )(x, *spectrum, g, casa_h, casa_l, cbsb_h, cbsb_l, cos_t, sin_t, inv_h, inv_l)


def _proj_body(f_ref, q_ref, w_ref, s_ref, o_ref, g_scr):
    @pl.when(pl.program_id(0) == 0)
    def _():
        gated = (q_ref[...].astype(jnp.float32) * f_ref[...].astype(jnp.float32)).astype(jnp.bfloat16)
        g_scr[...] = gated.astype(jnp.float32).T.astype(jnp.bfloat16)

    width = o_ref.shape[2]
    for p in range(o_ref.shape[0]):
        acc = None
        for b in range(w_ref.shape[0] // BLK):
            part = jnp.dot(g_scr[:, b * BLK : (b + 1) * BLK],
                           w_ref[b * BLK : (b + 1) * BLK, p * width : (p + 1) * width],
                           preferred_element_type=jnp.float32) * s_ref[b : b + 1, p * width : (p + 1) * width]
            acc = part if acc is None else acc + part
        o_ref[p] = acc.astype(jnp.bfloat16)


def project(filtered_home, q_cols, out_values, scale_cols, n_pieces, steps=2):
    chans, rows = filtered_home.shape
    width = out_values.shape[1] // n_pieces
    per_step = n_pieces // steps
    return pl.pallas_call(
        _proj_body,
        grid=(steps,),
        in_specs=[
            pl.BlockSpec((chans, rows), lambda j: (0, 0)),
            pl.BlockSpec((chans, rows), lambda j: (0, 0)),
            pl.BlockSpec((chans, width * per_step), lambda j: (0, j)),
            pl.BlockSpec((scale_cols.shape[0], width * per_step), lambda j: (0, j)),
        ],
        out_specs=pl.BlockSpec((per_step, rows, width), lambda j: (j, 0, 0)),
        out_shape=jax.ShapeDtypeStruct((n_pieces, rows, width), jnp.bfloat16),
        scratch_shapes=[pltpu.VMEM((rows, chans), jnp.bfloat16)],
    )(filtered_home, q_cols, out_values, scale_cols)


def multiply_round(left_arr, right_arr):
    return (left_arr.astype(jnp.float32) * right_arr.astype(jnp.float32)).astype(jnp.bfloat16)


def local(projected, feat_weight, long_filter, skip_gain, out_values, out_scales):
    groups = lax.axis_size("seq")
    tok_rows = projected.shape[1]
    local_ch = projected.shape[2]
    length = tok_rows * groups
    rim_width = KS - 1
    prior_rows = passed_along(projected[:, tok_rows - rim_width :, :], "seq", 1)
    q_feat, gated_kv = featurize_kv(projected, prior_rows, feat_weight)
    tabs = conv_tables(2 * length // 256, 256)
    spectrum = filter_spectrum(long_filter, tabs)
    kv_owned = lax.all_to_all(gated_kv.reshape(groups, -1, tok_rows), "seq", 0, 0, tiled=True)
    filtered = long_conv(kv_owned, spectrum, skip_gain, tabs)
    filtered_home = lax.all_to_all(filtered, "seq", 0, 0, tiled=True).reshape(local_ch, tok_rows)
    n_tensor = lax.axis_size("tensor")
    scale_cols = jnp.repeat(out_scales, BLK, axis=1)
    pieces = project(filtered_home, q_feat, out_values, scale_cols, n_tensor)
    gathered = lax.all_to_all(pieces, "tensor", 0, 0, tiled=True)
    return jnp.sum(gathered.astype(jnp.float32), axis=0).astype(jnp.bfloat16)


def solution(mesh):
    return jax.shard_map(
        local,
        mesh=mesh,
        in_specs=(
            P(None, "seq", "tensor"),
            P(None, None, "tensor"),
            P(("tensor", "seq"), None),
            P(("tensor", "seq")),
            P("tensor", None),
            P("tensor", None),
        ),
        out_specs=P("seq", "tensor"),
        check_vma=False,
    )
```

```python
import math

import jax
import jax.numpy as jnp
from jax import lax
from jax.sharding import PartitionSpec as P
from jax.experimental import pallas as pl
from jax.experimental.pallas import tpu as pltpu

KS = 7
BLK = 128


TRIPLE = lax.Precision.HIGH


def passed_along(x, axis, by):
    size = lax.axis_size(axis)
    pairs = [(i, i + by) for i in range(size) if 0 <= i + by < size]
    return lax.ppermute(x, axis, pairs)


def split_length(whole):
    for candidate in range(2, whole + 1, 2):
        if whole % candidate == 0 and candidate * candidate >= whole:
            return (candidate, whole // candidate)
    return (whole, 1)


def angle_pair(row_count, col_count, period):
    row_ids = lax.broadcasted_iota(jnp.int32, (row_count, col_count), 0)
    col_ids = lax.broadcasted_iota(jnp.int32, (row_count, col_count), 1)
    angles = (row_ids * col_ids % period).astype(jnp.float32) * (2.0 * math.pi / period)
    return (jnp.cos(angles), jnp.sin(angles))


def make_tables(length):
    whole = 2 * length
    size_a, size_b = split_length(whole)
    return (
        angle_pair(size_a, size_a, size_a),
        angle_pair(size_b, size_b, size_b),
        angle_pair(size_a, size_b, whole),
        size_a,
        size_b,
    )


def right_mul(signal, matrix):
    return jnp.einsum("ckn,nm->ckm", signal, matrix, precision=TRIPLE)


def forward(signal, tables):
    (cos_a, sin_a), (cos_b, sin_b), (cos_t, sin_t), size_a, size_b = tables
    half_a = size_a // 2
    blocks = signal.reshape(signal.shape[0], half_a, size_b)
    real_a = jnp.einsum("kn,cnb->ckb", cos_a[:, :half_a], blocks, precision=TRIPLE)
    imag_a = -jnp.einsum("kn,cnb->ckb", sin_a[:, :half_a], blocks, precision=TRIPLE)
    real_t = real_a * cos_t + imag_a * sin_t
    imag_t = imag_a * cos_t - real_a * sin_t
    real_f = right_mul(real_t, cos_b) + right_mul(imag_t, sin_b)
    imag_f = right_mul(imag_t, cos_b) - right_mul(real_t, sin_b)
    return (real_f, imag_f)


def inverse(real_f, imag_f, tables):
    (cos_a, sin_a), (cos_b, sin_b), (cos_t, sin_t), size_a, size_b = tables
    half_a = size_a // 2
    real_z = right_mul(real_f, cos_b) - right_mul(imag_f, sin_b)
    imag_z = right_mul(imag_f, cos_b) + right_mul(real_f, sin_b)
    real_w = real_z * cos_t - imag_z * sin_t
    imag_w = imag_z * cos_t + real_z * sin_t
    out_half = jnp.einsum("nk,ckb->cnb", cos_a[:half_a, :], real_w, precision=TRIPLE) - jnp.einsum(
        "nk,ckb->cnb", sin_a[:half_a, :], imag_w, precision=TRIPLE
    )
    return out_half.reshape(out_half.shape[0], half_a * size_b) * (1.0 / (size_a * size_b))


def long_mix(gated_kv, spectrum, own_gain, tables):
    kv_values = gated_kv.astype(jnp.float32)
    real_u, imag_u = forward(kv_values, tables)
    real_h, imag_h = spectrum
    real_p = real_u * real_h - imag_u * imag_h
    imag_p = real_u * imag_h + imag_u * real_h
    convolved = inverse(real_p, imag_p, tables)
    return (convolved + own_gain[:, None] * kv_values).astype(jnp.bfloat16)


def featurize(extended, weights, length):
    tap_count = weights.shape[1]
    running = jnp.zeros(extended.shape[:1] + (length,) + extended.shape[2:], jnp.float32)
    for lag_idx in range(tap_count):
        offset = tap_count - 1 - lag_idx
        running = running + weights[:, lag_idx, None, :] * extended[
            :, offset : offset + length, :
        ].astype(jnp.float32)
    return running.astype(jnp.bfloat16)


def _feat_body(proj_ref, prior_ref, w_ref, q_ref, kv_ref, ext_ref):
    rows = proj_ref.shape[1]
    feats = []
    for a in range(3):
        ext_ref[0:2, :] = jnp.zeros((2, ext_ref.shape[1]), jnp.float32)
        ext_ref[2:8, :] = prior_ref[a].astype(jnp.float32)
        ext_ref[8 : 8 + rows, :] = proj_ref[a].astype(jnp.float32)
        acc = jnp.zeros((rows, ext_ref.shape[1]), jnp.float32)
        for j in range(KS):
            acc = acc + w_ref[a, j : j + 1, :] * ext_ref[8 - j : 8 - j + rows, :]
        feats.append(acc.astype(jnp.bfloat16))
    q_ref[...] = feats[0].astype(jnp.float32).T.astype(jnp.bfloat16)
    kv = feats[1].astype(jnp.float32) * feats[2].astype(jnp.float32)
    kv_ref[...] = kv.astype(jnp.bfloat16).astype(jnp.float32).T.astype(jnp.bfloat16)

def featurize_kv(projected, prior, weights, lane_block=256, interpret=False):
    _, rows, chans = projected.shape
    grid = (chans // lane_block,)
    return pl.pallas_call(
        _feat_body,
        grid=grid,
        in_specs=[
            pl.BlockSpec((3, rows, lane_block), lambda i: (0, 0, i)),
            pl.BlockSpec((3, KS - 1, lane_block), lambda i: (0, 0, i)),
            pl.BlockSpec((3, KS, lane_block), lambda i: (0, 0, i)),
        ],
        out_specs=[
            pl.BlockSpec((lane_block, rows), lambda i: (i, 0)),
            pl.BlockSpec((lane_block, rows), lambda i: (i, 0)),
        ],
        out_shape=[jax.ShapeDtypeStruct((chans, rows), jnp.bfloat16)] * 2,
        scratch_shapes=[pltpu.VMEM((rows + 8, lane_block), jnp.float32)],
        interpret=interpret,
    )(projected, prior, weights)


def _split(a):
    hi = a.astype(jnp.bfloat16)
    return hi, (a - hi.astype(jnp.float32)).astype(jnp.bfloat16)


def _mm(a, b):
    return jnp.dot(a, b, preferred_element_type=jnp.float32)


def _left3(t_hi, t_lo, v):
    v_hi, v_lo = _split(v)
    return _mm(t_hi, v_hi) + _mm(t_lo, v_hi) + _mm(t_hi, v_lo)


def _right3(v, t_hi, t_lo):
    v_hi, v_lo = _split(v)
    return _mm(v_hi, t_hi) + _mm(v_lo, t_hi) + _mm(v_hi, t_lo)


def _right2(v, t_hi, t_lo):
    v_hi = v.astype(jnp.bfloat16)
    return _mm(v_hi, t_hi) + _mm(v_hi, t_lo)


def _spectrum(a_re, a_im, ct, st, cbsb_h, cbsb_l):
    rows, width = ct.shape
    t_re = a_re * ct + a_im * st
    t_im = a_im * ct - a_re * st
    r = _right3(jnp.concatenate([t_re, t_im], axis=0), cbsb_h, cbsb_l)
    f_re = r[:rows, :width] + r[rows:, width:]
    f_im = r[rows:, :width] - r[:rows, width:]
    return f_re, f_im


def _filter_body(h_ref, casa_h, casa_l, cbsb_h, cbsb_l, ct_ref, st_ref, re_ref, im_ref):
    ct = ct_ref[...]
    st = st_ref[...]
    rows = ct.shape[0]
    for c in range(h_ref.shape[0]):
        a = _left3(casa_h[...], casa_l[...], h_ref[c])
        re_ref[c], im_ref[c] = _spectrum(a[:rows], -a[rows:], ct, st, cbsb_h[...], cbsb_l[...])


def _conv_body(x_ref, fh_re_ref, fh_im_ref, g_ref, casa_h, casa_l, cbsb_h, cbsb_l,
               ct_ref, st_ref, inv_h, inv_l, o_ref):
    ct = ct_ref[...]
    st = st_ref[...]
    rows, width = ct.shape
    chans = fh_re_ref.shape[0]
    x_b = jnp.concatenate([x_ref[:, c, :] for c in range(chans)], axis=1)
    a = _mm(casa_h[...], x_b) + _mm(casa_l[...], x_b)
    pieces = []
    for c in range(chans):
        a_re = a[:rows, c * width : (c + 1) * width]
        a_im = -a[rows:, c * width : (c + 1) * width]
        pieces.append(a_re * ct + a_im * st)
        pieces.append(a_im * ct - a_re * st)
    r = _right2(jnp.concatenate(pieces, axis=0), cbsb_h[...], cbsb_l[...])
    prods = []
    for c in range(chans):
        lo = 2 * rows * c
        f_re = r[lo : lo + rows, :width] + r[lo + rows : lo + 2 * rows, width:]
        f_im = r[lo + rows : lo + 2 * rows, :width] - r[lo : lo + rows, width:]
        fh_re = fh_re_ref[c]
        fh_im = fh_im_ref[c]
        prods.append(f_re * fh_re - f_im * fh_im)
        prods.append(f_re * fh_im + f_im * fh_re)
    q = _right2(jnp.concatenate(prods, axis=0), cbsb_h[...], cbsb_l[...])
    cols = []
    for c in range(chans):
        lo = 2 * rows * c
        z_re = q[lo : lo + rows, :width] - q[lo + rows : lo + 2 * rows, width:]
        z_im = q[lo + rows : lo + 2 * rows, :width] + q[lo : lo + rows, width:]
        w_re = z_re * ct - z_im * st
        w_im = z_im * ct + z_re * st
        cols.append(jnp.concatenate([w_re, w_im], axis=0))
    out = _left3(inv_h[...], inv_l[...], jnp.concatenate(cols, axis=1))
    res = (out * (1.0 / (rows * width)) + g_ref[...] * x_b.astype(jnp.float32)).astype(jnp.bfloat16)
    for c in range(chans):
        o_ref[:, c, :] = res[:, c * width : (c + 1) * width]


def conv_tables(size_a, size_b):
    whole = size_a * size_b
    half_a = size_a // 2

    def pair(r, c, period):
        ri = lax.broadcasted_iota(jnp.int32, (r, c), 0)
        ci = lax.broadcasted_iota(jnp.int32, (r, c), 1)
        ang = (ri * ci % period).astype(jnp.float32) * (2.0 * math.pi / period)
        return jnp.cos(ang), jnp.sin(ang)

    cos_a, sin_a = pair(size_a, half_a, size_a)
    cos_b, sin_b = pair(size_b, size_b, size_b)
    cos_t, sin_t = pair(size_a, size_b, whole)
    inv = jnp.concatenate([cos_a.T, -sin_a.T], axis=1)
    casa = jnp.concatenate([cos_a, sin_a], axis=0)
    cbsb = jnp.concatenate([cos_b, sin_b], axis=1)
    return (*_split(casa), *_split(cbsb), cos_t, sin_t, *_split(inv))


def filter_spectrum(filt, tabs, ch_block=2, size_b=256):
    ch, length = filt.shape
    half_a = length // size_b
    size_a = 2 * half_a
    h = filt.reshape(ch, half_a, size_b)
    full = lambda t: pl.BlockSpec(t.shape, lambda i: (0,) * t.ndim)
    blk_out = pl.BlockSpec((ch_block, size_a, size_b), lambda i: (i, 0, 0))
    return pl.pallas_call(
        _filter_body,
        grid=(ch // ch_block,),
        in_specs=[pl.BlockSpec((ch_block, half_a, size_b), lambda i: (i, 0, 0))]
        + [full(t) for t in tabs[:6]],
        out_specs=[blk_out, blk_out],
        out_shape=[jax.ShapeDtypeStruct((ch, size_a, size_b), jnp.float32)] * 2,
    )(h, *tabs[:6])


def long_conv(x, spectrum, gain, tabs):
    blocks, ch, size_b = x.shape
    g = jnp.repeat(gain, size_b)[None, :]
    casa_h, casa_l, cbsb_h, cbsb_l, cos_t, sin_t, inv_h, inv_l = tabs
    return pl.pallas_call(
        _conv_body,
        out_shape=jax.ShapeDtypeStruct((blocks, ch, size_b), jnp.bfloat16),
    )(x, *spectrum, g, casa_h, casa_l, cbsb_h, cbsb_l, cos_t, sin_t, inv_h, inv_l)


def _proj_body(f_ref, q_ref, w_ref, s_ref, o_ref, g_scr):
    @pl.when(pl.program_id(0) == 0)
    def _():
        gated = (q_ref[...].astype(jnp.float32) * f_ref[...].astype(jnp.float32)).astype(jnp.bfloat16)
        g_scr[...] = gated.astype(jnp.float32).T.astype(jnp.bfloat16)

    width = o_ref.shape[2]
    for p in range(o_ref.shape[0]):
        acc = None
        for b in range(w_ref.shape[0] // BLK):
            part = jnp.dot(g_scr[:, b * BLK : (b + 1) * BLK],
                           w_ref[b * BLK : (b + 1) * BLK, p * width : (p + 1) * width],
                           preferred_element_type=jnp.float32) * s_ref[b : b + 1, p * width : (p + 1) * width]
            acc = part if acc is None else acc + part
        o_ref[p] = acc.astype(jnp.bfloat16)


def project(filtered_home, q_cols, out_values, scale_cols, n_pieces, steps=1):
    chans, rows = filtered_home.shape
    width = out_values.shape[1] // n_pieces
    per_step = n_pieces // steps
    return pl.pallas_call(
        _proj_body,
        grid=(steps,),
        in_specs=[
            pl.BlockSpec((chans, rows), lambda j: (0, 0)),
            pl.BlockSpec((chans, rows), lambda j: (0, 0)),
            pl.BlockSpec((chans, width * per_step), lambda j: (0, j)),
            pl.BlockSpec((scale_cols.shape[0], width * per_step), lambda j: (0, j)),
        ],
        out_specs=pl.BlockSpec((per_step, rows, width), lambda j: (j, 0, 0)),
        out_shape=jax.ShapeDtypeStruct((n_pieces, rows, width), jnp.bfloat16),
        scratch_shapes=[pltpu.VMEM((rows, chans), jnp.bfloat16)],
    )(filtered_home, q_cols, out_values, scale_cols)


def multiply_round(left_arr, right_arr):
    return (left_arr.astype(jnp.float32) * right_arr.astype(jnp.float32)).astype(jnp.bfloat16)


def local(projected, feat_weight, long_filter, skip_gain, out_values, out_scales):
    groups = lax.axis_size("seq")
    tok_rows = projected.shape[1]
    local_ch = projected.shape[2]
    length = tok_rows * groups
    rim_width = KS - 1
    prior_rows = passed_along(projected[:, tok_rows - rim_width :, :], "seq", 1)
    q_feat, gated_kv = featurize_kv(projected, prior_rows, feat_weight)
    tabs = conv_tables(2 * length // 256, 256)
    spectrum = filter_spectrum(long_filter, tabs)
    kv_owned = lax.all_to_all(gated_kv.reshape(groups, -1, tok_rows), "seq", 0, 0, tiled=True)
    filtered = long_conv(kv_owned, spectrum, skip_gain, tabs)
    filtered_home = lax.all_to_all(filtered, "seq", 0, 0, tiled=True).reshape(local_ch, tok_rows)
    n_tensor = lax.axis_size("tensor")
    scale_cols = jnp.repeat(out_scales, BLK, axis=1)
    pieces = project(filtered_home, q_feat, out_values, scale_cols, n_tensor)
    gathered = lax.all_to_all(pieces, "tensor", 0, 0, tiled=True)
    return jnp.sum(gathered.astype(jnp.float32), axis=0).astype(jnp.bfloat16)


def solution(mesh):
    return jax.shard_map(
        local,
        mesh=mesh,
        in_specs=(
            P(None, "seq", "tensor"),
            P(None, None, "tensor"),
            P(("tensor", "seq"), None),
            P(("tensor", "seq")),
            P("tensor", None),
            P("tensor", None),
        ),
        out_specs=P("seq", "tensor"),
        check_vma=False,
    )
```
